512 devices in a mesh: row: 16 (over y, z_hi), col: 32 (over z_lo, x, core).
Axes of the slice: x: 4, y: 4, z: 16 (z_hi: 4, z_lo: 4; z = z_hi * 4 + z_lo), core: 2. Of those that a mesh axis runs over, the one named last changes fastest.
Arguments:
- object_field: float32 [2, 6144, 8192], P(None, 'row', 'col'), may hold values from -5 to 5
- probe_modes: float32 [2, 2, 256, 256], replicated, may hold values from -4 to 4
- scan_positions: int32 [16, 32, 2, 2], P('row', 'col'), may hold values from 0 to 256, as said below
- amplitudes: bfloat16 [16, 32, 2, 256, 256], P('row', 'col'), may hold values from 0.5 to 1.5
Outputs:
- object_out: float32 [2, 6144, 8192], P(None, 'row', 'col')
- probe_out: float32 [2, 2, 256, 256], replicated
The draws below stay inside these ranges and needn't reach their ends.
Inputs may be any that keep to these rules, and one draw needn't show every extreme that they name: `scan_positions`: in even batches the row offset is at most 128; in odd batches it is at least 192. The column offset lies in 32 to 128 in every batch. Every window lies inside its tile extended by 128 rows below and 128 columns to the right.
All inputs are finite; a program needn't handle non-finite values.
Results may differ from the reference program's by a relative error of at most 0.0003.
Values sent between devices are 32-bit elements; how exact they have to be, the bound alone decides.
No kernel may reach another device: no remote copies, remote signals or barrier semaphores. Data moves between devices by JAX's collectives and lax.ppermute only.
A program may use at most 64 MiB of HBM per device.

```python
import math
import jax
import jax.numpy as jnp
from jax import lax

WIN = 256
MODES = 2
HALO = 128
TILE_R = 384
TILE_C = 256
BATCHES = 2
OUTER = 1
NY = 6144
NX = 8192
POS_ALL = 1024
N_ROW = 16
N_COL = 32


def draw_scan_positions(key, part):
    key_rows = jax.random.fold_in(key, 11)
    key_cols = jax.random.fold_in(key, 23)
    lowest = jnp.array([0 if step % 2 == 0 else TILE_R + HALO - WIN - HALO // 2 for step in range(BATCHES)], jnp.int32)
    highest = jnp.array([TILE_R - WIN if step % 2 == 0 else TILE_R + HALO - WIN for step in range(BATCHES)], jnp.int32)
    rows = jax.random.randint(key_rows, (N_ROW, N_COL, BATCHES), lowest, highest + 1)
    cols = jax.random.randint(key_cols, (N_ROW, N_COL, BATCHES), HALO // 4, TILE_C + HALO - WIN + 1)
    rows = rows.at[0, 0, 0].set(0)
    rows = rows.at[0, 0, 1].set(TILE_R + HALO - WIN)
    cols = cols.at[0, 0, 0].set(HALO // 4)
    cols = cols.at[0, 0, 1].set(TILE_C + HALO - WIN)
    return jnp.stack([rows, cols], axis=-1).astype(jnp.int32)


def block_levels(key, shape, pieces, least, high):
    def one(axis_at, parts):
        draws = jax.random.uniform(jax.random.fold_in(jax.random.fold_in(key, 6), axis_at), (parts,), jnp.float32, least / len(pieces), high / len(pieces))
        return jnp.repeat(jnp.exp(draws), shape[axis_at] // parts).reshape((-1,) + (1,) * (len(shape) - axis_at - 1))

    factor_of = one(*pieces[0])
    for cut in pieces[1:]:
        factor_of = factor_of * one(*cut)
    return factor_of


def centred(key, dims, width, limit, split=(), held_as=jnp.bfloat16):
    result = width * jax.random.normal(key, dims, jnp.float32)
    if split:
        result = result * block_levels(key, dims, split, -0.22, 0.18)
    return jnp.clip(result, -limit, limit).astype(held_as)


def setup_inputs(seed: int = 0) -> dict:
    key_list = jax.random.split(jax.random.key(seed), 5)
    return {
        "object_field": centred(key_list[0], (2, NY, NX), 0.7, 5.0, ((1, 16), (2, 32)), jnp.float32),
        "probe_modes": centred(key_list[1], (MODES, 2, WIN, WIN), 0.5, 4.0, (), jnp.float32),
        "scan_positions": draw_scan_positions(jax.random.fold_in(key_list[4], 71), 0),
        "amplitudes": jnp.clip(0.5 + 1.0 * jax.random.uniform(key_list[3], (N_ROW, N_COL, BATCHES, WIN, WIN), jnp.float32) ** block_levels(key_list[3], (N_ROW, N_COL, BATCHES, WIN, WIN), ((0, 16), (1, 32)), -0.2, 0.2), 0.5, 1.5).astype(jnp.bfloat16),
    }


def window_fit(window, probe_modes, amplitude):
    object_window = window[0] + 1j * window[1]
    probe_complex = probe_modes[:, 0] + 1j * probe_modes[:, 1]
    wave = probe_complex * object_window
    far_field = jnp.fft.fft2(wave, norm='ortho')
    intensity = lax.optimization_barrier(jnp.sum(far_field.real ** 2 + far_field.imag ** 2, axis=0))
    factor = amplitude / jnp.sqrt(jnp.maximum(intensity, 0.1)) - 1.0
    chi_field = jnp.fft.ifft2(far_field * factor, norm='ortho')
    object_grad = lax.optimization_barrier(jnp.sum(jnp.conj(probe_complex) * chi_field, axis=0))
    probe_grad = jnp.conj(object_window) * chi_field
    object_part = jnp.stack([object_grad.real, object_grad.imag], axis=0)
    probe_part = jnp.stack([probe_grad.real, probe_grad.imag], axis=1)
    return (object_part, probe_part)

def reference(object_field, probe_modes, scan_positions, amplitudes):
    for outer_step in range(OUTER):
        power = jnp.sum(probe_modes * probe_modes) / (WIN * WIN)
        update_step = 1.0 / (power + 1e-06)
        probe_sum = jnp.zeros_like(probe_modes)
        for batch_index in range(BATCHES):
            padded = jnp.pad(object_field, ((0, 0), (0, HALO), (0, HALO)))

            def visit(carry, flat_index, padded=padded, batch_index=batch_index):
                gradient, probe_acc = carry
                tile_row = (flat_index // N_COL).astype(jnp.int32)
                tile_col = (flat_index % N_COL).astype(jnp.int32)
                offsets = scan_positions[tile_row, tile_col, batch_index]
                row_start = (tile_row * TILE_R + offsets[0]).astype(jnp.int32)
                col_start = (tile_col * TILE_C + offsets[1]).astype(jnp.int32)
                anchor = (jnp.int32(0), row_start, col_start)
                window = lax.dynamic_slice(padded, anchor, (2, WIN, WIN))
                amplitude = amplitudes[tile_row, tile_col, batch_index].astype(jnp.float32)
                object_part, probe_part = window_fit(window, probe_modes, amplitude)
                current = lax.dynamic_slice(gradient, anchor, (2, WIN, WIN))
                gradient = lax.dynamic_update_slice(gradient, current + object_part, anchor)
                return ((gradient, probe_acc + probe_part), None)
            start = (jnp.zeros_like(padded), jnp.zeros_like(probe_modes))
            (gradient, probe_acc), _ = lax.scan(visit, start, jnp.arange(N_ROW * N_COL, dtype=jnp.int32))
            object_field = object_field + update_step * gradient[:, :NY, :NX]
            probe_sum = probe_sum + probe_acc
        probe_modes = probe_modes + probe_sum / math.sqrt(POS_ALL)
    return (object_field, probe_modes)
```

```python
import math

import jax
import jax.numpy as jnp
import numpy as np
from jax import lax
from jax.experimental import pallas as pl
from jax.experimental.pallas import tpu as pltpu
from jax.sharding import Mesh
from jax.sharding import PartitionSpec as P

HALO = 128
BATCHES = 2
WIN = 256
HALF = 128
INTERPRET = False
ROW = ("row_0", "row_1")
COL = ("col_0", "col_1", "col_2")
PLANE = ("row_0", "col_1")
DEPTH = ("row_1", "col_0")
CORE = "col_2"


def halves(x):
    high = x.astype(jnp.bfloat16)
    low = (x - high.astype(np.float64)).astype(jnp.bfloat16)
    return high, low


def dft_constants():
    index = np.arange(HALF)
    angle = 2.0 * np.pi * (np.outer(index, index) % HALF) / HALF
    cosine = np.cos(angle) / 16.0
    sine = -np.sin(angle) / 16.0
    forward = np.block([[cosine, -sine], [sine, cosine]])
    high, low = halves(forward)
    left = np.concatenate([high, high, low], axis=1)
    left_t = np.concatenate([high.T, high.T, low.T], axis=1)
    right = np.concatenate([high, high, low], axis=0)
    right_t = np.concatenate([high.T, high.T, low.T], axis=0)
    turn = 2.0 * np.pi * index / WIN
    twiddle = np.stack([np.cos(turn), -np.sin(turn)]).astype(np.float32)
    rows = np.ascontiguousarray(np.broadcast_to(twiddle[:, :, None], (2, HALF, HALF)))
    cols = np.ascontiguousarray(np.broadcast_to(twiddle[:, None, :], (2, 8, HALF)))
    return left, left_t, right, right_t, rows, cols


def split3(x, order, axis):
    high = x.astype(jnp.bfloat16)
    low = (x - high.astype(jnp.float32)).astype(jnp.bfloat16)
    return jnp.concatenate([high, low, high], axis=axis)


def left_dft(matrix, x):
    return jnp.dot(matrix, split3(x, 0, 0), preferred_element_type=jnp.float32)


def right_dft(x, matrix):
    return jnp.dot(split3(x, 0, 1), matrix, preferred_element_type=jnp.float32)


def forward_dft(real, imag, left, right_t, twr, twc):
    t_r, t_i = twr
    c_r, c_i = twc
    a_r, b_r, a_i, b_i = real[:HALF], real[HALF:], imag[:HALF], imag[HALF:]
    d_r, d_i = a_r - b_r, a_i - b_i
    even = left_dft(left, jnp.concatenate([a_r + b_r, a_i + b_i], axis=0))
    odd = left_dft(left, jnp.concatenate([d_r * t_r - d_i * t_i, d_r * t_i + d_i * t_r], axis=0))
    real = jnp.concatenate([even[:HALF], odd[:HALF]], axis=0)
    imag = jnp.concatenate([even[HALF:], odd[HALF:]], axis=0)
    a_r, b_r, a_i, b_i = real[:, :HALF], real[:, HALF:], imag[:, :HALF], imag[:, HALF:]
    d_r, d_i = a_r - b_r, a_i - b_i
    even = right_dft(jnp.concatenate([a_r + b_r, a_i + b_i], axis=1), right_t)
    odd = right_dft(jnp.concatenate([d_r * c_r - d_i * c_i, d_r * c_i + d_i * c_r], axis=1), right_t)
    real = jnp.concatenate([even[:, :HALF], odd[:, :HALF]], axis=1)
    imag = jnp.concatenate([even[:, HALF:], odd[:, HALF:]], axis=1)
    return real, imag


def inverse_dft(real, imag, left_t, right, twr, twc):
    t_r, t_i = twr
    c_r, c_i = twc
    even = right_dft(jnp.concatenate([real[:, :HALF], imag[:, :HALF]], axis=1), right)
    odd = right_dft(jnp.concatenate([real[:, HALF:], imag[:, HALF:]], axis=1), right)
    o_r, o_i = odd[:, :HALF], odd[:, HALF:]
    o_r, o_i = o_r * c_r + o_i * c_i, o_i * c_r - o_r * c_i
    e_r, e_i = even[:, :HALF], even[:, HALF:]
    real = jnp.concatenate([e_r + o_r, e_r - o_r], axis=1)
    imag = jnp.concatenate([e_i + o_i, e_i - o_i], axis=1)
    even = left_dft(left_t, jnp.concatenate([real[:HALF], imag[:HALF]], axis=0))
    odd = left_dft(left_t, jnp.concatenate([real[HALF:], imag[HALF:]], axis=0))
    o_r, o_i = odd[:HALF], odd[HALF:]
    o_r, o_i = o_r * t_r + o_i * t_i, o_i * t_r - o_r * t_i
    e_r, e_i = even[:HALF], even[HALF:]
    real = jnp.concatenate([e_r + o_r, e_r - o_r], axis=0)
    imag = jnp.concatenate([e_i + o_i, e_i - o_i], axis=0)
    return real, imag


def window_fit(window, probe, amplitude, tables, far, window_ref, gradient, add_probe):
    left, left_t, right, right_t, rows, cols = tables
    window_ref[0] = window[0]
    window_ref[1] = window[1]

    def twiddles():
        twr = tuple(jnp.concatenate([rows[k], rows[k]], axis=1) for k in range(2))
        twc = tuple(cols[k][:1] for k in range(2))
        return twr, twc

    def outward(m, carry):
        twr, twc = twiddles()
        w_r, w_i = window_ref[0], window_ref[1]
        p_r, p_i = probe[m, 0], probe[m, 1]
        f_r, f_i = forward_dft(p_r * w_r - p_i * w_i, p_r * w_i + p_i * w_r, left[...], right_t[...], twr, twc)
        far[m, 0] = f_r
        far[m, 1] = f_i
        return carry

    lax.fori_loop(0, 2, outward, 0)
    intensity = far[0, 0] * far[0, 0] + far[0, 1] * far[0, 1]
    intensity = intensity + (far[1, 0] * far[1, 0] + far[1, 1] * far[1, 1])
    factor = amplitude / jnp.sqrt(jnp.maximum(intensity, 0.1)) - 1.0
    for m in range(2):
        far[m, 0] = far[m, 0] * factor
        far[m, 1] = far[m, 1] * factor
    gradient[...] = jnp.zeros(gradient.shape, jnp.float32)

    def inward(m, carry):
        twr, twc = twiddles()
        x_r, x_i = inverse_dft(far[m, 0], far[m, 1], left_t[...], right[...], twr, twc)
        w_r, w_i = window_ref[0], window_ref[1]
        p_r, p_i = probe[m, 0], probe[m, 1]
        gradient[0] += p_r * x_r + p_i * x_i
        gradient[1] += p_r * x_i - p_i * x_r
        add_probe(m, w_r * x_r + w_i * x_i, w_r * x_i - w_i * x_r)
        return carry

    lax.fori_loop(0, 2, inward, 0)


def before_kernel(probe, amp, amp_out, step_out):
    out_at = lax.broadcasted_iota(jnp.int32, (WIN, WIN), 0)
    in_at = lax.broadcasted_iota(jnp.int32, (WIN, WIN), 1)
    wanted = jnp.where(out_at < HALF, 2 * out_at, 2 * (out_at - HALF) + 1)
    pick = jnp.where(in_at == wanted, 1.0, 0.0).astype(jnp.bfloat16)
    for b in range(BATCHES):
        rows = jnp.dot(pick, amp[b], preferred_element_type=jnp.float32).astype(jnp.bfloat16)
        amp_out[b] = lax.dot_general(rows, pick, (((1,), (1,)), ((), ())), preferred_element_type=jnp.float32)
    total = jnp.zeros((8, HALF), jnp.float32)
    for m in range(2):
        for k in range(2):
            square = probe[m, k] * probe[m, k]
            square = jnp.sum(square.reshape(WIN // 8, 8, WIN), axis=0)
            total = total + square[:, :HALF] + square[:, HALF:]
    power = jnp.sum(total) / (WIN * WIN)
    step_out[...] = jnp.full((8, HALF), 1.0, jnp.float32) / (power + 1e-06)


def first_kernel(pos, obj, halo, probe, amp, step, left, left_t, right, right_t, rows, cols,
                 new_obj, spill, edge, probe_sum, far, win, grad):
    row, col = pos[0, 0], pos[0, 1]
    frame = TILE_R

    def cut(k):
        wide = jnp.concatenate([obj[k], halo[k]], axis=1)
        wide = pltpu.roll(wide, 384 - col, 1)[:, :WIN]
        return pltpu.roll(wide, lax.rem(frame - row, frame), 0)[:WIN]

    def add_probe(m, real, imag):
        probe_sum[m, 0] = real
        probe_sum[m, 1] = imag

    window_fit((cut(0), cut(1)), probe, amp[0], (left, left_t, right, right_t, rows, cols), far, win, grad, add_probe)
    scale = step[:1, :1]
    for k in range(2):
        g = jnp.concatenate([grad[k] * scale, jnp.zeros((frame - WIN, WIN), jnp.float32)], axis=0)
        g = pltpu.roll(g, row, 0)
        g = jnp.concatenate([g, jnp.zeros((frame, HALO), jnp.float32)], axis=1)
        g = pltpu.roll(g, col, 1)
        updated = obj[k] + g[:, :WIN]
        new_obj[k] = updated
        edge[k] = updated[:, :HALO]
        spill[k] = g[:, WIN:]


TILE_R = 384
LAST = 384 - WIN


def merge_kernel(info, obj, from_left, spill, from_right, wide, upward):
    above_col = info[0]
    keep = info[1].astype(jnp.float32)
    for k in range(2):
        left = obj[k][:, :HALO] + from_left[k]
        ext = jnp.concatenate([left, obj[k][:, HALO:], from_right[k] + spill[k] * keep], axis=1)
        wide[k] = ext
        upward[k] = pltpu.roll(ext[:HALO], lax.rem(384 - above_col, 384), 1)[:, :WIN]


def second_kernel(pos, wide, below, probe, amp, step, probe_in, left, left_t, right, right_t, rows, cols,
                  new_obj, spill, downward, probe_sum, far, win, grad):
    row, col = pos[1, 0] - LAST, pos[1, 1]
    frame = TILE_R

    def cut(k):
        upper = pltpu.roll(wide[k][LAST:], 384 - col, 1)[:, :WIN]
        tall = jnp.concatenate([upper, below[k]], axis=0)
        return pltpu.roll(tall, frame - row, 0)[:WIN]

    def add_probe(m, real, imag):
        probe_sum[m, 0] = probe_in[m, 0] + real
        probe_sum[m, 1] = probe_in[m, 1] + imag

    window_fit((cut(0), cut(1)), probe, amp[1], (left, left_t, right, right_t, rows, cols), far, win, grad, add_probe)
    scale = step[:1, :1]
    for k in range(2):
        g = jnp.concatenate([grad[k] * scale, jnp.zeros((frame - WIN, WIN), jnp.float32)], axis=0)
        g = pltpu.roll(g, row, 0)
        downward[k] = g[WIN:]
        g = jnp.concatenate([g[:WIN], jnp.zeros((WIN, HALO), jnp.float32)], axis=1)
        g = pltpu.roll(g, col, 1)
        new_obj[k, :LAST] = wide[k][:LAST, :WIN]
        new_obj[k, LAST:] = wide[k][LAST:, :WIN] + g[:, :WIN]
        spill[k, :LAST] = jnp.zeros((LAST, HALO), jnp.float32)
        spill[k, LAST:] = g[:, WIN:]


def place_kernel(info, obj, spill, from_above, new_obj, new_spill):
    above_col = info[0]
    for k in range(2):
        g = jnp.concatenate([from_above[k], jnp.zeros((HALO, HALO), jnp.float32)], axis=1)
        g = pltpu.roll(g, above_col, 1)
        new_obj[k, :HALO] = obj[k][:HALO] + g[:, :WIN]
        new_obj[k, HALO:] = obj[k][HALO:]
        new_spill[k, :HALO] = spill[k][:HALO] + g[:, WIN:]
        new_spill[k, HALO:] = spill[k][HALO:]


def call(kernel, outs, scratch, scalars, *arrays):
    vmem = pl.BlockSpec(memory_space=pltpu.VMEM)
    smem = pl.BlockSpec(memory_space=pltpu.SMEM)
    return pl.pallas_call(
        kernel,
        out_shape=[jax.ShapeDtypeStruct(s, jnp.float32) for s in outs],
        in_specs=[smem] * len(scalars) + [vmem] * len(arrays),
        out_specs=[vmem] * len(outs),
        scratch_shapes=[pltpu.VMEM(s, jnp.float32) for s in scratch],
        interpret=INTERPRET,
    )(*scalars, *arrays)


def passed_along(block, axis, distance):
    devices = range(lax.axis_size(axis))
    route = [(i - distance, i) for i in devices if i - distance in devices]
    return lax.ppermute(block, axis, route)


def exchanged(parts, axes):
    return lax.all_to_all(parts, axes, 0, 0, tiled=False)


def summed_everywhere(probe_term, core, divisor):
    plane, depth = lax.axis_size(PLANE), lax.axis_size(DEPTH)
    swap = [(0, 1), (1, 0)]
    keep = lax.dynamic_index_in_dim(probe_term, core, 0, keepdims=False)
    send = lax.dynamic_index_in_dim(probe_term, 1 - core, 0, keepdims=False)
    mode = keep + lax.ppermute(send, CORE, swap)
    parts = exchanged(mode.reshape(plane, -1, WIN), PLANE)
    share = jnp.sum(parts, axis=0)
    parts = exchanged(jnp.broadcast_to(share, (depth, *share.shape)), DEPTH)
    share = jnp.sum(parts, axis=0) / divisor
    mode = exchanged(jnp.broadcast_to(share, (plane, *share.shape)), PLANE).reshape(2, WIN, WIN)
    other = lax.ppermute(mode, CORE, swap)
    first = core == 0
    return jnp.where(first, mode, other), jnp.where(first, other, mode)


def local(object_field, probe_modes, scan_positions, amplitudes):
    tables = [jnp.asarray(t) for t in dft_constants()]
    positions = scan_positions[0, 0]
    device_count = lax.axis_size(ROW) * lax.axis_size(COL)
    divisor = math.sqrt(device_count * BATCHES)
    core = lax.axis_index(CORE)
    has_right = (lax.axis_index(COL) < lax.axis_size(COL) - 1).astype(jnp.int32)
    tile, side, probe_shape = (2, TILE_R, WIN), (2, TILE_R, HALO), (2, 2, WIN, WIN)
    fit_scratch = [(2, 2, WIN, WIN), (2, WIN, WIN), (2, WIN, WIN)]

    halo = passed_along(object_field[:, :, :HALO], COL, -1)
    above = passed_along(positions, ROW, 1)
    info = jnp.stack([above[1, 1], has_right])
    amp, step = call(before_kernel, [(BATCHES, WIN, WIN), (8, HALF)], [], [], probe_modes, amplitudes[0, 0])
    first, spill, edge, probe_sum = call(
        first_kernel, [tile, side, side, probe_shape], fit_scratch, [positions],
        object_field, halo, probe_modes, amp, step, *tables)
    from_left = passed_along(spill, COL, 1)
    from_right = passed_along(edge, COL, -1)
    wide, upward = call(
        merge_kernel, [(2, TILE_R, 384), (2, HALO, WIN)], [], [info], first, from_left, spill, from_right)
    below = passed_along(upward, ROW, -1)
    second, spill, downward, probe_sum = call(
        second_kernel, [tile, side, (2, HALO, WIN), probe_shape], fit_scratch, [positions],
        wide, below, probe_modes, amp, step, probe_sum, *tables)
    from_above = passed_along(downward, ROW, 1)
    first_mode, second_mode = summed_everywhere(probe_sum, core, divisor)
    second, spill = call(place_kernel, [tile, side], [], [info], second, spill, from_above)
    from_left = passed_along(spill, COL, 1)
    object_out = jnp.concatenate([second[:, :, :HALO] + from_left, second[:, :, HALO:]], axis=2)
    probe_out = probe_modes + jnp.stack([first_mode, second_mode])
    return (object_out, probe_out)


def solution(mesh):
    torus = Mesh(mesh.devices.reshape(4, 4, 4, 4, 2), ("row_0", "row_1", "col_0", "col_1", "col_2"))
    in_specs = (P(None, ROW, COL), P(), P(ROW, COL, None, None), P(ROW, COL, None, None, None))
    out_specs = (P(None, ROW, COL), P())
    return jax.shard_map(local, mesh=torus, in_specs=in_specs, out_specs=out_specs, check_vma=False)
```

```python
import math

import jax
import jax.numpy as jnp
import numpy as np
from jax import lax
from jax.experimental import pallas as pl
from jax.experimental.pallas import tpu as pltpu
from jax.sharding import Mesh
from jax.sharding import PartitionSpec as P


HALO = 128
BATCHES = 2
WIN = 256
HALF = 128
INTERPRET = False
ROW = ("row_0", "row_1")
COL = ("col_0", "col_1", "col_2")
PLANE = ("row_0", "col_1")
DEPTH = ("row_1", "col_0")
CORE = "col_2"


def halves(x):
    high = x.astype(jnp.bfloat16)
    low = (x - high.astype(np.float64)).astype(jnp.bfloat16)
    return high, low


def dft_constants():
    index = np.arange(HALF)
    angle = 2.0 * np.pi * (np.outer(index, index) % HALF) / HALF
    cosine = np.cos(angle) / 16.0
    sine = -np.sin(angle) / 16.0
    forward = np.block([[cosine, -sine], [sine, cosine]])
    high, low = halves(forward)
    left = np.concatenate([high, high, low], axis=1)
    left_t = np.concatenate([high.T, high.T, low.T], axis=1)
    right = np.concatenate([high, high, low], axis=0)
    right_t = np.concatenate([high.T, high.T, low.T], axis=0)
    turn = 2.0 * np.pi * index / WIN
    twiddle = np.stack([np.cos(turn), -np.sin(turn)]).astype(np.float32)
    rows = np.ascontiguousarray(np.broadcast_to(twiddle[:, :, None], (2, HALF, HALF)))
    cols = np.ascontiguousarray(np.broadcast_to(twiddle[:, None, :], (2, 8, HALF)))
    return left, left_t, right, right_t, rows, cols


def split3(x, axis):
    high = x.astype(jnp.bfloat16)
    low = (x - high.astype(jnp.float32)).astype(jnp.bfloat16)
    return jnp.concatenate([high, low, high], axis=axis)


def left_dft(matrix, x):
    return jnp.dot(matrix, split3(x, 0), preferred_element_type=jnp.float32)


def right_dft(x, matrix):
    return jnp.dot(split3(x, 1), matrix, preferred_element_type=jnp.float32)


def forward_dft(real, imag, left, right_t, twr, twc):
    t_r, t_i = twr
    c_r, c_i = twc
    a_r, b_r, a_i, b_i = real[:HALF], real[HALF:], imag[:HALF], imag[HALF:]
    d_r, d_i = a_r - b_r, a_i - b_i
    even = left_dft(left, jnp.concatenate([a_r + b_r, a_i + b_i], axis=0))
    odd = left_dft(left, jnp.concatenate([d_r * t_r - d_i * t_i, d_r * t_i + d_i * t_r], axis=0))
    real = jnp.concatenate([even[:HALF], odd[:HALF]], axis=0)
    imag = jnp.concatenate([even[HALF:], odd[HALF:]], axis=0)
    a_r, b_r, a_i, b_i = real[:, :HALF], real[:, HALF:], imag[:, :HALF], imag[:, HALF:]
    d_r, d_i = a_r - b_r, a_i - b_i
    even = right_dft(jnp.concatenate([a_r + b_r, a_i + b_i], axis=1), right_t)
    odd = right_dft(jnp.concatenate([d_r * c_r - d_i * c_i, d_r * c_i + d_i * c_r], axis=1), right_t)
    real = jnp.concatenate([even[:, :HALF], odd[:, :HALF]], axis=1)
    imag = jnp.concatenate([even[:, HALF:], odd[:, HALF:]], axis=1)
    return real, imag


def inverse_dft(real, imag, left_t, right, twr, twc):
    t_r, t_i = twr
    c_r, c_i = twc
    even = right_dft(jnp.concatenate([real[:, :HALF], imag[:, :HALF]], axis=1), right)
    odd = right_dft(jnp.concatenate([real[:, HALF:], imag[:, HALF:]], axis=1), right)
    o_r, o_i = odd[:, :HALF], odd[:, HALF:]
    o_r, o_i = o_r * c_r + o_i * c_i, o_i * c_r - o_r * c_i
    e_r, e_i = even[:, :HALF], even[:, HALF:]
    real = jnp.concatenate([e_r + o_r, e_r - o_r], axis=1)
    imag = jnp.concatenate([e_i + o_i, e_i - o_i], axis=1)
    even = left_dft(left_t, jnp.concatenate([real[:HALF], imag[:HALF]], axis=0))
    odd = left_dft(left_t, jnp.concatenate([real[HALF:], imag[HALF:]], axis=0))
    o_r, o_i = odd[:HALF], odd[HALF:]
    o_r, o_i = o_r * t_r + o_i * t_i, o_i * t_r - o_r * t_i
    e_r, e_i = even[:HALF], even[HALF:]
    real = jnp.concatenate([e_r + o_r, e_r - o_r], axis=0)
    imag = jnp.concatenate([e_i + o_i, e_i - o_i], axis=0)
    return real, imag


def window_fit(window, probe, amplitude, tables, far, window_ref, gradient, add_probe):
    left, left_t, right, right_t, rows, cols = tables
    window_ref[0] = window[0]
    window_ref[1] = window[1]

    def twiddles():
        twr = tuple(jnp.concatenate([rows[k], rows[k]], axis=1) for k in range(2))
        twc = tuple(cols[k][:1] for k in range(2))
        return twr, twc

    def outward(m, carry):
        twr, twc = twiddles()
        w_r, w_i = window_ref[0], window_ref[1]
        p_r, p_i = probe[m, 0], probe[m, 1]
        f_r, f_i = forward_dft(p_r * w_r - p_i * w_i, p_r * w_i + p_i * w_r, left[...], right_t[...], twr, twc)
        far[m, 0] = f_r
        far[m, 1] = f_i
        return carry

    lax.fori_loop(0, 2, outward, 0)
    intensity = far[0, 0] * far[0, 0] + far[0, 1] * far[0, 1]
    intensity = intensity + (far[1, 0] * far[1, 0] + far[1, 1] * far[1, 1])
    factor = amplitude / jnp.sqrt(jnp.maximum(intensity, 0.1)) - 1.0
    for m in range(2):
        far[m, 0] = far[m, 0] * factor
        far[m, 1] = far[m, 1] * factor
    gradient[...] = jnp.zeros(gradient.shape, jnp.float32)

    def inward(m, carry):
        twr, twc = twiddles()
        x_r, x_i = inverse_dft(far[m, 0], far[m, 1], left_t[...], right[...], twr, twc)
        w_r, w_i = window_ref[0], window_ref[1]
        p_r, p_i = probe[m, 0], probe[m, 1]
        gradient[0] += p_r * x_r + p_i * x_i
        gradient[1] += p_r * x_i - p_i * x_r
        add_probe(m, w_r * x_r + w_i * x_i, w_r * x_i - w_i * x_r)
        return carry

    lax.fori_loop(0, 2, inward, 0)


def before_kernel(probe, amp, amp_out, step_out):
    out_at = lax.broadcasted_iota(jnp.int32, (WIN, WIN), 0)
    in_at = lax.broadcasted_iota(jnp.int32, (WIN, WIN), 1)
    wanted = jnp.where(out_at < HALF, 2 * out_at, 2 * (out_at - HALF) + 1)
    pick = jnp.where(in_at == wanted, 1.0, 0.0).astype(jnp.bfloat16)
    for b in range(BATCHES):
        rows = jnp.dot(pick, amp[b], preferred_element_type=jnp.float32).astype(jnp.bfloat16)
        amp_out[b] = lax.dot_general(rows, pick, (((1,), (1,)), ((), ())), preferred_element_type=jnp.float32)
    total = jnp.zeros((8, HALF), jnp.float32)
    for m in range(2):
        for k in range(2):
            square = probe[m, k] * probe[m, k]
            square = jnp.sum(square.reshape(WIN // 8, 8, WIN), axis=0)
            total = total + square[:, :HALF] + square[:, HALF:]
    power = jnp.sum(total) / (WIN * WIN)
    step_out[...] = jnp.full((8, HALF), 1.0, jnp.float32) / (power + 1e-06)


TILE_R = 384
LAST = TILE_R - WIN
WIDE = WIN + HALO


def first_kernel(pos, above, obj, halo, probe, amp, step, left, left_t, right, right_t, rows, cols,
                 new_obj, spill, edge, middle, probe_sum, far, win, grad):
    row, col = pos[0, 0], pos[0, 1]

    def cut(k):
        wide = jnp.concatenate([obj[k], halo[k]], axis=1)
        wide = pltpu.roll(wide, WIDE - col, 1)[:, :WIN]
        return pltpu.roll(wide, lax.rem(TILE_R - row, TILE_R), 0)[:WIN]

    def add_probe(m, real, imag):
        probe_sum[m, 0] = real
        probe_sum[m, 1] = imag

    window_fit((cut(0), cut(1)), probe, amp[0], (left, left_t, right, right_t, rows, cols), far, win, grad, add_probe)
    scale = step[:1, :1]
    for k in range(2):
        g = jnp.concatenate([grad[k] * scale, jnp.zeros((TILE_R - WIN, WIN), jnp.float32)], axis=0)
        g = pltpu.roll(g, row, 0)
        g = jnp.concatenate([g, jnp.zeros((TILE_R, HALO), jnp.float32)], axis=1)
        g = pltpu.roll(g, col, 1)
        updated = obj[k] + g[:, :WIN]
        new_obj[k] = updated
        edge[k] = updated[:, :HALO]
        middle[k] = updated[:HALO, HALO:]
        spill[k] = g[:, WIN:]


def lanes():
    return lax.broadcasted_iota(jnp.int32, (HALO, HALO), 1)


def upward_kernel(info, edge, from_left, from_right, spill, upward):
    keep = info[1].astype(jnp.float32)
    for k in range(2):
        own = edge[k, :HALO] + from_left[k, :HALO]
        upward[k] = jnp.where(lanes() >= info[0], own, from_right[k, :HALO] + spill[k, :HALO] * keep)


def second_kernel(pos, info, obj, from_left, from_right, spill, below_mid, below_rest, probe, amp, step, probe_in,
                  left, left_t, right, right_t, rows, cols,
                  new_obj, new_spill, downward, keep_sum, send_sum, far, win, grad):
    row, col = pos[1, 0] - LAST, pos[1, 1]
    keep, core = info[1].astype(jnp.float32), info[2]

    def cut(k):
        upper = jnp.concatenate(
            [obj[k, LAST:, :HALO] + from_left[k, LAST:], obj[k, LAST:, HALO:], from_right[k, LAST:] + spill[k, LAST:] * keep],
            axis=1)
        lower = jnp.concatenate([below_rest[k], below_mid[k], below_rest[k]], axis=1)
        tall = pltpu.roll(jnp.concatenate([upper, lower], axis=0), WIDE - col, 1)[:, :WIN]
        return pltpu.roll(tall, lax.rem(TILE_R - row, TILE_R), 0)[:WIN]

    def add_probe(m, real, imag):
        @pl.when(m == core)
        def _():
            keep_sum[0] = probe_in[m, 0] + real
            keep_sum[1] = probe_in[m, 1] + imag

        @pl.when(m != core)
        def _():
            send_sum[0] = probe_in[m, 0] + real
            send_sum[1] = probe_in[m, 1] + imag

    window_fit((cut(0), cut(1)), probe, amp[1], (left, left_t, right, right_t, rows, cols), far, win, grad, add_probe)
    scale = step[:1, :1]
    for k in range(2):
        g = jnp.concatenate([grad[k] * scale, jnp.zeros((TILE_R - WIN, WIN), jnp.float32)], axis=0)
        g = pltpu.roll(g, row, 0)
        g = jnp.concatenate([g, jnp.zeros((TILE_R, HALO), jnp.float32)], axis=1)
        g = pltpu.roll(g, col, 1)
        downward[k, :, :HALO] = g[WIN:, :HALO] + g[WIN:, WIN:]
        downward[k, :, HALO:] = g[WIN:, HALO:WIN]
        new_obj[k, :LAST, :HALO] = obj[k, :LAST, :HALO] + from_left[k, :LAST]
        new_obj[k, :LAST, HALO:] = obj[k, :LAST, HALO:]
        new_obj[k, LAST:, :HALO] = obj[k, LAST:, :HALO] + from_left[k, LAST:] + g[:WIN, :HALO]
        new_obj[k, LAST:, HALO:] = obj[k, LAST:, HALO:] + g[:WIN, HALO:WIN]
        new_spill[k] = g[:WIN, WIN:]


def spill_kernel(info, spill, from_above, new_spill):
    for k in range(2):
        new_spill[k, :HALO] = jnp.where(lanes() < info[0], from_above[k, :, :HALO], 0.0)
        new_spill[k, HALO:] = spill[k]


def object_kernel(info, obj, from_above, from_left, out):
    for k in range(2):
        fell = jnp.where(lanes() >= info[0], from_above[k, :, :HALO], 0.0)
        out[k, :HALO, :HALO] = obj[k, :HALO, :HALO] + fell + from_left[k, :HALO]
        out[k, HALO:, :HALO] = obj[k, HALO:, :HALO] + from_left[k, HALO:]
        out[k, :HALO, HALO:] = obj[k, :HALO, HALO:] + from_above[k, :, HALO:]
        out[k, HALO:, HALO:] = obj[k, HALO:, HALO:]


def probe_kernel(info, probe, own, other, out):
    core = info[2]
    out[core] = probe[core] + own[...]
    out[1 - core] = probe[1 - core] + other[...]


def call(kernel, outs, scratch, scalars, *arrays, last=False):
    vmem = pl.BlockSpec(memory_space=pltpu.VMEM)
    smem = pl.BlockSpec(memory_space=pltpu.SMEM)
    if INTERPRET or last:
        shapes = [jax.ShapeDtypeStruct(s, jnp.float32) for s in outs]
    else:
        shapes = [pltpu.VMEM(s, jnp.float32) for s in outs]
    if not INTERPRET:
        arrays = [pltpu.with_memory_space_constraint(x, pltpu.VMEM) for x in arrays]
    return pl.pallas_call(
        kernel,
        out_shape=shapes,
        in_specs=[smem] * len(scalars) + [vmem] * len(arrays),
        out_specs=[vmem] * len(outs),
        scratch_shapes=[pltpu.VMEM(s, jnp.float32) for s in scratch],
        compiler_params=pltpu.CompilerParams(vmem_limit_bytes=24 * 1024 * 1024),
        interpret=INTERPRET,
    )(*scalars, *arrays)


def passed_along(block, axis, distance):
    devices = range(lax.axis_size(axis))
    route = [(i - distance, i) for i in devices if i - distance in devices]
    return lax.ppermute(block, axis, route)


def exchanged(parts, axes):
    return lax.all_to_all(parts, axes, 0, 0, tiled=False)


def swapped(block):
    return lax.ppermute(block, CORE, [(0, 1), (1, 0)])


def summed_everywhere(keep, send, divisor):
    plane, depth = lax.axis_size(PLANE), lax.axis_size(DEPTH)
    mode = keep + swapped(send)
    parts = exchanged(mode.reshape(plane, -1, WIN), PLANE)
    share = jnp.sum(parts, axis=0)
    parts = exchanged(jnp.broadcast_to(share, (depth, *share.shape)), DEPTH)
    share = jnp.sum(parts, axis=0) / divisor
    mode = exchanged(jnp.broadcast_to(share, (plane, *share.shape)), PLANE).reshape(2, WIN, WIN)
    return mode, swapped(mode)


def step_once(object_field, probe_modes, scan_positions, amplitudes):
    tables = [jnp.asarray(t) for t in dft_constants()]
    positions = scan_positions[0, 0]
    device_count = lax.axis_size(ROW) * lax.axis_size(COL)
    divisor = math.sqrt(device_count * BATCHES)
    has_right = (lax.axis_index(COL) < lax.axis_size(COL) - 1).astype(jnp.int32)
    tile, side, probe_shape = (2, TILE_R, WIN), (2, TILE_R, HALO), (2, 2, WIN, WIN)
    block = (2, HALO, HALO)
    fit_scratch = [probe_shape, (2, WIN, WIN), (2, WIN, WIN)]

    halo = passed_along(object_field[:, :, :HALO], COL, -1)
    above = passed_along(positions, ROW, 1)
    info = jnp.stack([above[1, 1], has_right, lax.axis_index(CORE)])
    amp, step = call(before_kernel, [(BATCHES, WIN, WIN), (8, HALF)], [], [], probe_modes, amplitudes[0, 0])
    obj, spill, edge, middle, probe_sum = call(
        first_kernel, [tile, side, side, block, probe_shape], fit_scratch, [positions, info],
        object_field, halo, probe_modes, amp, step, *tables)
    from_left = passed_along(spill, COL, 1)
    from_right = passed_along(edge, COL, -1)
    below_mid = passed_along(middle, ROW, -1)
    (upward,) = call(upward_kernel, [block], [], [info], edge, from_left, from_right, spill)
    below_rest = passed_along(upward, ROW, -1)
    obj, spill, downward, keep, send = call(
        second_kernel, [tile, (2, WIN, HALO), (2, HALO, WIN), (2, WIN, WIN), (2, WIN, WIN)], fit_scratch, [positions, info],
        obj, from_left, from_right, spill, below_mid, below_rest, probe_modes, amp, step, probe_sum, *tables)
    from_above = passed_along(downward, ROW, 1)
    own, other = summed_everywhere(keep, send, divisor)
    (spill,) = call(spill_kernel, [side], [], [info], spill, from_above)
    from_left = passed_along(spill, COL, 1)
    (object_out,) = call(object_kernel, [tile], [], [info], obj, from_above, from_left, last=True)
    (probe_out,) = call(probe_kernel, [probe_shape], [], [info], probe_modes, own, other, last=True)
    return (object_out, probe_out)


def solution(mesh):
    torus = Mesh(mesh.devices.reshape(4, 4, 4, 4, 2), ("row_0", "row_1", "col_0", "col_1", "col_2"))
    in_specs = (P(None, ROW, COL), P(), P(ROW, COL, None, None), P(ROW, COL, None, None, None))
    out_specs = (P(None, ROW, COL), P())
    return jax.shard_map(step_once, mesh=torus, in_specs=in_specs, out_specs=out_specs, check_vma=False)
```

```python
import math

import jax
import jax.numpy as jnp
import numpy as np
from jax import lax
from jax.experimental import pallas as pl
from jax.experimental.pallas import tpu as pltpu
from jax.sharding import Mesh
from jax.sharding import PartitionSpec as P


HALO = 128
BATCHES = 2
WIN = 256
HALF = 128
INTERPRET = False
ROW = ("row_0", "row_1")
COL = ("col_0", "col_1", "col_2")
PLANE = ("row_0", "col_1")
CORE = "col_2"


def halves(x):
    high = x.astype(jnp.bfloat16)
    low = (x - high.astype(np.float64)).astype(jnp.bfloat16)
    return high, low


def dft_constants():
    index = np.arange(HALF)
    angle = 2.0 * np.pi * (np.outer(index, index) % HALF) / HALF
    cosine = np.cos(angle) / 16.0
    sine = -np.sin(angle) / 16.0
    forward = np.block([[cosine, -sine], [sine, cosine]])
    high, low = halves(forward)
    turn = 2.0 * np.pi * index / WIN
    twiddle = np.stack([np.cos(turn), -np.sin(turn)]).astype(np.float32)
    rows = np.ascontiguousarray(np.broadcast_to(twiddle[:, :, None], (2, HALF, HALF)))
    cols = np.ascontiguousarray(np.broadcast_to(twiddle[:, None, :], (2, 8, HALF)))
    return high, low, np.ascontiguousarray(high.T), np.ascontiguousarray(low.T), rows, cols


def split3(x, axis):
    high = x.astype(jnp.bfloat16)
    low = (x - high.astype(jnp.float32)).astype(jnp.bfloat16)
    return jnp.concatenate([high, low, high], axis=axis)


def left_dft(matrix, x):
    return jnp.dot(matrix, split3(x, 0), preferred_element_type=jnp.float32)


def right_dft(x, matrix):
    return jnp.dot(split3(x, 1), matrix, preferred_element_type=jnp.float32)


def forward_dft(real, imag, left, right_t, twr, twc):
    t_r, t_i = twr
    c_r, c_i = twc
    a_r, b_r, a_i, b_i = real[:HALF], real[HALF:], imag[:HALF], imag[HALF:]
    d_r, d_i = a_r - b_r, a_i - b_i
    even = left_dft(left, jnp.concatenate([a_r + b_r, a_i + b_i], axis=0))
    odd = left_dft(left, jnp.concatenate([d_r * t_r - d_i * t_i, d_r * t_i + d_i * t_r], axis=0))
    real = jnp.concatenate([even[:HALF], odd[:HALF]], axis=0)
    imag = jnp.concatenate([even[HALF:], odd[HALF:]], axis=0)
    a_r, b_r, a_i, b_i = real[:, :HALF], real[:, HALF:], imag[:, :HALF], imag[:, HALF:]
    d_r, d_i = a_r - b_r, a_i - b_i
    even = right_dft(jnp.concatenate([a_r + b_r, a_i + b_i], axis=1), right_t)
    odd = right_dft(jnp.concatenate([d_r * c_r - d_i * c_i, d_r * c_i + d_i * c_r], axis=1), right_t)
    real = jnp.concatenate([even[:, :HALF], odd[:, :HALF]], axis=1)
    imag = jnp.concatenate([even[:, HALF:], odd[:, HALF:]], axis=1)
    return real, imag


def inverse_dft(real, imag, left_t, right, twr, twc):
    t_r, t_i = twr
    c_r, c_i = twc
    even = right_dft(jnp.concatenate([real[:, :HALF], imag[:, :HALF]], axis=1), right)
    odd = right_dft(jnp.concatenate([real[:, HALF:], imag[:, HALF:]], axis=1), right)
    o_r, o_i = odd[:, :HALF], odd[:, HALF:]
    o_r, o_i = o_r * c_r + o_i * c_i, o_i * c_r - o_r * c_i
    e_r, e_i = even[:, :HALF], even[:, HALF:]
    real = jnp.concatenate([e_r + o_r, e_r - o_r], axis=1)
    imag = jnp.concatenate([e_i + o_i, e_i - o_i], axis=1)
    even = left_dft(left_t, jnp.concatenate([real[:HALF], imag[:HALF]], axis=0))
    odd = left_dft(left_t, jnp.concatenate([real[HALF:], imag[HALF:]], axis=0))
    o_r, o_i = odd[:HALF], odd[HALF:]
    o_r, o_i = o_r * t_r + o_i * t_i, o_i * t_r - o_r * t_i
    e_r, e_i = even[:HALF], even[HALF:]
    real = jnp.concatenate([e_r + o_r, e_r - o_r], axis=0)
    imag = jnp.concatenate([e_i + o_i, e_i - o_i], axis=0)
    return real, imag


def left_of(high, low):
    return jnp.concatenate([high[...], high[...], low[...]], axis=1)


def right_of(high, low):
    return jnp.concatenate([high[...], high[...], low[...]], axis=0)


def window_fit(window, probe, amplitude, tables, far, window_ref, gradient, add_probe):
    high, low, high_t, low_t, rows, cols = tables
    window_ref[0] = window[0]
    window_ref[1] = window[1]

    def twiddles():
        twr = tuple(jnp.concatenate([rows[k], rows[k]], axis=1) for k in range(2))
        twc = tuple(cols[k][:1] for k in range(2))
        return twr, twc

    def outward(m, carry):
        twr, twc = twiddles()
        w_r, w_i = window_ref[0], window_ref[1]
        p_r, p_i = probe[m, 0], probe[m, 1]
        f_r, f_i = forward_dft(p_r * w_r - p_i * w_i, p_r * w_i + p_i * w_r,
                               left_of(high, low), right_of(high_t, low_t), twr, twc)
        far[m, 0] = f_r
        far[m, 1] = f_i
        return carry

    lax.fori_loop(0, 2, outward, 0)
    intensity = far[0, 0] * far[0, 0] + far[0, 1] * far[0, 1]
    intensity = intensity + (far[1, 0] * far[1, 0] + far[1, 1] * far[1, 1])
    factor = amplitude / jnp.sqrt(jnp.maximum(intensity, 0.1)) - 1.0
    for m in range(2):
        far[m, 0] = far[m, 0] * factor
        far[m, 1] = far[m, 1] * factor
    gradient[...] = jnp.zeros(gradient.shape, jnp.float32)

    def inward(m, carry):
        twr, twc = twiddles()
        x_r, x_i = inverse_dft(far[m, 0], far[m, 1], left_of(high_t, low_t), right_of(high, low), twr, twc)
        w_r, w_i = window_ref[0], window_ref[1]
        p_r, p_i = probe[m, 0], probe[m, 1]
        gradient[0] += p_r * x_r + p_i * x_i
        gradient[1] += p_r * x_i - p_i * x_r
        add_probe(m, w_r * x_r + w_i * x_i, w_r * x_i - w_i * x_r)
        return carry

    lax.fori_loop(0, 2, inward, 0)


def before_kernel(probe, amp, amp_out, step_out):
    out_at = lax.broadcasted_iota(jnp.int32, (WIN, WIN), 0)
    in_at = lax.broadcasted_iota(jnp.int32, (WIN, WIN), 1)
    wanted = jnp.where(out_at < HALF, 2 * out_at, 2 * (out_at - HALF) + 1)
    pick = jnp.where(in_at == wanted, 1.0, 0.0).astype(jnp.bfloat16)
    for b in range(BATCHES):
        rows = jnp.dot(pick, amp[b], preferred_element_type=jnp.float32).astype(jnp.bfloat16)
        amp_out[b] = lax.dot_general(rows, pick, (((1,), (1,)), ((), ())), preferred_element_type=jnp.float32)
    total = jnp.zeros((8, HALF), jnp.float32)
    for m in range(2):
        for k in range(2):
            square = probe[m, k] * probe[m, k]
            square = jnp.sum(square.reshape(WIN // 8, 8, WIN), axis=0)
            total = total + square[:, :HALF] + square[:, HALF:]
    power = jnp.sum(total) / (WIN * WIN)
    step_out[...] = jnp.full((8, HALF), 1.0, jnp.float32) / (power + 1e-06)


TILE_R = 384
LAST = TILE_R - WIN
WIDE = WIN + HALO


def first_kernel(pos, obj, halo, probe, amp, step, high, low, high_t, low_t, rows, cols,
                 new_obj, spill, edge, middle, probe_sum, far, win, grad):
    row, col = pos[0, 0], pos[0, 1]

    def cut(k):
        wide = jnp.concatenate([obj[k], halo[k]], axis=1)
        wide = pltpu.roll(wide, WIDE - col, 1)[:, :WIN]
        return pltpu.roll(wide, lax.rem(TILE_R - row, TILE_R), 0)[:WIN]

    def add_probe(m, real, imag):
        probe_sum[m, 0] = real
        probe_sum[m, 1] = imag

    window_fit((cut(0), cut(1)), probe, amp[0], (high, low, high_t, low_t, rows, cols), far, win, grad, add_probe)
    scale = step[:1, :1]
    for k in range(2):
        g = jnp.concatenate([grad[k] * scale, jnp.zeros((TILE_R - WIN, WIN), jnp.float32)], axis=0)
        g = pltpu.roll(g, row, 0)
        g = jnp.concatenate([g, jnp.zeros((TILE_R, HALO), jnp.float32)], axis=1)
        g = pltpu.roll(g, col, 1)
        updated = obj[k] + g[:, :WIN]
        new_obj[k] = updated
        edge[k] = updated[:, :HALO]
        middle[k] = updated[:HALO, HALO:]
        spill[k] = g[:, WIN:]


def lanes():
    return lax.broadcasted_iota(jnp.int32, (HALO, HALO), 1)


def upward_kernel(above, info, edge, from_left, from_right, spill, upward):
    keep = info[0].astype(jnp.float32)
    for k in range(2):
        own = edge[k, :HALO] + from_left[k, :HALO]
        upward[k] = jnp.where(lanes() >= above[1, 1], own, from_right[k, :HALO] + spill[k, :HALO] * keep)


def second_kernel(pos, info, obj, from_left, from_right, spill, below_mid, below_rest, probe, amp, step, probe_in,
                  high, low, high_t, low_t, rows, cols,
                  new_obj, new_spill, downward, keep_sum, send_sum, far, win, grad):
    row, col = pos[1, 0] - LAST, pos[1, 1]
    keep, core = info[0].astype(jnp.float32), info[1]

    def cut(k):
        upper = jnp.concatenate(
            [obj[k, LAST:, :HALO] + from_left[k, LAST:], obj[k, LAST:, HALO:], from_right[k, LAST:] + spill[k, LAST:] * keep],
            axis=1)
        lower = jnp.concatenate([below_rest[k], below_mid[k], below_rest[k]], axis=1)
        tall = pltpu.roll(jnp.concatenate([upper, lower], axis=0), WIDE - col, 1)[:, :WIN]
        return pltpu.roll(tall, lax.rem(TILE_R - row, TILE_R), 0)[:WIN]

    def add_probe(m, real, imag):
        @pl.when(m == core)
        def _():
            keep_sum[0] = probe_in[m, 0] + real
            keep_sum[1] = probe_in[m, 1] + imag

        @pl.when(m != core)
        def _():
            send_sum[0] = probe_in[m, 0] + real
            send_sum[1] = probe_in[m, 1] + imag

    window_fit((cut(0), cut(1)), probe, amp[1], (high, low, high_t, low_t, rows, cols), far, win, grad, add_probe)
    scale = step[:1, :1]
    for k in range(2):
        g = jnp.concatenate([grad[k] * scale, jnp.zeros((TILE_R - WIN, WIN), jnp.float32)], axis=0)
        g = pltpu.roll(g, row, 0)
        g = jnp.concatenate([g, jnp.zeros((TILE_R, HALO), jnp.float32)], axis=1)
        g = pltpu.roll(g, col, 1)
        downward[k] = g[WIN:, :WIN]
        new_obj[k, :LAST, :HALO] = obj[k, :LAST, :HALO] + from_left[k, :LAST]
        new_obj[k, :LAST, HALO:] = obj[k, :LAST, HALO:]
        new_obj[k, LAST:, :HALO] = obj[k, LAST:, :HALO] + from_left[k, LAST:] + g[:WIN, :HALO]
        new_obj[k, LAST:, HALO:] = obj[k, LAST:, HALO:] + g[:WIN, HALO:WIN]
        new_spill[k] = g[:, WIN:]


def down_kernel(downward, from_left, out):
    for k in range(2):
        out[k, :, :HALO] = downward[k, :, :HALO] + from_left[k, WIN:]
        out[k, :, HALO:] = downward[k, :, HALO:]


def object_kernel(obj, from_left, from_above, out):
    for k in range(2):
        out[k, :LAST] = obj[k, :LAST] + from_above[k]
        out[k, LAST:, :HALO] = obj[k, LAST:, :HALO] + from_left[k, :WIN]
        out[k, LAST:, HALO:] = obj[k, LAST:, HALO:]


def probe_kernel(info, probe, own, other, out):
    core = info[1]
    out[core] = probe[core] + own[...]
    out[1 - core] = probe[1 - core] + other[...]


def call(kernel, outs, scratch, scalars, *arrays, last=False):
    vmem = pl.BlockSpec(memory_space=pltpu.VMEM)
    smem = pl.BlockSpec(memory_space=pltpu.SMEM)
    if INTERPRET or last:
        shapes = [jax.ShapeDtypeStruct(s, jnp.float32) for s in outs]
    else:
        shapes = [pltpu.VMEM(s, jnp.float32) for s in outs]
    if not INTERPRET:
        arrays = [pltpu.with_memory_space_constraint(x, pltpu.VMEM) for x in arrays]
    return pl.pallas_call(
        kernel,
        out_shape=shapes,
        in_specs=[smem] * len(scalars) + [vmem] * len(arrays),
        out_specs=[vmem] * len(outs),
        scratch_shapes=[pltpu.VMEM(s, jnp.float32) for s in scratch],
        compiler_params=pltpu.CompilerParams(vmem_limit_bytes=24 * 1024 * 1024),
        interpret=INTERPRET,
    )(*scalars, *arrays)


def passed_along(block, axis, distance):
    devices = range(lax.axis_size(axis))
    route = [(i - distance, i) for i in devices if i - distance in devices]
    return lax.ppermute(block, axis, route)


def exchanged(parts, axes):
    return lax.all_to_all(parts, axes, 0, 0, tiled=False)


def swapped(block):
    return lax.ppermute(block, CORE, [(0, 1), (1, 0)])


def summed_everywhere(keep, send, divisor):
    plane = lax.axis_size(PLANE)
    mode = keep + swapped(send)
    parts = exchanged(mode.reshape(plane, -1, WIN), PLANE)
    share = jnp.sum(parts, axis=0)
    for axis in ("col_0", "row_1"):
        parts = exchanged(jnp.broadcast_to(share, (lax.axis_size(axis), *share.shape)), axis)
        share = jnp.sum(parts, axis=0)
    share = share / divisor
    mode = exchanged(jnp.broadcast_to(share, (plane, *share.shape)), PLANE).reshape(2, WIN, WIN)
    return mode, swapped(mode)


def step_once(object_field, probe_modes, scan_positions, amplitudes):
    tables = [jnp.asarray(t) for t in dft_constants()]
    positions = scan_positions[0, 0]
    device_count = lax.axis_size(ROW) * lax.axis_size(COL)
    divisor = math.sqrt(device_count * BATCHES)
    has_right = (lax.axis_index(COL) < lax.axis_size(COL) - 1).astype(jnp.int32)
    tile, side, probe_shape = (2, TILE_R, WIN), (2, TILE_R, HALO), (2, 2, WIN, WIN)
    block = (2, HALO, HALO)
    fit_scratch = [probe_shape, (2, WIN, WIN), (2, WIN, WIN)]

    halo = passed_along(object_field[:, :, :HALO], COL, -1)
    above = passed_along(positions, ROW, 1)
    info = jnp.stack([has_right, lax.axis_index(CORE)])
    amp, step = call(before_kernel, [(BATCHES, WIN, WIN), (8, HALF)], [], [], probe_modes, amplitudes[0, 0])
    obj, spill, edge, middle, probe_sum = call(
        first_kernel, [tile, side, side, block, probe_shape], fit_scratch, [positions],
        object_field, halo, probe_modes, amp, step, *tables)
    from_left = passed_along(spill, COL, 1)
    from_right = passed_along(edge, COL, -1)
    below_mid = passed_along(middle, ROW, -1)
    (upward,) = call(upward_kernel, [block], [], [above, info], edge, from_left, from_right, spill)
    below_rest = passed_along(upward, ROW, -1)
    obj, spill, downward, keep, send = call(
        second_kernel, [tile, side, (2, HALO, WIN), (2, WIN, WIN), (2, WIN, WIN)], fit_scratch, [positions, info],
        obj, from_left, from_right, spill, below_mid, below_rest, probe_modes, amp, step, probe_sum, *tables)
    own, other = summed_everywhere(keep, send, divisor)
    from_left = passed_along(spill, COL, 1)
    (downward,) = call(down_kernel, [(2, HALO, WIN)], [], [], downward, from_left)
    from_above = passed_along(downward, ROW, 1)
    (object_out,) = call(object_kernel, [tile], [], [], obj, from_left, from_above, last=True)
    (probe_out,) = call(probe_kernel, [probe_shape], [], [info], probe_modes, own, other, last=True)
    return (object_out, probe_out)


def solution(mesh):
    torus = Mesh(mesh.devices.reshape(4, 4, 4, 4, 2), ("row_0", "row_1", "col_0", "col_1", "col_2"))
    in_specs = (P(None, ROW, COL), P(), P(ROW, COL, None, None), P(ROW, COL, None, None, None))
    out_specs = (P(None, ROW, COL), P())
    return jax.shard_map(step_once, mesh=torus, in_specs=in_specs, out_specs=out_specs, check_vma=False)
```

```python
import math

import jax
import jax.numpy as jnp
import numpy as np
from jax import lax
from jax.experimental import pallas as pl
from jax.experimental.pallas import tpu as pltpu
from jax.sharding import Mesh
from jax.sharding import PartitionSpec as P


HALO = 128
BATCHES = 2
WIN = 256
HALF = 128
INTERPRET = False
ROW = ("row_0", "row_1")
COL = ("col_0", "col_1", "col_2")
PLANE = ("row_0", "col_1")
CORE = "col_2"


def halves(x):
    high = x.astype(jnp.bfloat16)
    low = (x - high.astype(np.float64)).astype(jnp.bfloat16)
    return high, low


def dft_constants():
    index = np.arange(HALF)
    angle = 2.0 * np.pi * (np.outer(index, index) % HALF) / HALF
    cosine = np.cos(angle) / 16.0
    sine = -np.sin(angle) / 16.0
    forward = np.block([[cosine, -sine], [sine, cosine]])
    high, low = halves(forward)
    turn = 2.0 * np.pi * index / WIN
    twiddle = np.stack([np.cos(turn), -np.sin(turn)]).astype(np.float32)
    rows = np.ascontiguousarray(np.broadcast_to(twiddle[:, :, None], (2, HALF, HALF)))
    cols = np.ascontiguousarray(np.broadcast_to(twiddle[:, None, :], (2, 8, HALF)))
    return high, low, np.ascontiguousarray(high.T), np.ascontiguousarray(low.T), rows, cols


def split3(x, axis):
    high = x.astype(jnp.bfloat16)
    low = (x - high.astype(jnp.float32)).astype(jnp.bfloat16)
    return jnp.concatenate([high, low, high], axis=axis)


def left_dft(matrix, x):
    return jnp.dot(matrix, split3(x, 0), preferred_element_type=jnp.float32)


def right_dft(x, matrix):
    return jnp.dot(split3(x, 1), matrix, preferred_element_type=jnp.float32)


def forward_dft(real, imag, left, right_t, twr, twc):
    t_r, t_i = twr
    c_r, c_i = twc
    a_r, b_r, a_i, b_i = real[:HALF], real[HALF:], imag[:HALF], imag[HALF:]
    d_r, d_i = a_r - b_r, a_i - b_i
    even = left_dft(left, jnp.concatenate([a_r + b_r, a_i + b_i], axis=0))
    odd = left_dft(left, jnp.concatenate([d_r * t_r - d_i * t_i, d_r * t_i + d_i * t_r], axis=0))
    real = jnp.concatenate([even[:HALF], odd[:HALF]], axis=0)
    imag = jnp.concatenate([even[HALF:], odd[HALF:]], axis=0)
    a_r, b_r, a_i, b_i = real[:, :HALF], real[:, HALF:], imag[:, :HALF], imag[:, HALF:]
    d_r, d_i = a_r - b_r, a_i - b_i
    even = right_dft(jnp.concatenate([a_r + b_r, a_i + b_i], axis=1), right_t)
    odd = right_dft(jnp.concatenate([d_r * c_r - d_i * c_i, d_r * c_i + d_i * c_r], axis=1), right_t)
    real = jnp.concatenate([even[:, :HALF], odd[:, :HALF]], axis=1)
    imag = jnp.concatenate([even[:, HALF:], odd[:, HALF:]], axis=1)
    return real, imag


def inverse_dft(real, imag, left_t, right, twr, twc):
    t_r, t_i = twr
    c_r, c_i = twc
    even = right_dft(jnp.concatenate([real[:, :HALF], imag[:, :HALF]], axis=1), right)
    odd = right_dft(jnp.concatenate([real[:, HALF:], imag[:, HALF:]], axis=1), right)
    o_r, o_i = odd[:, :HALF], odd[:, HALF:]
    o_r, o_i = o_r * c_r + o_i * c_i, o_i * c_r - o_r * c_i
    e_r, e_i = even[:, :HALF], even[:, HALF:]
    real = jnp.concatenate([e_r + o_r, e_r - o_r], axis=1)
    imag = jnp.concatenate([e_i + o_i, e_i - o_i], axis=1)
    even = left_dft(left_t, jnp.concatenate([real[:HALF], imag[:HALF]], axis=0))
    odd = left_dft(left_t, jnp.concatenate([real[HALF:], imag[HALF:]], axis=0))
    o_r, o_i = odd[:HALF], odd[HALF:]
    o_r, o_i = o_r * t_r + o_i * t_i, o_i * t_r - o_r * t_i
    e_r, e_i = even[:HALF], even[HALF:]
    real = jnp.concatenate([e_r + o_r, e_r - o_r], axis=0)
    imag = jnp.concatenate([e_i + o_i, e_i - o_i], axis=0)
    return real, imag


def left_of(high, low):
    return jnp.concatenate([high[...], high[...], low[...]], axis=1)


def right_of(high, low):
    return jnp.concatenate([high[...], high[...], low[...]], axis=0)


def window_fit(window, probe, amplitude, tables, far, window_ref, gradient, add_probe, probe_copy, amp_copy):
    high, low, high_t, low_t, rows, cols = tables
    window_ref[0] = window[0]
    window_ref[1] = window[1]

    def twiddles():
        twr = tuple(jnp.concatenate([rows[k], rows[k]], axis=1) for k in range(2))
        twc = tuple(cols[k][:1] for k in range(2))
        return twr, twc

    def outward(m, carry):
        probe_copy(m).wait()
        twr, twc = twiddles()
        w_r, w_i = window_ref[0], window_ref[1]
        p_r, p_i = probe[m, 0], probe[m, 1]
        f_r, f_i = forward_dft(p_r * w_r - p_i * w_i, p_r * w_i + p_i * w_r,
                               left_of(high, low), right_of(high_t, low_t), twr, twc)
        far[m, 0] = f_r
        far[m, 1] = f_i
        return carry

    lax.fori_loop(0, 2, outward, 0)
    intensity = far[0, 0] * far[0, 0] + far[0, 1] * far[0, 1]
    intensity = intensity + (far[1, 0] * far[1, 0] + far[1, 1] * far[1, 1])
    amp_copy.wait()
    factor = amplitude[...] / jnp.sqrt(jnp.maximum(intensity, 0.1)) - 1.0
    for m in range(2):
        far[m, 0] = far[m, 0] * factor
        far[m, 1] = far[m, 1] * factor
    gradient[...] = jnp.zeros(gradient.shape, jnp.float32)

    def inward(m, carry):
        twr, twc = twiddles()
        x_r, x_i = inverse_dft(far[m, 0], far[m, 1], left_of(high_t, low_t), right_of(high, low), twr, twc)
        w_r, w_i = window_ref[0], window_ref[1]
        p_r, p_i = probe[m, 0], probe[m, 1]
        gradient[0] += p_r * x_r + p_i * x_i
        gradient[1] += p_r * x_i - p_i * x_r
        add_probe(m, w_r * x_r + w_i * x_i, w_r * x_i - w_i * x_r)
        return carry

    lax.fori_loop(0, 2, inward, 0)


def before_kernel(probe_hbm, amp_hbm, amp_out, step_out, probe, amp, ordered, sems):
    amp_copy = pltpu.make_async_copy(amp_hbm, amp, sems.at[0])
    probe_copy = pltpu.make_async_copy(probe_hbm, probe, sems.at[1])
    out_copy = lambda b: pltpu.make_async_copy(ordered.at[b], amp_out.at[b], sems.at[2 + b])
    amp_copy.start()
    probe_copy.start()
    out_at = lax.broadcasted_iota(jnp.int32, (WIN, WIN), 0)
    in_at = lax.broadcasted_iota(jnp.int32, (WIN, WIN), 1)
    wanted = jnp.where(out_at < HALF, 2 * out_at, 2 * (out_at - HALF) + 1)
    pick = jnp.where(in_at == wanted, 1.0, 0.0).astype(jnp.bfloat16)
    amp_copy.wait()
    for b in range(BATCHES):
        rows = jnp.dot(pick, amp[b], preferred_element_type=jnp.float32).astype(jnp.bfloat16)
        ordered[b] = lax.dot_general(rows, pick, (((1,), (1,)), ((), ())), preferred_element_type=jnp.float32)
        out_copy(b).start()
    probe_copy.wait()
    total = jnp.zeros((8, HALF), jnp.float32)
    for m in range(2):
        for k in range(2):
            square = probe[m, k] * probe[m, k]
            square = jnp.sum(square.reshape(WIN // 8, 8, WIN), axis=0)
            total = total + square[:, :HALF] + square[:, HALF:]
    power = jnp.sum(total) / (WIN * WIN)
    step_out[...] = jnp.full((8, HALF), 1.0, jnp.float32) / (power + 1e-06)
    for b in range(BATCHES):
        out_copy(b).wait()


TILE_R = 384
LAST = TILE_R - WIN
WIDE = WIN + HALO


def first_kernel(pos, obj, halo, probe_hbm, amp_hbm, step, high, low, high_t, low_t, rows, cols,
                 obj_hbm, spill, edge, middle, sum_hbm, far, win, grad, probe, amp, new_obj, probe_sum, sems):
    row, col = pos[0, 0], pos[0, 1]
    probe_copy = lambda m: pltpu.make_async_copy(probe_hbm.at[m], probe.at[m], sems.at[m])
    sum_copy = lambda m: pltpu.make_async_copy(probe_sum.at[m], sum_hbm.at[m], sems.at[2 + m])
    obj_copy = lambda k: pltpu.make_async_copy(new_obj.at[k], obj_hbm.at[k], sems.at[4 + k])
    amp_copy = pltpu.make_async_copy(amp_hbm.at[0], amp, sems.at[6])
    probe_copy(0).start()
    probe_copy(1).start()
    amp_copy.start()

    def cut(k):
        wide = jnp.concatenate([obj[k], halo[k]], axis=1)
        wide = pltpu.roll(wide, WIDE - col, 1)[:, :WIN]
        return pltpu.roll(wide, lax.rem(TILE_R - row, TILE_R), 0)[:WIN]

    def add_probe(m, real, imag):
        probe_sum[m, 0] = real
        probe_sum[m, 1] = imag
        sum_copy(m).start()

    window_fit((cut(0), cut(1)), probe, amp, (high, low, high_t, low_t, rows, cols), far, win, grad, add_probe,
               probe_copy, amp_copy)
    scale = step[:1, :1]
    for k in range(2):
        g = jnp.concatenate([grad[k] * scale, jnp.zeros((TILE_R - WIN, WIN), jnp.float32)], axis=0)
        g = pltpu.roll(g, row, 0)
        g = jnp.concatenate([g, jnp.zeros((TILE_R, HALO), jnp.float32)], axis=1)
        g = pltpu.roll(g, col, 1)
        updated = obj[k] + g[:, :WIN]
        new_obj[k] = updated
        obj_copy(k).start()
        edge[k] = updated[:, :HALO]
        middle[k] = updated[:HALO, HALO:]
        spill[k] = g[:, WIN:]
    for k in range(2):
        sum_copy(k).wait()
        obj_copy(k).wait()


def lanes():
    return lax.broadcasted_iota(jnp.int32, (HALO, HALO), 1)


def upward_kernel(above, info, edge, from_left, from_right, spill, upward):
    keep = info[0].astype(jnp.float32)
    for k in range(2):
        own = edge[k, :HALO] + from_left[k, :HALO]
        upward[k] = jnp.where(lanes() >= above[1, 1], own, from_right[k, :HALO] + spill[k, :HALO] * keep)


def merge_kernel(info, obj, from_left, from_right, spill, whole, source):
    keep = info[0].astype(jnp.float32)
    for k in range(2):
        left = obj[k, :, :HALO] + from_left[k]
        whole[k, :, :HALO] = left
        whole[k, :, HALO:] = obj[k, :, HALO:]
        source[k, :, :HALO] = left[LAST:]
        source[k, :, HALO:WIN] = obj[k, LAST:, HALO:]
        source[k, :, WIN:] = from_right[k, LAST:] + spill[k, LAST:] * keep


def second_kernel(pos, info, source, below_mid, below_rest, probe_hbm, amp_hbm, step, before_hbm,
                  high, low, high_t, low_t, rows, cols,
                  grad_hbm, spill, downward, keep_sum, send_sum, far, win, grad, probe, amp, own_grad, before, sems):
    row, col, core = pos[1, 0] - LAST, pos[1, 1], info[1]
    probe_copy = lambda m: pltpu.make_async_copy(probe_hbm.at[m], probe.at[m], sems.at[m])
    before_copy = lambda m: pltpu.make_async_copy(before_hbm.at[m], before.at[m], sems.at[2 + m])
    grad_copy = lambda k: pltpu.make_async_copy(own_grad.at[k], grad_hbm.at[k], sems.at[4 + k])
    amp_copy = pltpu.make_async_copy(amp_hbm.at[1], amp, sems.at[6])
    probe_copy(0).start()
    probe_copy(1).start()
    amp_copy.start()
    before_copy(0).start()
    before_copy(1).start()

    def cut(k):
        lower = jnp.concatenate([below_rest[k], below_mid[k], below_rest[k]], axis=1)
        tall = pltpu.roll(jnp.concatenate([source[k], lower], axis=0), WIDE - col, 1)[:, :WIN]
        return pltpu.roll(tall, lax.rem(TILE_R - row, TILE_R), 0)[:WIN]

    def add_probe(m, real, imag):
        before_copy(m).wait()

        @pl.when(m == core)
        def _():
            keep_sum[0] = before[m, 0] + real
            keep_sum[1] = before[m, 1] + imag

        @pl.when(m != core)
        def _():
            send_sum[0] = before[m, 0] + real
            send_sum[1] = before[m, 1] + imag

    window_fit((cut(0), cut(1)), probe, amp, (high, low, high_t, low_t, rows, cols), far, win, grad, add_probe,
               probe_copy, amp_copy)
    scale = step[:1, :1]
    for k in range(2):
        g = jnp.concatenate([grad[k] * scale, jnp.zeros((TILE_R - WIN, WIN), jnp.float32)], axis=0)
        g = pltpu.roll(g, row, 0)
        g = jnp.concatenate([g, jnp.zeros((TILE_R, HALO), jnp.float32)], axis=1)
        g = pltpu.roll(g, col, 1)
        own_grad[k] = g[:WIN, :WIN]
        grad_copy(k).start()
        downward[k, :, :HALO] = g[WIN:, :HALO] + g[WIN:, WIN:]
        downward[k, :, HALO:] = g[WIN:, HALO:WIN]
        spill[k] = g[:WIN, WIN:]
    for k in range(2):
        grad_copy(k).wait()


def spill_kernel(above, spill, from_above, new_spill):
    for k in range(2):
        new_spill[k, :HALO] = jnp.where(lanes() < above[1, 1], from_above[k, :, :HALO], 0.0)
        new_spill[k, HALO:] = spill[k]


def object_kernel(above, whole, grad, from_above, from_left, out):
    for k in range(2):
        fell = jnp.where(lanes() >= above[1, 1], from_above[k, :, :HALO], 0.0)
        out[k, :LAST, :HALO] = whole[k, :LAST, :HALO] + fell + from_left[k, :LAST]
        out[k, :LAST, HALO:] = whole[k, :LAST, HALO:] + from_above[k, :, HALO:]
        out[k, LAST:, :HALO] = whole[k, LAST:, :HALO] + grad[k, :, :HALO] + from_left[k, LAST:]
        out[k, LAST:, HALO:] = whole[k, LAST:, HALO:] + grad[k, :, HALO:]


def probe_kernel(info, probe, own, other, out):
    core = info[1]
    out[core] = probe[core] + own[...]
    out[1 - core] = probe[1 - core] + other[...]


HBM = object()
AUTO = object()


def call(kernel, outs, scratch, scalars, arrays, copies=0):
    smem = pl.BlockSpec(memory_space=pltpu.SMEM)
    specs = {None: pl.BlockSpec(memory_space=pltpu.VMEM), HBM: pl.BlockSpec(memory_space=pltpu.HBM)}
    specs[AUTO] = specs[None]
    arrays = [x if isinstance(x, tuple) else (x, None) for x in arrays]
    outs = [(o[0], o[1]) if isinstance(o[0], tuple) else (o, None) for o in outs]
    spaces = {None: pltpu.VMEM, HBM: pltpu.HBM, AUTO: pltpu.HBM}
    shapes = [
        jax.ShapeDtypeStruct(shape, jnp.float32) if INTERPRET or where is AUTO else spaces[where](shape, jnp.float32)
        for shape, where in outs
    ]
    operands = [
        x if INTERPRET or where is AUTO else pltpu.with_memory_space_constraint(x, spaces[where]) for x, where in arrays
    ]
    return pl.pallas_call(
        kernel,
        out_shape=shapes,
        in_specs=[smem] * len(scalars) + [specs[where] for _, where in arrays],
        out_specs=[specs[where] for _, where in outs],
        scratch_shapes=[pltpu.VMEM(s, jnp.float32) if isinstance(s, tuple) else s for s in scratch]
        + ([pltpu.SemaphoreType.DMA((copies,))] if copies else []),
        compiler_params=pltpu.CompilerParams(vmem_limit_bytes=24 * 1024 * 1024),
        interpret=INTERPRET,
    )(*scalars, *operands)


def passed_along(block, axis, distance):
    devices = range(lax.axis_size(axis))
    route = [(i - distance, i) for i in devices if i - distance in devices]
    return lax.ppermute(block, axis, route)


def exchanged(parts, axes):
    return lax.all_to_all(parts, axes, 0, 0, tiled=False)


def swapped(block):
    return lax.ppermute(block, CORE, [(0, 1), (1, 0)])


def summed_everywhere(keep, send, divisor):
    plane = lax.axis_size(PLANE)
    mode = keep + swapped(send)
    parts = exchanged(mode.reshape(plane, -1, WIN), PLANE)
    share = jnp.sum(parts, axis=0)
    for axis in ("col_0", "row_1"):
        parts = exchanged(jnp.broadcast_to(share, (lax.axis_size(axis), *share.shape)), axis)
        share = jnp.sum(parts, axis=0)
    share = share / divisor
    mode = exchanged(jnp.broadcast_to(share, (plane, *share.shape)), PLANE).reshape(2, WIN, WIN)
    return mode, swapped(mode)


def step_once(object_field, probe_modes, scan_positions, amplitudes):
    tables = [jnp.asarray(t) for t in dft_constants()]
    positions = scan_positions[0, 0]
    device_count = lax.axis_size(ROW) * lax.axis_size(COL)
    divisor = math.sqrt(device_count * BATCHES)
    has_right = (lax.axis_index(COL) < lax.axis_size(COL) - 1).astype(jnp.int32)
    tile, side, probe_shape = (2, TILE_R, WIN), (2, TILE_R, HALO), (2, 2, WIN, WIN)
    block, window = (2, HALO, HALO), (2, WIN, WIN)
    fit_scratch = [probe_shape, window, window, probe_shape, (WIN, WIN)]

    halo = passed_along(object_field[:, :, :HALO], COL, -1)
    above = passed_along(positions, ROW, 1)
    info = jnp.stack([has_right, lax.axis_index(CORE)])
    amp, step = call(
        before_kernel, [((BATCHES, WIN, WIN), HBM), (8, HALF)],
        [probe_shape, pltpu.VMEM((BATCHES, WIN, WIN), jnp.bfloat16), (BATCHES, WIN, WIN)],
        [], [(probe_modes, HBM), (amplitudes[0, 0], HBM)], copies=4)
    obj, spill, edge, middle, probe_sum = call(
        first_kernel, [(tile, HBM), side, side, block, (probe_shape, HBM)], fit_scratch + [tile, probe_shape],
        [positions], [object_field, halo, (probe_modes, HBM), (amp, HBM), step, *tables], copies=7)
    below_mid = passed_along(middle, ROW, -1)
    from_right = passed_along(edge, COL, -1)
    from_left = passed_along(spill, COL, 1)
    (upward,) = call(upward_kernel, [block], [], [above, info], [edge, from_left, from_right, spill])
    below_rest = passed_along(upward, ROW, -1)
    whole, source = call(
        merge_kernel, [(tile, AUTO), (2, WIN, WIDE)], [], [info], [(obj, AUTO), from_left, from_right, spill])
    grad, spill, downward, keep, send = call(
        second_kernel, [(window, HBM), (2, WIN, HALO), (2, HALO, WIN), window, window],
        fit_scratch + [window, probe_shape], [positions, info],
        [source, below_mid, below_rest, (probe_modes, HBM), (amp, HBM), step, (probe_sum, HBM), *tables], copies=7)
    own, other = summed_everywhere(keep, send, divisor)
    from_above = passed_along(downward, ROW, 1)
    (spill,) = call(spill_kernel, [side], [], [above], [spill, from_above])
    from_left = passed_along(spill, COL, 1)
    (object_out,) = call(
        object_kernel, [(tile, AUTO)], [], [above], [(whole, AUTO), (grad, AUTO), from_above, from_left])
    (probe_out,) = call(probe_kernel, [(probe_shape, AUTO)], [], [info], [(probe_modes, AUTO), own, other])
    return (object_out, probe_out)


def solution(mesh):
    torus = Mesh(mesh.devices.reshape(4, 4, 4, 4, 2), ("row_0", "row_1", "col_0", "col_1", "col_2"))
    in_specs = (P(None, ROW, COL), P(), P(ROW, COL, None, None), P(ROW, COL, None, None, None))
    out_specs = (P(None, ROW, COL), P())
    return jax.shard_map(step_once, mesh=torus, in_specs=in_specs, out_specs=out_specs, check_vma=False)
```

```python
import math

import jax
import jax.numpy as jnp
import numpy as np
from jax import lax
from jax.experimental import pallas as pl
from jax.experimental.pallas import tpu as pltpu
from jax.sharding import Mesh
from jax.sharding import PartitionSpec as P


HALO = 128
BATCHES = 2
WIN = 256
HALF = 128
INTERPRET = False
ROW = ("row_0", "row_1")
COL = ("col_0", "col_1", "col_2")
PLANE = ("row_0", "col_1")
CORE = "col_2"


def halves(x):
    high = x.astype(jnp.bfloat16)
    low = (x - high.astype(np.float64)).astype(jnp.bfloat16)
    return high, low


def dft_constants():
    index = np.arange(HALF)
    angle = 2.0 * np.pi * (np.outer(index, index) % HALF) / HALF
    cosine = np.cos(angle) / 16.0
    sine = -np.sin(angle) / 16.0
    forward = np.block([[cosine, -sine], [sine, cosine]])
    high, low = halves(forward)
    turn = 2.0 * np.pi * index / WIN
    twiddle = np.stack([np.cos(turn), -np.sin(turn)]).astype(np.float32)
    rows = np.ascontiguousarray(np.broadcast_to(twiddle[:, :, None], (2, HALF, HALF)))
    cols = np.ascontiguousarray(np.broadcast_to(twiddle[:, None, :], (2, 8, HALF)))
    return high, low, np.ascontiguousarray(high.T), np.ascontiguousarray(low.T), rows, cols


def split3(x, axis):
    high = x.astype(jnp.bfloat16)
    low = (x - high.astype(jnp.float32)).astype(jnp.bfloat16)
    return jnp.concatenate([high, low, high], axis=axis)


def left_dft(matrix, x):
    return jnp.dot(matrix, split3(x, 0), preferred_element_type=jnp.float32)


def right_dft(x, matrix):
    return jnp.dot(split3(x, 1), matrix, preferred_element_type=jnp.float32)


def forward_dft(real, imag, left, right_t, twr, twc):
    t_r, t_i = twr
    c_r, c_i = twc
    a_r, b_r, a_i, b_i = real[:HALF], real[HALF:], imag[:HALF], imag[HALF:]
    d_r, d_i = a_r - b_r, a_i - b_i
    even = left_dft(left, jnp.concatenate([a_r + b_r, a_i + b_i], axis=0))
    odd = left_dft(left, jnp.concatenate([d_r * t_r - d_i * t_i, d_r * t_i + d_i * t_r], axis=0))
    real = jnp.concatenate([even[:HALF], odd[:HALF]], axis=0)
    imag = jnp.concatenate([even[HALF:], odd[HALF:]], axis=0)
    a_r, b_r, a_i, b_i = real[:, :HALF], real[:, HALF:], imag[:, :HALF], imag[:, HALF:]
    d_r, d_i = a_r - b_r, a_i - b_i
    even = right_dft(jnp.concatenate([a_r + b_r, a_i + b_i], axis=1), right_t)
    odd = right_dft(jnp.concatenate([d_r * c_r - d_i * c_i, d_r * c_i + d_i * c_r], axis=1), right_t)
    real = jnp.concatenate([even[:, :HALF], odd[:, :HALF]], axis=1)
    imag = jnp.concatenate([even[:, HALF:], odd[:, HALF:]], axis=1)
    return real, imag


def inverse_dft(real, imag, left_t, right, twr, twc):
    t_r, t_i = twr
    c_r, c_i = twc
    even = right_dft(jnp.concatenate([real[:, :HALF], imag[:, :HALF]], axis=1), right)
    odd = right_dft(jnp.concatenate([real[:, HALF:], imag[:, HALF:]], axis=1), right)
    o_r, o_i = odd[:, :HALF], odd[:, HALF:]
    o_r, o_i = o_r * c_r + o_i * c_i, o_i * c_r - o_r * c_i
    e_r, e_i = even[:, :HALF], even[:, HALF:]
    real = jnp.concatenate([e_r + o_r, e_r - o_r], axis=1)
    imag = jnp.concatenate([e_i + o_i, e_i - o_i], axis=1)
    even = left_dft(left_t, jnp.concatenate([real[:HALF], imag[:HALF]], axis=0))
    odd = left_dft(left_t, jnp.concatenate([real[HALF:], imag[HALF:]], axis=0))
    o_r, o_i = odd[:HALF], odd[HALF:]
    o_r, o_i = o_r * t_r + o_i * t_i, o_i * t_r - o_r * t_i
    e_r, e_i = even[:HALF], even[HALF:]
    real = jnp.concatenate([e_r + o_r, e_r - o_r], axis=0)
    imag = jnp.concatenate([e_i + o_i, e_i - o_i], axis=0)
    return real, imag


def left_of(high, low):
    return jnp.concatenate([high[...], high[...], low[...]], axis=1)


def right_of(high, low):
    return jnp.concatenate([high[...], high[...], low[...]], axis=0)


def window_fit(window, probe, amplitude, tables, far, window_ref, gradient, add_probe, probe_copy, amp_copy):
    high, low, high_t, low_t, rows, cols = tables
    window_ref[0] = window[0]
    window_ref[1] = window[1]

    def twiddles():
        twr = tuple(jnp.concatenate([rows[k], rows[k]], axis=1) for k in range(2))
        twc = tuple(cols[k][:1] for k in range(2))
        return twr, twc

    def outward(m, carry):
        probe_copy(m).wait()
        twr, twc = twiddles()
        w_r, w_i = window_ref[0], window_ref[1]
        p_r, p_i = probe[m, 0], probe[m, 1]
        f_r, f_i = forward_dft(p_r * w_r - p_i * w_i, p_r * w_i + p_i * w_r,
                               left_of(high, low), right_of(high_t, low_t), twr, twc)
        far[m, 0] = f_r
        far[m, 1] = f_i
        return carry

    lax.fori_loop(0, 2, outward, 0)
    intensity = far[0, 0] * far[0, 0] + far[0, 1] * far[0, 1]
    intensity = intensity + (far[1, 0] * far[1, 0] + far[1, 1] * far[1, 1])
    amp_copy.wait()
    factor = amplitude[...] / jnp.sqrt(jnp.maximum(intensity, 0.1)) - 1.0
    for m in range(2):
        far[m, 0] = far[m, 0] * factor
        far[m, 1] = far[m, 1] * factor
    gradient[...] = jnp.zeros(gradient.shape, jnp.float32)

    def inward(m, carry):
        twr, twc = twiddles()
        x_r, x_i = inverse_dft(far[m, 0], far[m, 1], left_of(high_t, low_t), right_of(high, low), twr, twc)
        w_r, w_i = window_ref[0], window_ref[1]
        p_r, p_i = probe[m, 0], probe[m, 1]
        gradient[0] += p_r * x_r + p_i * x_i
        gradient[1] += p_r * x_i - p_i * x_r
        add_probe(m, w_r * x_r + w_i * x_i, w_r * x_i - w_i * x_r)
        return carry

    lax.fori_loop(0, 2, inward, 0)


def before_kernel(probe_hbm, amp_hbm, amp_out, step_out, probe, amp, ordered, sems):
    amp_copy = pltpu.make_async_copy(amp_hbm, amp, sems.at[0])
    probe_copy = pltpu.make_async_copy(probe_hbm, probe, sems.at[1])
    out_copy = lambda b: pltpu.make_async_copy(ordered.at[b], amp_out.at[b], sems.at[2 + b])
    amp_copy.start()
    probe_copy.start()
    out_at = lax.broadcasted_iota(jnp.int32, (WIN, WIN), 0)
    in_at = lax.broadcasted_iota(jnp.int32, (WIN, WIN), 1)
    wanted = jnp.where(out_at < HALF, 2 * out_at, 2 * (out_at - HALF) + 1)
    pick = jnp.where(in_at == wanted, 1.0, 0.0).astype(jnp.bfloat16)
    amp_copy.wait()
    for b in range(BATCHES):
        rows = jnp.dot(pick, amp[b], preferred_element_type=jnp.float32).astype(jnp.bfloat16)
        ordered[b] = lax.dot_general(rows, pick, (((1,), (1,)), ((), ())), preferred_element_type=jnp.float32)
        out_copy(b).start()
    probe_copy.wait()
    total = jnp.zeros((8, HALF), jnp.float32)
    for m in range(2):
        for k in range(2):
            square = probe[m, k] * probe[m, k]
            square = jnp.sum(square.reshape(WIN // 8, 8, WIN), axis=0)
            total = total + square[:, :HALF] + square[:, HALF:]
    power = jnp.sum(total) / (WIN * WIN)
    step_out[...] = jnp.full((8, HALF), 1.0, jnp.float32) / (power + 1e-06)
    for b in range(BATCHES):
        out_copy(b).wait()


TILE_R = 384
LAST = TILE_R - WIN
WIDE = WIN + HALO


def first_kernel(pos, obj, halo, probe_hbm, amp_hbm, step, high, low, high_t, low_t, rows, cols,
                 new_obj, spill_top, spill_low, edge_top, edge_low, middle, sum_hbm,
                 far, win, grad, probe, amp, probe_sum, sems):
    row, col = pos[0, 0], pos[0, 1]
    probe_copy = lambda m: pltpu.make_async_copy(probe_hbm.at[m], probe.at[m], sems.at[m])
    sum_copy = lambda m: pltpu.make_async_copy(probe_sum.at[m], sum_hbm.at[m], sems.at[2 + m])
    amp_copy = pltpu.make_async_copy(amp_hbm.at[0], amp, sems.at[4])
    probe_copy(0).start()
    probe_copy(1).start()
    amp_copy.start()

    def cut(k):
        wide = jnp.concatenate([obj[k], halo[k]], axis=1)
        wide = pltpu.roll(wide, WIDE - col, 1)[:, :WIN]
        return pltpu.roll(wide, lax.rem(TILE_R - row, TILE_R), 0)[:WIN]

    def add_probe(m, real, imag):
        probe_sum[m, 0] = real
        probe_sum[m, 1] = imag
        sum_copy(m).start()

    window_fit((cut(0), cut(1)), probe, amp, (high, low, high_t, low_t, rows, cols), far, win, grad, add_probe,
               probe_copy, amp_copy)
    scale = step[:1, :1]
    for k in range(2):
        g = jnp.concatenate([grad[k] * scale, jnp.zeros((TILE_R - WIN, WIN), jnp.float32)], axis=0)
        g = pltpu.roll(g, row, 0)
        g = jnp.concatenate([g, jnp.zeros((TILE_R, HALO), jnp.float32)], axis=1)
        g = pltpu.roll(g, col, 1)
        updated = obj[k] + g[:, :WIN]
        new_obj[k] = updated
        edge_top[k] = updated[:LAST, :HALO]
        edge_low[k] = updated[LAST:, :HALO]
        middle[k] = updated[:HALO, HALO:]
        spill_top[k] = g[:LAST, WIN:]
        spill_low[k] = g[LAST:, WIN:]
    for k in range(2):
        sum_copy(k).wait()


def lanes():
    return lax.broadcasted_iota(jnp.int32, (HALO, HALO), 1)


def upward_kernel(above, info, edge, from_left, from_right, spill, upward):
    keep = info[0].astype(jnp.float32)
    for k in range(2):
        own = edge[k] + from_left[k]
        upward[k] = jnp.where(lanes() >= above[1, 1], own, from_right[k] + spill[k] * keep)


def merge_kernel(info, obj, left_top, left_low, right_low, spill_low, whole_hbm, source, whole, sems):
    keep = info[0].astype(jnp.float32)
    whole_copy = lambda k: pltpu.make_async_copy(whole.at[k], whole_hbm.at[k], sems.at[k])
    for k in range(2):
        low = obj[k, LAST:, :HALO] + left_low[k]
        whole[k, :LAST, :HALO] = obj[k, :LAST, :HALO] + left_top[k]
        whole[k, LAST:, :HALO] = low
        whole[k, :, HALO:] = obj[k, :, HALO:]
        whole_copy(k).start()
        source[k, :, :HALO] = low
        source[k, :, HALO:WIN] = obj[k, LAST:, HALO:]
        source[k, :, WIN:] = right_low[k] + spill_low[k] * keep
    for k in range(2):
        whole_copy(k).wait()


def second_kernel(pos, info, source, below_mid, below_rest, probe_hbm, amp_hbm, step, before_hbm,
                  high, low, high_t, low_t, rows, cols,
                  own_grad, packed, middle, keep_sum, send_sum, far, win, grad, probe, amp, before, sems):
    row, col, core = pos[1, 0] - LAST, pos[1, 1], info[1]
    probe_copy = lambda m: pltpu.make_async_copy(probe_hbm.at[m], probe.at[m], sems.at[m])
    before_copy = lambda m: pltpu.make_async_copy(before_hbm.at[m], before.at[m], sems.at[2 + m])
    amp_copy = pltpu.make_async_copy(amp_hbm.at[1], amp, sems.at[4])
    probe_copy(0).start()
    probe_copy(1).start()
    amp_copy.start()
    before_copy(0).start()
    before_copy(1).start()

    def cut(k):
        lower = jnp.concatenate([below_rest[k], below_mid[k], below_rest[k]], axis=1)
        tall = pltpu.roll(jnp.concatenate([source[k], lower], axis=0), WIDE - col, 1)[:, :WIN]
        return pltpu.roll(tall, lax.rem(TILE_R - row, TILE_R), 0)[:WIN]

    def add_probe(m, real, imag):
        before_copy(m).wait()

        @pl.when(m == core)
        def _():
            keep_sum[0] = before[m, 0] + real
            keep_sum[1] = before[m, 1] + imag

        @pl.when(m != core)
        def _():
            send_sum[0] = before[m, 0] + real
            send_sum[1] = before[m, 1] + imag

    window_fit((cut(0), cut(1)), probe, amp, (high, low, high_t, low_t, rows, cols), far, win, grad, add_probe,
               probe_copy, amp_copy)
    scale = step[:1, :1]
    for k in range(2):
        g = jnp.concatenate([grad[k] * scale, jnp.zeros((TILE_R - WIN, WIN), jnp.float32)], axis=0)
        g = pltpu.roll(g, row, 0)
        g = jnp.concatenate([g, jnp.zeros((TILE_R, HALO), jnp.float32)], axis=1)
        g = pltpu.roll(g, col, 1)
        own_grad[k] = g[:WIN]
        packed[k] = g[WIN:, :HALO] + g[WIN:, WIN:]
        middle[k] = g[WIN:, HALO:WIN]


def spill_kernel(above, own_grad, from_above, new_spill):
    for k in range(2):
        new_spill[k, :HALO] = jnp.where(lanes() < above[1, 1], from_above[k], 0.0)
        new_spill[k, HALO:] = own_grad[k, :, WIN:]


def object_kernel(above, whole, own_grad, from_above, mid_above, from_left, out):
    for k in range(2):
        fell = jnp.where(lanes() >= above[1, 1], from_above[k], 0.0)
        out[k, :LAST, :HALO] = whole[k, :LAST, :HALO] + fell + from_left[k, :LAST]
        out[k, :LAST, HALO:] = whole[k, :LAST, HALO:] + mid_above[k]
        out[k, LAST:, :HALO] = whole[k, LAST:, :HALO] + own_grad[k, :, :HALO] + from_left[k, LAST:]
        out[k, LAST:, HALO:] = whole[k, LAST:, HALO:] + own_grad[k, :, HALO:WIN]


def probe_kernel(info, probe, own, other, out):
    core = info[1]
    out[core] = probe[core] + own[...]
    out[1 - core] = probe[1 - core] + other[...]


HBM = object()
AUTO = object()


def call(kernel, outs, scratch, scalars, arrays, copies=0, in_place=None):
    smem = pl.BlockSpec(memory_space=pltpu.SMEM)
    specs = {None: pl.BlockSpec(memory_space=pltpu.VMEM), HBM: pl.BlockSpec(memory_space=pltpu.HBM)}
    specs[AUTO] = specs[None]
    arrays = [x if isinstance(x, tuple) else (x, None) for x in arrays]
    outs = [(o[0], o[1]) if isinstance(o[0], tuple) else (o, None) for o in outs]
    spaces = {None: pltpu.VMEM, HBM: pltpu.HBM, AUTO: pltpu.HBM}
    shapes = [
        jax.ShapeDtypeStruct(shape, jnp.float32) if INTERPRET or where is AUTO else spaces[where](shape, jnp.float32)
        for shape, where in outs
    ]
    operands = [
        x if INTERPRET or where is AUTO else pltpu.with_memory_space_constraint(x, spaces[where]) for x, where in arrays
    ]
    return pl.pallas_call(
        kernel,
        out_shape=shapes,
        in_specs=[smem] * len(scalars) + [specs[where] for _, where in arrays],
        out_specs=[specs[where] for _, where in outs],
        scratch_shapes=[pltpu.VMEM(s, jnp.float32) if isinstance(s, tuple) else s for s in scratch]
        + ([pltpu.SemaphoreType.DMA((copies,))] if copies else []),
        compiler_params=pltpu.CompilerParams(vmem_limit_bytes=24 * 1024 * 1024),
        input_output_aliases={} if in_place is None else {in_place: 0},
        interpret=INTERPRET,
    )(*scalars, *operands)


def passed_along(block, axis, distance):
    devices = range(lax.axis_size(axis))
    route = [(i - distance, i) for i in devices if i - distance in devices]
    return lax.ppermute(block, axis, route)


def exchanged(parts, axes):
    return lax.all_to_all(parts, axes, 0, 0, tiled=False)


def swapped(block):
    return lax.ppermute(block, CORE, [(0, 1), (1, 0)])


def summed_everywhere(keep, send, divisor):
    plane = lax.axis_size(PLANE)
    mode = keep + swapped(send)
    parts = exchanged(mode.reshape(plane, -1, WIN), PLANE)
    share = jnp.sum(parts, axis=0)
    for axis in ("col_0", "row_1"):
        parts = exchanged(jnp.broadcast_to(share, (lax.axis_size(axis), *share.shape)), axis)
        share = jnp.sum(parts, axis=0)
    share = share / divisor
    mode = exchanged(jnp.broadcast_to(share, (plane, *share.shape)), PLANE).reshape(2, WIN, WIN)
    return mode, swapped(mode)


def step_once(object_field, probe_modes, scan_positions, amplitudes):
    tables = [jnp.asarray(t) for t in dft_constants()]
    positions = scan_positions[0, 0]
    device_count = lax.axis_size(ROW) * lax.axis_size(COL)
    divisor = math.sqrt(device_count * BATCHES)
    has_right = (lax.axis_index(COL) < lax.axis_size(COL) - 1).astype(jnp.int32)
    tile, side, probe_shape = (2, TILE_R, WIN), (2, TILE_R, HALO), (2, 2, WIN, WIN)
    block, window = (2, HALO, HALO), (2, WIN, WIN)
    fit_scratch = [probe_shape, window, window, probe_shape, (WIN, WIN)]

    halo = passed_along(object_field[:, :, :HALO], COL, -1)
    above = passed_along(positions, ROW, 1)
    info = jnp.stack([has_right, lax.axis_index(CORE)])
    amp, step = call(
        before_kernel, [((BATCHES, WIN, WIN), HBM), (8, HALF)],
        [probe_shape, pltpu.VMEM((BATCHES, WIN, WIN), jnp.bfloat16), (BATCHES, WIN, WIN)],
        [], [(probe_modes, HBM), (amplitudes[0, 0], HBM)], copies=4)
    low = (2, WIN, HALO)
    obj, spill_top, spill_low, edge_top, edge_low, middle, probe_sum = call(
        first_kernel, [tile, block, low, block, low, block, (probe_shape, HBM)], fit_scratch + [probe_shape],
        [positions], [object_field, halo, (probe_modes, HBM), (amp, HBM), step, *tables], copies=5, in_place=1)
    below_mid = passed_along(middle, ROW, -1)
    right_top = passed_along(edge_top, COL, -1)
    left_top = passed_along(spill_top, COL, 1)
    (upward,) = call(upward_kernel, [block], [], [above, info], [edge_top, left_top, right_top, spill_top])
    below_rest = passed_along(upward, ROW, -1)
    right_low = passed_along(edge_low, COL, -1)
    left_low = passed_along(spill_low, COL, 1)
    whole, source = call(
        merge_kernel, [(tile, HBM), (2, WIN, WIDE)], [tile], [info], [obj, left_top, left_low, right_low, spill_low], copies=2)
    grad, packed, middle, keep, send = call(
        second_kernel, [(2, WIN, WIDE), block, block, window, window],
        fit_scratch + [probe_shape], [positions, info],
        [source, below_mid, below_rest, (probe_modes, HBM), (amp, HBM), step, (probe_sum, HBM), *tables], copies=5, in_place=2)
    own, other = summed_everywhere(keep, send, divisor)
    from_above = passed_along(packed, ROW, 1)
    (spill,) = call(spill_kernel, [side], [], [above], [grad, from_above])
    from_left = passed_along(spill, COL, 1)
    mid_above = passed_along(middle, ROW, 1)
    (object_out,) = call(
        object_kernel, [(tile, AUTO)], [], [above], [(whole, AUTO), (grad, AUTO), from_above, mid_above, from_left])
    (probe_out,) = call(probe_kernel, [(probe_shape, AUTO)], [], [info], [(probe_modes, AUTO), own, other])
    return (object_out, probe_out)


def solution(mesh):
    torus = Mesh(mesh.devices.reshape(4, 4, 4, 4, 2), ("row_0", "row_1", "col_0", "col_1", "col_2"))
    in_specs = (P(None, ROW, COL), P(), P(ROW, COL, None, None), P(ROW, COL, None, None, None))
    out_specs = (P(None, ROW, COL), P())
    return jax.shard_map(step_once, mesh=torus, in_specs=in_specs, out_specs=out_specs, check_vma=False)
```

```python
import math

import jax
import jax.numpy as jnp
import numpy as np
from jax import lax
from jax.experimental import pallas as pl
from jax.experimental.pallas import tpu as pltpu
from jax.sharding import Mesh
from jax.sharding import PartitionSpec as P


HALO = 128
BATCHES = 2
WIN = 256
HALF = 128
INTERPRET = False
ROW = ("row_0", "row_1")
COL = ("col_0", "col_1", "col_2")
PLANE = ("row_0", "col_1")
CORE = "col_2"


def halves(x):
    high = x.astype(jnp.bfloat16)
    low = (x - high.astype(np.float64)).astype(jnp.bfloat16)
    return high, low


def dft_constants():
    index = np.arange(HALF)
    angle = 2.0 * np.pi * (np.outer(index, index) % HALF) / HALF
    cosine = np.cos(angle) / 16.0
    sine = -np.sin(angle) / 16.0
    forward = np.block([[cosine, -sine], [sine, cosine]])
    high, low = halves(forward)
    turn = 2.0 * np.pi * index / WIN
    twiddle = np.stack([np.cos(turn), -np.sin(turn)]).astype(np.float32)
    rows = np.ascontiguousarray(np.broadcast_to(twiddle[:, :, None], (2, HALF, HALF)))
    cols = np.ascontiguousarray(np.broadcast_to(twiddle[:, None, :], (2, 8, HALF)))
    return high, low, np.ascontiguousarray(high.T), np.ascontiguousarray(low.T), rows, cols


def split3(x, axis):
    high = x.astype(jnp.bfloat16)
    low = (x - high.astype(jnp.float32)).astype(jnp.bfloat16)
    return jnp.concatenate([high, low, high], axis=axis)


def left_dft(matrix, x):
    return jnp.dot(matrix, split3(x, 0), preferred_element_type=jnp.float32)


def right_dft(x, matrix):
    return jnp.dot(split3(x, 1), matrix, preferred_element_type=jnp.float32)


def forward_dft(real, imag, left, right_t, twr, twc):
    t_r, t_i = twr
    c_r, c_i = twc
    a_r, b_r, a_i, b_i = real[:HALF], real[HALF:], imag[:HALF], imag[HALF:]
    d_r, d_i = a_r - b_r, a_i - b_i
    even = left_dft(left, jnp.concatenate([a_r + b_r, a_i + b_i], axis=0))
    odd = left_dft(left, jnp.concatenate([d_r * t_r - d_i * t_i, d_r * t_i + d_i * t_r], axis=0))
    real = jnp.concatenate([even[:HALF], odd[:HALF]], axis=0)
    imag = jnp.concatenate([even[HALF:], odd[HALF:]], axis=0)
    a_r, b_r, a_i, b_i = real[:, :HALF], real[:, HALF:], imag[:, :HALF], imag[:, HALF:]
    d_r, d_i = a_r - b_r, a_i - b_i
    even = right_dft(jnp.concatenate([a_r + b_r, a_i + b_i], axis=1), right_t)
    odd = right_dft(jnp.concatenate([d_r * c_r - d_i * c_i, d_r * c_i + d_i * c_r], axis=1), right_t)
    real = jnp.concatenate([even[:, :HALF], odd[:, :HALF]], axis=1)
    imag = jnp.concatenate([even[:, HALF:], odd[:, HALF:]], axis=1)
    return real, imag


def inverse_dft(real, imag, left_t, right, twr, twc):
    t_r, t_i = twr
    c_r, c_i = twc
    even = right_dft(jnp.concatenate([real[:, :HALF], imag[:, :HALF]], axis=1), right)
    odd = right_dft(jnp.concatenate([real[:, HALF:], imag[:, HALF:]], axis=1), right)
    o_r, o_i = odd[:, :HALF], odd[:, HALF:]
    o_r, o_i = o_r * c_r + o_i * c_i, o_i * c_r - o_r * c_i
    e_r, e_i = even[:, :HALF], even[:, HALF:]
    real = jnp.concatenate([e_r + o_r, e_r - o_r], axis=1)
    imag = jnp.concatenate([e_i + o_i, e_i - o_i], axis=1)
    even = left_dft(left_t, jnp.concatenate([real[:HALF], imag[:HALF]], axis=0))
    odd = left_dft(left_t, jnp.concatenate([real[HALF:], imag[HALF:]], axis=0))
    o_r, o_i = odd[:HALF], odd[HALF:]
    o_r, o_i = o_r * t_r + o_i * t_i, o_i * t_r - o_r * t_i
    e_r, e_i = even[:HALF], even[HALF:]
    real = jnp.concatenate([e_r + o_r, e_r - o_r], axis=0)
    imag = jnp.concatenate([e_i + o_i, e_i - o_i], axis=0)
    return real, imag


def left_of(high, low):
    return jnp.concatenate([high[...], high[...], low[...]], axis=1)


def right_of(high, low):
    return jnp.concatenate([high[...], high[...], low[...]], axis=0)


def window_fit(window, probe, amplitude, tables, far, window_ref, gradient, add_probe, probe_copy, amp_copy):
    high, low, high_t, low_t, rows, cols = tables
    window_ref[0] = window[0]
    window_ref[1] = window[1]

    def twiddles():
        twr = tuple(jnp.concatenate([rows[k], rows[k]], axis=1) for k in range(2))
        twc = tuple(cols[k][:1] for k in range(2))
        return twr, twc

    def outward(m, carry):
        probe_copy(m).wait()
        twr, twc = twiddles()
        w_r, w_i = window_ref[0], window_ref[1]
        p_r, p_i = probe[m, 0], probe[m, 1]
        f_r, f_i = forward_dft(p_r * w_r - p_i * w_i, p_r * w_i + p_i * w_r,
                               left_of(high, low), right_of(high_t, low_t), twr, twc)
        far[m, 0] = f_r
        far[m, 1] = f_i
        return carry

    lax.fori_loop(0, 2, outward, 0)
    intensity = far[0, 0] * far[0, 0] + far[0, 1] * far[0, 1]
    intensity = intensity + (far[1, 0] * far[1, 0] + far[1, 1] * far[1, 1])
    amp_copy.wait()
    factor = amplitude[...] / jnp.sqrt(jnp.maximum(intensity, 0.1)) - 1.0
    for m in range(2):
        far[m, 0] = far[m, 0] * factor
        far[m, 1] = far[m, 1] * factor
    gradient[...] = jnp.zeros(gradient.shape, jnp.float32)

    def inward(m, carry):
        twr, twc = twiddles()
        x_r, x_i = inverse_dft(far[m, 0], far[m, 1], left_of(high_t, low_t), right_of(high, low), twr, twc)
        w_r, w_i = window_ref[0], window_ref[1]
        p_r, p_i = probe[m, 0], probe[m, 1]
        gradient[0] += p_r * x_r + p_i * x_i
        gradient[1] += p_r * x_i - p_i * x_r
        add_probe(m, w_r * x_r + w_i * x_i, w_r * x_i - w_i * x_r)
        return carry

    lax.fori_loop(0, 2, inward, 0)


def before_kernel(probe_hbm, amp_hbm, amp_out, step_out, probe, amp, ordered, sems):
    amp_copy = pltpu.make_async_copy(amp_hbm, amp, sems.at[0])
    probe_copy = pltpu.make_async_copy(probe_hbm, probe, sems.at[1])
    out_copy = lambda b: pltpu.make_async_copy(ordered.at[b], amp_out.at[b], sems.at[2 + b])
    amp_copy.start()
    probe_copy.start()
    out_at = lax.broadcasted_iota(jnp.int32, (WIN, WIN), 0)
    in_at = lax.broadcasted_iota(jnp.int32, (WIN, WIN), 1)
    wanted = jnp.where(out_at < HALF, 2 * out_at, 2 * (out_at - HALF) + 1)
    pick = jnp.where(in_at == wanted, 1.0, 0.0).astype(jnp.bfloat16)
    amp_copy.wait()
    for b in range(BATCHES):
        rows = jnp.dot(pick, amp[b], preferred_element_type=jnp.float32).astype(jnp.bfloat16)
        ordered[b] = lax.dot_general(rows, pick, (((1,), (1,)), ((), ())), preferred_element_type=jnp.float32)
        out_copy(b).start()
    probe_copy.wait()
    total = jnp.zeros((8, HALF), jnp.float32)
    for m in range(2):
        for k in range(2):
            square = probe[m, k] * probe[m, k]
            square = jnp.sum(square.reshape(WIN // 8, 8, WIN), axis=0)
            total = total + square[:, :HALF] + square[:, HALF:]
    power = jnp.sum(total) / (WIN * WIN)
    step_out[...] = jnp.full((8, HALF), 1.0, jnp.float32) / (power + 1e-06)
    for b in range(BATCHES):
        out_copy(b).wait()


TILE_R = 384
LAST = TILE_R - WIN
WIDE = WIN + HALO


def first_kernel(pos, obj, halo, probe_hbm, amp_hbm, step, high, low, high_t, low_t, rows, cols,
                 new_obj, spill, edge, middle, sum_hbm,
                 far, win, grad, probe, amp, probe_sum, sems):
    row, col = pos[0, 0], pos[0, 1]
    probe_copy = lambda m: pltpu.make_async_copy(probe_hbm.at[m], probe.at[m], sems.at[m])
    sum_copy = lambda m: pltpu.make_async_copy(probe_sum.at[m], sum_hbm.at[m], sems.at[2 + m])
    amp_copy = pltpu.make_async_copy(amp_hbm.at[0], amp, sems.at[4])
    probe_copy(0).start()
    probe_copy(1).start()
    amp_copy.start()

    def cut(k):
        wide = jnp.concatenate([obj[k], halo[k]], axis=1)
        wide = pltpu.roll(wide, WIDE - col, 1)[:, :WIN]
        return pltpu.roll(wide, lax.rem(TILE_R - row, TILE_R), 0)[:WIN]

    def add_probe(m, real, imag):
        probe_sum[m, 0] = real
        probe_sum[m, 1] = imag
        sum_copy(m).start()

    window_fit((cut(0), cut(1)), probe, amp, (high, low, high_t, low_t, rows, cols), far, win, grad, add_probe,
               probe_copy, amp_copy)
    scale = step[:1, :1]
    for k in range(2):
        g = jnp.concatenate([grad[k] * scale, jnp.zeros((TILE_R - WIN, WIN), jnp.float32)], axis=0)
        g = pltpu.roll(g, row, 0)
        g = jnp.concatenate([g, jnp.zeros((TILE_R, HALO), jnp.float32)], axis=1)
        g = pltpu.roll(g, col, 1)
        updated = obj[k] + g[:, :WIN]
        new_obj[k] = updated
        edge[k] = updated[:, :HALO]
        middle[k] = updated[:HALO, HALO:]
        spill[k] = g[:, WIN:]
    for k in range(2):
        sum_copy(k).wait()


def lanes():
    return lax.broadcasted_iota(jnp.int32, (HALO, HALO), 1)


def upward_kernel(above, info, edge, from_left, from_right, spill, upward):
    keep = info[0].astype(jnp.float32)
    for k in range(2):
        own = edge[k, :HALO] + from_left[k, :HALO]
        upward[k] = jnp.where(lanes() >= above[1, 1], own, from_right[k, :HALO] + spill[k, :HALO] * keep)


def merge_kernel(info, obj, from_left, from_right, spill, whole_hbm, source, whole, sems):
    keep = info[0].astype(jnp.float32)
    whole_copy = lambda k: pltpu.make_async_copy(whole.at[k], whole_hbm.at[k], sems.at[k])
    for k in range(2):
        left = obj[k, :, :HALO] + from_left[k]
        whole[k, :, :HALO] = left
        whole[k, :, HALO:] = obj[k, :, HALO:]
        whole_copy(k).start()
        source[k, :, :HALO] = left[LAST:]
        source[k, :, HALO:WIN] = obj[k, LAST:, HALO:]
        source[k, :, WIN:] = from_right[k, LAST:] + spill[k, LAST:] * keep
    for k in range(2):
        whole_copy(k).wait()


def second_kernel(pos, info, source, below_mid, below_rest, probe_hbm, amp_hbm, step, before_hbm,
                  high, low, high_t, low_t, rows, cols,
                  own_grad, downward, keep_sum, send_sum, far, win, grad, probe, amp, before, sems):
    row, col, core = pos[1, 0] - LAST, pos[1, 1], info[1]
    probe_copy = lambda m: pltpu.make_async_copy(probe_hbm.at[m], probe.at[m], sems.at[m])
    before_copy = lambda m: pltpu.make_async_copy(before_hbm.at[m], before.at[m], sems.at[2 + m])
    amp_copy = pltpu.make_async_copy(amp_hbm.at[1], amp, sems.at[4])
    probe_copy(0).start()
    probe_copy(1).start()
    amp_copy.start()
    before_copy(0).start()
    before_copy(1).start()

    def cut(k):
        lower = jnp.concatenate([below_rest[k], below_mid[k], below_rest[k]], axis=1)
        tall = pltpu.roll(jnp.concatenate([source[k], lower], axis=0), WIDE - col, 1)[:, :WIN]
        return pltpu.roll(tall, lax.rem(TILE_R - row, TILE_R), 0)[:WIN]

    def add_probe(m, real, imag):
        before_copy(m).wait()

        @pl.when(m == core)
        def _():
            keep_sum[0] = before[m, 0] + real
            keep_sum[1] = before[m, 1] + imag

        @pl.when(m != core)
        def _():
            send_sum[0] = before[m, 0] + real
            send_sum[1] = before[m, 1] + imag

    window_fit((cut(0), cut(1)), probe, amp, (high, low, high_t, low_t, rows, cols), far, win, grad, add_probe,
               probe_copy, amp_copy)
    scale = step[:1, :1]
    for k in range(2):
        g = jnp.concatenate([grad[k] * scale, jnp.zeros((TILE_R - WIN, WIN), jnp.float32)], axis=0)
        g = pltpu.roll(g, row, 0)
        g = jnp.concatenate([g, jnp.zeros((TILE_R, HALO), jnp.float32)], axis=1)
        g = pltpu.roll(g, col, 1)
        own_grad[k] = g[:WIN]
        downward[k, :, :HALO] = g[WIN:, :HALO] + g[WIN:, WIN:]
        downward[k, :, HALO:] = g[WIN:, HALO:WIN]


def spill_kernel(above, own_grad, from_above, new_spill):
    for k in range(2):
        new_spill[k, :HALO] = jnp.where(lanes() < above[1, 1], from_above[k, :, :HALO], 0.0)
        new_spill[k, HALO:] = own_grad[k, :, WIN:]


def object_kernel(above, whole, own_grad, from_above, from_left, out):
    for k in range(2):
        fell = jnp.where(lanes() >= above[1, 1], from_above[k, :, :HALO], 0.0)
        out[k, :LAST, :HALO] = whole[k, :LAST, :HALO] + fell + from_left[k, :LAST]
        out[k, :LAST, HALO:] = whole[k, :LAST, HALO:] + from_above[k, :, HALO:]
        out[k, LAST:, :HALO] = whole[k, LAST:, :HALO] + own_grad[k, :, :HALO] + from_left[k, LAST:]
        out[k, LAST:, HALO:] = whole[k, LAST:, HALO:] + own_grad[k, :, HALO:WIN]


def probe_kernel(info, probe, own, other, out):
    core = info[1]
    out[core] = probe[core] + own[...]
    out[1 - core] = probe[1 - core] + other[...]


HBM = object()
AUTO = object()


def call(kernel, outs, scratch, scalars, arrays, copies=0, in_place=None):
    smem = pl.BlockSpec(memory_space=pltpu.SMEM)
    specs = {None: pl.BlockSpec(memory_space=pltpu.VMEM), HBM: pl.BlockSpec(memory_space=pltpu.HBM)}
    specs[AUTO] = specs[None]
    arrays = [x if isinstance(x, tuple) else (x, None) for x in arrays]
    outs = [(o[0], o[1]) if isinstance(o[0], tuple) else (o, None) for o in outs]
    spaces = {None: pltpu.VMEM, HBM: pltpu.HBM, AUTO: pltpu.HBM}
    shapes = [
        jax.ShapeDtypeStruct(shape, jnp.float32) if INTERPRET or where is AUTO else spaces[where](shape, jnp.float32)
        for shape, where in outs
    ]
    operands = [
        x if INTERPRET or where is AUTO else pltpu.with_memory_space_constraint(x, spaces[where]) for x, where in arrays
    ]
    return pl.pallas_call(
        kernel,
        out_shape=shapes,
        in_specs=[smem] * len(scalars) + [specs[where] for _, where in arrays],
        out_specs=[specs[where] for _, where in outs],
        scratch_shapes=[pltpu.VMEM(s, jnp.float32) if isinstance(s, tuple) else s for s in scratch]
        + ([pltpu.SemaphoreType.DMA((copies,))] if copies else []),
        compiler_params=pltpu.CompilerParams(vmem_limit_bytes=24 * 1024 * 1024),
        input_output_aliases={} if in_place is None else {in_place: 0},
        interpret=INTERPRET,
    )(*scalars, *operands)


def passed_along(block, axis, distance):
    devices = range(lax.axis_size(axis))
    route = [(i - distance, i) for i in devices if i - distance in devices]
    return lax.ppermute(block, axis, route)


def exchanged(parts, axes):
    return lax.all_to_all(parts, axes, 0, 0, tiled=False)


def swapped(block):
    return lax.ppermute(block, CORE, [(0, 1), (1, 0)])


def summed_everywhere(keep, send, divisor):
    plane = lax.axis_size(PLANE)
    mode = keep + swapped(send)
    parts = exchanged(mode.reshape(plane, -1, WIN), PLANE)
    share = jnp.sum(parts, axis=0)
    for axis in ("col_0", "row_1"):
        parts = exchanged(jnp.broadcast_to(share, (lax.axis_size(axis), *share.shape)), axis)
        share = jnp.sum(parts, axis=0)
    share = share / divisor
    mode = exchanged(jnp.broadcast_to(share, (plane, *share.shape)), PLANE).reshape(2, WIN, WIN)
    return mode, swapped(mode)


def step_once(object_field, probe_modes, scan_positions, amplitudes):
    tables = [jnp.asarray(t) for t in dft_constants()]
    positions = scan_positions[0, 0]
    device_count = lax.axis_size(ROW) * lax.axis_size(COL)
    divisor = math.sqrt(device_count * BATCHES)
    has_right = (lax.axis_index(COL) < lax.axis_size(COL) - 1).astype(jnp.int32)
    tile, side, probe_shape = (2, TILE_R, WIN), (2, TILE_R, HALO), (2, 2, WIN, WIN)
    block, window = (2, HALO, HALO), (2, WIN, WIN)
    fit_scratch = [probe_shape, window, window, probe_shape, (WIN, WIN)]

    halo = passed_along(object_field[:, :, :HALO], COL, -1)
    above = passed_along(positions, ROW, 1)
    info = jnp.stack([has_right, lax.axis_index(CORE)])
    amp, step = call(
        before_kernel, [((BATCHES, WIN, WIN), HBM), (8, HALF)],
        [probe_shape, pltpu.VMEM((BATCHES, WIN, WIN), jnp.bfloat16), (BATCHES, WIN, WIN)],
        [], [(probe_modes, HBM), (amplitudes[0, 0], HBM)], copies=4)
    obj, spill, edge, middle, probe_sum = call(
        first_kernel, [tile, side, side, block, (probe_shape, HBM)], fit_scratch + [probe_shape],
        [positions], [object_field, halo, (probe_modes, HBM), (amp, HBM), step, *tables], copies=5, in_place=1)
    from_right = passed_along(edge, COL, -1)
    from_left = passed_along(spill, COL, 1)
    below_mid = passed_along(middle, ROW, -1)
    (upward,) = call(upward_kernel, [block], [], [above, info], [edge, from_left, from_right, spill])
    below_rest = passed_along(upward, ROW, -1)
    whole, source = call(
        merge_kernel, [(tile, HBM), (2, WIN, WIDE)], [tile], [info], [obj, from_left, from_right, spill], copies=2)
    grad, downward, keep, send = call(
        second_kernel, [(2, WIN, WIDE), (2, HALO, WIN), window, window],
        fit_scratch + [probe_shape], [positions, info],
        [source, below_mid, below_rest, (probe_modes, HBM), (amp, HBM), step, (probe_sum, HBM), *tables], copies=5, in_place=2)
    own, other = summed_everywhere(keep, send, divisor)
    from_above = passed_along(downward, ROW, 1)
    (spill,) = call(spill_kernel, [side], [], [above], [grad, from_above])
    from_left = passed_along(spill, COL, 1)
    (object_out,) = call(
        object_kernel, [(tile, AUTO)], [], [above], [(whole, AUTO), (grad, AUTO), from_above, from_left])
    (probe_out,) = call(probe_kernel, [(probe_shape, AUTO)], [], [info], [(probe_modes, AUTO), own, other])
    return (object_out, probe_out)


def solution(mesh):
    torus = Mesh(mesh.devices.reshape(4, 4, 4, 4, 2), ("row_0", "row_1", "col_0", "col_1", "col_2"))
    in_specs = (P(None, ROW, COL), P(), P(ROW, COL, None, None), P(ROW, COL, None, None, None))
    out_specs = (P(None, ROW, COL), P())
    return jax.shard_map(step_once, mesh=torus, in_specs=in_specs, out_specs=out_specs, check_vma=False)
```

```python
import math

import jax
import jax.numpy as jnp
import numpy as np
from jax import lax
from jax.experimental import pallas as pl
from jax.experimental.pallas import tpu as pltpu
from jax.sharding import Mesh
from jax.sharding import PartitionSpec as P


HALO = 128
BATCHES = 2
WIN = 256
HALF = 128
INTERPRET = False
ROW = ("row_0", "row_1")
COL = ("col_0", "col_1", "col_2")
PLANE = ("row_0", "col_1")
CORE = "col_2"


def halves(x):
    high = x.astype(jnp.bfloat16)
    low = (x - high.astype(np.float64)).astype(jnp.bfloat16)
    return high, low


def dft_constants():
    index = np.arange(HALF)
    angle = 2.0 * np.pi * (np.outer(index, index) % HALF) / HALF
    cosine = np.cos(angle) / 16.0
    sine = -np.sin(angle) / 16.0
    forward = np.block([[cosine, -sine], [sine, cosine]])
    high, low = halves(forward)
    turn = 2.0 * np.pi * index / WIN
    twiddle = np.stack([np.cos(turn), -np.sin(turn)]).astype(np.float32)
    rows = np.ascontiguousarray(np.broadcast_to(twiddle[:, :, None], (2, HALF, HALF)))
    cols = np.ascontiguousarray(np.broadcast_to(twiddle[:, None, :], (2, 8, HALF)))
    return high, low, np.ascontiguousarray(high.T), np.ascontiguousarray(low.T), rows, cols


def split3(x, axis):
    high = x.astype(jnp.bfloat16)
    low = (x - high.astype(jnp.float32)).astype(jnp.bfloat16)
    return jnp.concatenate([high, low, high], axis=axis)


def left_dft(matrix, x):
    return jnp.dot(matrix, split3(x, 0), preferred_element_type=jnp.float32)


def right_dft(x, matrix):
    return jnp.dot(split3(x, 1), matrix, preferred_element_type=jnp.float32)


def forward_dft(real, imag, left, right_t, twr, twc):
    t_r, t_i = twr
    c_r, c_i = twc
    a_r, b_r, a_i, b_i = real[:HALF], real[HALF:], imag[:HALF], imag[HALF:]
    d_r, d_i = a_r - b_r, a_i - b_i
    even = left_dft(left, jnp.concatenate([a_r + b_r, a_i + b_i], axis=0))
    odd = left_dft(left, jnp.concatenate([d_r * t_r - d_i * t_i, d_r * t_i + d_i * t_r], axis=0))
    real = jnp.concatenate([even[:HALF], odd[:HALF]], axis=0)
    imag = jnp.concatenate([even[HALF:], odd[HALF:]], axis=0)
    a_r, b_r, a_i, b_i = real[:, :HALF], real[:, HALF:], imag[:, :HALF], imag[:, HALF:]
    d_r, d_i = a_r - b_r, a_i - b_i
    even = right_dft(jnp.concatenate([a_r + b_r, a_i + b_i], axis=1), right_t)
    odd = right_dft(jnp.concatenate([d_r * c_r - d_i * c_i, d_r * c_i + d_i * c_r], axis=1), right_t)
    real = jnp.concatenate([even[:, :HALF], odd[:, :HALF]], axis=1)
    imag = jnp.concatenate([even[:, HALF:], odd[:, HALF:]], axis=1)
    return real, imag


def inverse_dft(real, imag, left_t, right, twr, twc):
    t_r, t_i = twr
    c_r, c_i = twc
    even = right_dft(jnp.concatenate([real[:, :HALF], imag[:, :HALF]], axis=1), right)
    odd = right_dft(jnp.concatenate([real[:, HALF:], imag[:, HALF:]], axis=1), right)
    o_r, o_i = odd[:, :HALF], odd[:, HALF:]
    o_r, o_i = o_r * c_r + o_i * c_i, o_i * c_r - o_r * c_i
    e_r, e_i = even[:, :HALF], even[:, HALF:]
    real = jnp.concatenate([e_r + o_r, e_r - o_r], axis=1)
    imag = jnp.concatenate([e_i + o_i, e_i - o_i], axis=1)
    even = left_dft(left_t, jnp.concatenate([real[:HALF], imag[:HALF]], axis=0))
    odd = left_dft(left_t, jnp.concatenate([real[HALF:], imag[HALF:]], axis=0))
    o_r, o_i = odd[:HALF], odd[HALF:]
    o_r, o_i = o_r * t_r + o_i * t_i, o_i * t_r - o_r * t_i
    e_r, e_i = even[:HALF], even[HALF:]
    real = jnp.concatenate([e_r + o_r, e_r - o_r], axis=0)
    imag = jnp.concatenate([e_i + o_i, e_i - o_i], axis=0)
    return real, imag


def left_of(high, low):
    return jnp.concatenate([high[...], high[...], low[...]], axis=1)


def right_of(high, low):
    return jnp.concatenate([high[...], high[...], low[...]], axis=0)


def window_fit(probe, amplitude, tables, far, window_ref, gradient, add_probe, probe_copy, amp_copy):
    high, low, high_t, low_t, rows, cols = tables

    def twiddles():
        twr = tuple(jnp.concatenate([rows[k], rows[k]], axis=1) for k in range(2))
        twc = tuple(cols[k][:1] for k in range(2))
        return twr, twc

    def outward(m, carry):
        if probe_copy is not None:
            probe_copy(m).wait()
        twr, twc = twiddles()
        w_r, w_i = window_ref[0], window_ref[1]
        p_r, p_i = probe[m, 0], probe[m, 1]
        f_r, f_i = forward_dft(p_r * w_r - p_i * w_i, p_r * w_i + p_i * w_r,
                               left_of(high, low), right_of(high_t, low_t), twr, twc)
        far[m, 0] = f_r
        far[m, 1] = f_i
        return carry

    lax.fori_loop(0, 2, outward, 0)
    intensity = far[0, 0] * far[0, 0] + far[0, 1] * far[0, 1]
    intensity = intensity + (far[1, 0] * far[1, 0] + far[1, 1] * far[1, 1])
    amp_copy.wait()
    factor = amplitude[...] * lax.rsqrt(jnp.maximum(intensity, 0.1)) - 1.0
    for m in range(2):
        far[m, 0] = far[m, 0] * factor
        far[m, 1] = far[m, 1] * factor
    gradient[...] = jnp.zeros(gradient.shape, jnp.float32)

    def inward(m, carry):
        twr, twc = twiddles()
        x_r, x_i = inverse_dft(far[m, 0], far[m, 1], left_of(high_t, low_t), right_of(high, low), twr, twc)
        w_r, w_i = window_ref[0], window_ref[1]
        p_r, p_i = probe[m, 0], probe[m, 1]
        gradient[0] += p_r * x_r + p_i * x_i
        gradient[1] += p_r * x_i - p_i * x_r
        add_probe(m, w_r * x_r + w_i * x_i, w_r * x_i - w_i * x_r)
        return carry

    lax.fori_loop(0, 2, inward, 0)


def before_kernel(probe_hbm, amp_hbm, amp_out, step_out, probe, amp, ordered, sems):
    amp_copy = pltpu.make_async_copy(amp_hbm, amp, sems.at[0])
    probe_copy = pltpu.make_async_copy(probe_hbm, probe, sems.at[1])
    out_copy = lambda b: pltpu.make_async_copy(ordered.at[b], amp_out.at[b], sems.at[2 + b])
    amp_copy.start()
    probe_copy.start()
    out_at = lax.broadcasted_iota(jnp.int32, (WIN, WIN), 0)
    in_at = lax.broadcasted_iota(jnp.int32, (WIN, WIN), 1)
    wanted = jnp.where(out_at < HALF, 2 * out_at, 2 * (out_at - HALF) + 1)
    pick = jnp.where(in_at == wanted, 1.0, 0.0).astype(jnp.bfloat16)
    amp_copy.wait()
    for b in range(BATCHES):
        rows = jnp.dot(pick, amp[b], preferred_element_type=jnp.float32).astype(jnp.bfloat16)
        ordered[b] = lax.dot_general(rows, pick, (((1,), (1,)), ((), ())), preferred_element_type=jnp.float32)
        out_copy(b).start()
    probe_copy.wait()
    total = jnp.zeros((8, HALF), jnp.float32)
    for m in range(2):
        for k in range(2):
            square = probe[m, k] * probe[m, k]
            square = jnp.sum(square.reshape(WIN // 8, 8, WIN), axis=0)
            total = total + square[:, :HALF] + square[:, HALF:]
    power = jnp.sum(total) / (WIN * WIN)
    step_out[...] = jnp.full((8, HALF), 1.0, jnp.float32) / (power + 1e-06)
    for b in range(BATCHES):
        out_copy(b).wait()


TILE_R = 384
LAST = TILE_R - WIN
WIDE = WIN + HALO


def cut_window(tiles, tall, win, row, col):
    base, rest = pl.multiple_of(row // 8 * 8, 8), lax.rem(row, 8)
    near = lax.broadcasted_iota(jnp.int32, (TILE_R, HALF), 1) < HALF - col
    upper = lax.broadcasted_iota(jnp.int32, (WIN // 8, 8, WIN), 1) < 8 - rest
    for k in range(2):
        first, second, third = (pltpu.roll(t, HALF - col, 1) for t in tiles(k))
        tall[k, :TILE_R, :HALF] = jnp.where(near, first, second)
        tall[k, :TILE_R, HALF:] = jnp.where(near, second, third)
        x = tall[k, pl.ds(base, WIN + 8), :].reshape(WIN // 8 + 1, 8, WIN)
        x = pltpu.roll(x, lax.rem(8 - rest, 8), 1)
        win[k] = jnp.where(upper, x[:-1], x[1:]).reshape(WIN, WIN)
        tall[k] = jnp.zeros((TILE_R + 8, WIN), jnp.float32)


def placed(grad, scale, tall, row, col, k):
    base, rest = pl.multiple_of(row // 8 * 8, 8), lax.rem(row, 8)
    lower = lax.broadcasted_iota(jnp.int32, (WIN // 8 + 1, 8, WIN), 1) >= rest
    x = pltpu.roll((grad[k] * scale).reshape(WIN // 8, 8, WIN), rest, 1)
    gap = jnp.zeros((1, 8, WIN), jnp.float32)
    x = jnp.where(lower, jnp.concatenate([x, gap], axis=0), jnp.concatenate([gap, x], axis=0))
    tall[k, pl.ds(base, WIN + 8), :] = x.reshape(WIN + 8, WIN)
    inside = lax.broadcasted_iota(jnp.int32, (TILE_R, HALF), 1) >= col
    first = pltpu.roll(tall[k, :TILE_R, :HALF], lax.rem(col, HALF), 1)
    second = pltpu.roll(tall[k, :TILE_R, HALF:], lax.rem(col, HALF), 1)
    return jnp.concatenate(
        [jnp.where(inside, first, 0.0), jnp.where(inside, second, first), jnp.where(inside, 0.0, second)], axis=1)


def first_kernel(pos, obj, halo, probe, amp_hbm, step, high, low, high_t, low_t, rows, cols,
                 new_obj, edge, spill, middle, sum_hbm,
                 far, win, grad, tall, amp, probe_sum, sems):
    row, col = pos[0, 0], pos[0, 1]
    sum_copy = lambda m: pltpu.make_async_copy(probe_sum.at[m], sum_hbm.at[m], sems.at[2 + m])
    amp_copy = pltpu.make_async_copy(amp_hbm.at[0], amp, sems.at[4])
    amp_copy.start()

    cut_window(lambda k: (obj[k, :, :HALO], obj[k, :, HALO:], halo[k]), tall, win, row, col)

    def add_probe(m, real, imag):
        probe_sum[m, 0] = real
        probe_sum[m, 1] = imag
        sum_copy(m).start()

    window_fit(probe, amp, (high, low, high_t, low_t, rows, cols), far, win, grad, add_probe,
               None, amp_copy)
    scale = step[:1, :1]
    for k in range(2):
        g = placed(grad, scale, tall, row, col, k)
        updated = obj[k] + g[:, :WIN]
        new_obj[k] = updated
        edge[k] = updated[:, :HALO]
        middle[k] = updated[:HALO, HALO:]
        spill[k] = g[:, WIN:]
    for k in range(2):
        sum_copy(k).wait()


def lanes():
    return lax.broadcasted_iota(jnp.int32, (HALO, HALO), 1)


def upward_kernel(above, info, edge, from_left, from_right, spill, upward):
    keep = info[0].astype(jnp.float32)
    for k in range(2):
        own = edge[k, :HALO] + from_left[k, :HALO]
        upward[k] = jnp.where(lanes() >= above[1, 1], own, from_right[k, :HALO] + spill[k, :HALO] * keep)


def merge_kernel(info, obj, from_left, from_right, spill, whole_hbm, source, whole, sems):
    keep = info[0].astype(jnp.float32)
    whole_copy = lambda k: pltpu.make_async_copy(whole.at[k], whole_hbm.at[k], sems.at[k])
    for k in range(2):
        left = obj[k, :, :HALO] + from_left[k]
        whole[k, :, :HALO] = left
        whole[k, :, HALO:] = obj[k, :, HALO:]
        whole_copy(k).start()
        source[k, :, :HALO] = left[LAST:]
        source[k, :, HALO:WIN] = obj[k, LAST:, HALO:]
        source[k, :, WIN:] = from_right[k, LAST:] + spill[k, LAST:] * keep
    for k in range(2):
        whole_copy(k).wait()


def second_kernel(pos, info, source, below_mid, below_rest, probe_hbm, amp_hbm, step, before_hbm,
                  high, low, high_t, low_t, rows, cols,
                  own_grad, downward, keep_sum, send_sum, far, win, grad, tall, amp, probe, before, sems):
    row, col, core = pos[1, 0] - LAST, pos[1, 1], info[1]
    probe_copy = lambda m: pltpu.make_async_copy(probe_hbm.at[m], probe.at[m], sems.at[m])
    before_copy = lambda m: pltpu.make_async_copy(before_hbm.at[m], before.at[m], sems.at[2 + m])
    amp_copy = pltpu.make_async_copy(amp_hbm.at[1], amp, sems.at[4])
    probe_copy(0).start()
    probe_copy(1).start()
    amp_copy.start()
    before_copy(0).start()
    before_copy(1).start()

    def tiles(k):
        lower = (below_rest[k], below_mid[k], below_rest[k])
        return [jnp.concatenate([source[k, :, HALO * t:HALO * t + HALO], lower[t]], axis=0) for t in range(3)]

    cut_window(tiles, tall, win, row, col)

    def add_probe(m, real, imag):
        before_copy(m).wait()

        @pl.when(m == core)
        def _():
            keep_sum[0] = before[m, 0] + real
            keep_sum[1] = before[m, 1] + imag

        @pl.when(m != core)
        def _():
            send_sum[0] = before[m, 0] + real
            send_sum[1] = before[m, 1] + imag

    window_fit(probe, amp, (high, low, high_t, low_t, rows, cols), far, win, grad, add_probe,
               probe_copy, amp_copy)
    scale = step[:1, :1]
    for k in range(2):
        g = placed(grad, scale, tall, row, col, k)
        own_grad[k] = g[:WIN]
        downward[k, :, :HALO] = g[WIN:, :HALO] + g[WIN:, WIN:]
        downward[k, :, HALO:] = g[WIN:, HALO:WIN]


def spill_kernel(above, own_grad, from_above, new_spill):
    for k in range(2):
        new_spill[k, :HALO] = jnp.where(lanes() < above[1, 1], from_above[k, :, :HALO], 0.0)
        new_spill[k, HALO:] = own_grad[k, :, WIN:]


def object_kernel(above, whole, own_grad, from_above, from_left, out):
    for k in range(2):
        fell = jnp.where(lanes() >= above[1, 1], from_above[k, :, :HALO], 0.0)
        out[k, :LAST, :HALO] = whole[k, :LAST, :HALO] + fell + from_left[k, :LAST]
        out[k, :LAST, HALO:] = whole[k, :LAST, HALO:] + from_above[k, :, HALO:]
        out[k, LAST:, :HALO] = whole[k, LAST:, :HALO] + own_grad[k, :, :HALO] + from_left[k, LAST:]
        out[k, LAST:, HALO:] = whole[k, LAST:, HALO:] + own_grad[k, :, HALO:WIN]


def probe_kernel(info, probe, own, other, out):
    core = info[1]
    out[core] = probe[core] + own[...]
    out[1 - core] = probe[1 - core] + other[...]


HBM = object()
AUTO = object()


def call(kernel, outs, scratch, scalars, arrays, copies=0, in_place=None):
    smem = pl.BlockSpec(memory_space=pltpu.SMEM)
    specs = {None: pl.BlockSpec(memory_space=pltpu.VMEM), HBM: pl.BlockSpec(memory_space=pltpu.HBM)}
    specs[AUTO] = specs[None]
    arrays = [x if isinstance(x, tuple) else (x, None) for x in arrays]
    outs = [(o[0], o[1]) if isinstance(o[0], tuple) else (o, None) for o in outs]
    spaces = {None: pltpu.VMEM, HBM: pltpu.HBM, AUTO: pltpu.HBM}
    shapes = [
        jax.ShapeDtypeStruct(shape, jnp.float32) if INTERPRET or where is AUTO else spaces[where](shape, jnp.float32)
        for shape, where in outs
    ]
    operands = [
        x if INTERPRET or where is AUTO else pltpu.with_memory_space_constraint(x, spaces[where]) for x, where in arrays
    ]
    return pl.pallas_call(
        kernel,
        out_shape=shapes,
        in_specs=[smem] * len(scalars) + [specs[where] for _, where in arrays],
        out_specs=[specs[where] for _, where in outs],
        scratch_shapes=[pltpu.VMEM(s, jnp.float32) if isinstance(s, tuple) else s for s in scratch]
        + ([pltpu.SemaphoreType.DMA((copies,))] if copies else []),
        compiler_params=pltpu.CompilerParams(vmem_limit_bytes=24 * 1024 * 1024),
        input_output_aliases=in_place or {},
        interpret=INTERPRET,
    )(*scalars, *operands)


def passed_along(block, axis, distance):
    devices = range(lax.axis_size(axis))
    route = [(i - distance, i) for i in devices if i - distance in devices]
    return lax.ppermute(block, axis, route)


def exchanged(parts, axes):
    return lax.all_to_all(parts, axes, 0, 0, tiled=False)


def swapped(block):
    return lax.ppermute(block, CORE, [(0, 1), (1, 0)])


def summed_everywhere(keep, send, divisor):
    plane = lax.axis_size(PLANE)
    mode = keep + swapped(send)
    parts = exchanged(mode.reshape(plane, -1, WIN), PLANE)
    share = jnp.sum(parts, axis=0)
    for axis in ("col_0", "row_1"):
        parts = exchanged(jnp.broadcast_to(share, (lax.axis_size(axis), *share.shape)), axis)
        share = jnp.sum(parts, axis=0)
    share = share / divisor
    mode = exchanged(jnp.broadcast_to(share, (plane, *share.shape)), PLANE).reshape(2, WIN, WIN)
    return mode, swapped(mode)


def step_once(object_field, probe_modes, scan_positions, amplitudes):
    tables = [jnp.asarray(t) for t in dft_constants()]
    positions = scan_positions[0, 0]
    device_count = lax.axis_size(ROW) * lax.axis_size(COL)
    divisor = math.sqrt(device_count * BATCHES)
    has_right = (lax.axis_index(COL) < lax.axis_size(COL) - 1).astype(jnp.int32)
    tile, side, probe_shape = (2, TILE_R, WIN), (2, TILE_R, HALO), (2, 2, WIN, WIN)
    block, window = (2, HALO, HALO), (2, WIN, WIN)
    fit_scratch = [probe_shape, window, window, (2, TILE_R + 8, WIN), (WIN, WIN), probe_shape]

    halo = passed_along(object_field[:, :, :HALO], COL, -1)
    above = passed_along(positions, ROW, 1)
    info = jnp.stack([has_right, lax.axis_index(CORE)])
    amp, step = call(
        before_kernel, [((BATCHES, WIN, WIN), HBM), (8, HALF)],
        [probe_shape, pltpu.VMEM((BATCHES, WIN, WIN), jnp.bfloat16), (BATCHES, WIN, WIN)],
        [], [(probe_modes, HBM), (amplitudes[0, 0], HBM)], copies=4)
    obj, edge, spill, middle, probe_sum = call(
        first_kernel, [tile, side, side, block, (probe_shape, HBM)], fit_scratch, [positions],
        [object_field, halo, probe_modes, (amp, HBM), step, *tables], copies=5, in_place={1: 0, 2: 1})
    from_right = passed_along(edge, COL, -1)
    from_left = passed_along(spill, COL, 1)
    below_mid = passed_along(middle, ROW, -1)
    (upward,) = call(upward_kernel, [block], [], [above, info], [edge, from_left, from_right, spill])
    below_rest = passed_along(upward, ROW, -1)
    whole, source = call(
        merge_kernel, [(tile, HBM), (2, WIN, WIDE)], [tile], [info], [obj, from_left, from_right, spill], copies=2)
    grad, downward, keep, send = call(
        second_kernel, [(2, WIN, WIDE), (2, HALO, WIN), window, window],
        fit_scratch + [probe_shape], [positions, info],
        [source, below_mid, below_rest, (probe_modes, HBM), (amp, HBM), step, (probe_sum, HBM), *tables], copies=5, in_place={2: 0})
    own, other = summed_everywhere(keep, send, divisor)
    from_above = passed_along(downward, ROW, 1)
    (spill,) = call(spill_kernel, [side], [], [above], [grad, from_above])
    from_left = passed_along(spill, COL, 1)
    (object_out,) = call(
        object_kernel, [(tile, AUTO)], [], [above], [(whole, AUTO), (grad, AUTO), (from_above, AUTO), (from_left, AUTO)])
    (probe_out,) = call(probe_kernel, [(probe_shape, AUTO)], [], [info], [(probe_modes, AUTO), own, other])
    return (object_out, probe_out)


def solution(mesh):
    torus = Mesh(mesh.devices.reshape(4, 4, 4, 4, 2), ("row_0", "row_1", "col_0", "col_1", "col_2"))
    in_specs = (P(None, ROW, COL), P(), P(ROW, COL, None, None), P(ROW, COL, None, None, None))
    out_specs = (P(None, ROW, COL), P())
    return jax.shard_map(step_once, mesh=torus, in_specs=in_specs, out_specs=out_specs, check_vma=False)
```

```python
import math

import jax
import jax.numpy as jnp
import numpy as np
from jax import lax
from jax.experimental import pallas as pl
from jax.experimental.pallas import tpu as pltpu
from jax.sharding import Mesh
from jax.sharding import PartitionSpec as P


HALO = 128
BATCHES = 2
WIN = 256
HALF = 128
INTERPRET = False
ROW = ("row_0", "row_1")
COL = ("col_0", "col_1", "col_2")
PLANE = ("row_0", "col_1")
CORE = "col_2"


def halves(x):
    high = x.astype(jnp.bfloat16)
    low = (x - high.astype(np.float64)).astype(jnp.bfloat16)
    return high, low


def dft_constants():
    index = np.arange(HALF)
    angle = 2.0 * np.pi * (np.outer(index, index) % HALF) / HALF
    cosine = np.cos(angle) / 16.0
    sine = -np.sin(angle) / 16.0
    forward = np.block([[cosine, -sine], [sine, cosine]])
    high, low = halves(forward)
    turn = 2.0 * np.pi * index / WIN
    twiddle = np.stack([np.cos(turn), -np.sin(turn)]).astype(np.float32)
    rows = np.ascontiguousarray(np.broadcast_to(twiddle[:, :, None], (2, HALF, HALF)))
    cols = np.ascontiguousarray(np.broadcast_to(twiddle[:, None, :], (2, 8, HALF)))
    return high, low, np.ascontiguousarray(high.T), np.ascontiguousarray(low.T), rows, cols


def split3(x, axis):
    high = x.astype(jnp.bfloat16)
    low = (x - high.astype(jnp.float32)).astype(jnp.bfloat16)
    return jnp.concatenate([high, low, high], axis=axis)


def left_dft(matrix, x):
    return jnp.dot(matrix, split3(x, 0), preferred_element_type=jnp.float32)


def right_dft(x, matrix):
    return jnp.dot(split3(x, 1), matrix, preferred_element_type=jnp.float32)


def forward_dft(real, imag, left, right_t, twr, twc):
    t_r, t_i = twr
    c_r, c_i = twc
    a_r, b_r, a_i, b_i = real[:HALF], real[HALF:], imag[:HALF], imag[HALF:]
    d_r, d_i = a_r - b_r, a_i - b_i
    even = left_dft(left, jnp.concatenate([a_r + b_r, a_i + b_i], axis=0))
    odd = left_dft(left, jnp.concatenate([d_r * t_r - d_i * t_i, d_r * t_i + d_i * t_r], axis=0))
    real = jnp.concatenate([even[:HALF], odd[:HALF]], axis=0)
    imag = jnp.concatenate([even[HALF:], odd[HALF:]], axis=0)
    a_r, b_r, a_i, b_i = real[:, :HALF], real[:, HALF:], imag[:, :HALF], imag[:, HALF:]
    d_r, d_i = a_r - b_r, a_i - b_i
    even = right_dft(jnp.concatenate([a_r + b_r, a_i + b_i], axis=1), right_t)
    odd = right_dft(jnp.concatenate([d_r * c_r - d_i * c_i, d_r * c_i + d_i * c_r], axis=1), right_t)
    real = jnp.concatenate([even[:, :HALF], odd[:, :HALF]], axis=1)
    imag = jnp.concatenate([even[:, HALF:], odd[:, HALF:]], axis=1)
    return real, imag


def inverse_dft(real, imag, left_t, right, twr, twc):
    t_r, t_i = twr
    c_r, c_i = twc
    even = right_dft(jnp.concatenate([real[:, :HALF], imag[:, :HALF]], axis=1), right)
    odd = right_dft(jnp.concatenate([real[:, HALF:], imag[:, HALF:]], axis=1), right)
    o_r, o_i = odd[:, :HALF], odd[:, HALF:]
    o_r, o_i = o_r * c_r + o_i * c_i, o_i * c_r - o_r * c_i
    e_r, e_i = even[:, :HALF], even[:, HALF:]
    real = jnp.concatenate([e_r + o_r, e_r - o_r], axis=1)
    imag = jnp.concatenate([e_i + o_i, e_i - o_i], axis=1)
    even = left_dft(left_t, jnp.concatenate([real[:HALF], imag[:HALF]], axis=0))
    odd = left_dft(left_t, jnp.concatenate([real[HALF:], imag[HALF:]], axis=0))
    o_r, o_i = odd[:HALF], odd[HALF:]
    o_r, o_i = o_r * t_r + o_i * t_i, o_i * t_r - o_r * t_i
    e_r, e_i = even[:HALF], even[HALF:]
    real = jnp.concatenate([e_r + o_r, e_r - o_r], axis=0)
    imag = jnp.concatenate([e_i + o_i, e_i - o_i], axis=0)
    return real, imag


def left_of(high, low):
    return jnp.concatenate([high[...], high[...], low[...]], axis=1)


def right_of(high, low):
    return jnp.concatenate([high[...], high[...], low[...]], axis=0)


def window_fit(probe, amplitude, tables, far, window_ref, gradient, add_probe, probe_copy, amp_copy):
    high, low, high_t, low_t, rows, cols = tables

    def twiddles():
        twr = tuple(jnp.concatenate([rows[k], rows[k]], axis=1) for k in range(2))
        twc = tuple(cols[k][:1] for k in range(2))
        return twr, twc

    def outward(m, carry):
        if probe_copy is not None:
            probe_copy(m).wait()
        twr, twc = twiddles()
        w_r, w_i = window_ref[0], window_ref[1]
        p_r, p_i = probe[m, 0], probe[m, 1]
        f_r, f_i = forward_dft(p_r * w_r - p_i * w_i, p_r * w_i + p_i * w_r,
                               left_of(high, low), right_of(high_t, low_t), twr, twc)
        far[m, 0] = f_r
        far[m, 1] = f_i
        return carry

    lax.fori_loop(0, 2, outward, 0)
    intensity = far[0, 0] * far[0, 0] + far[0, 1] * far[0, 1]
    intensity = intensity + (far[1, 0] * far[1, 0] + far[1, 1] * far[1, 1])
    amp_copy.wait()
    factor = amplitude[...] * lax.rsqrt(jnp.maximum(intensity, 0.1)) - 1.0
    for m in range(2):
        far[m, 0] = far[m, 0] * factor
        far[m, 1] = far[m, 1] * factor
    gradient[...] = jnp.zeros(gradient.shape, jnp.float32)

    def inward(m, carry):
        twr, twc = twiddles()
        x_r, x_i = inverse_dft(far[m, 0], far[m, 1], left_of(high_t, low_t), right_of(high, low), twr, twc)
        w_r, w_i = window_ref[0], window_ref[1]
        p_r, p_i = probe[m, 0], probe[m, 1]
        gradient[0] += p_r * x_r + p_i * x_i
        gradient[1] += p_r * x_i - p_i * x_r
        add_probe(m, w_r * x_r + w_i * x_i, w_r * x_i - w_i * x_r)
        return carry

    lax.fori_loop(0, 2, inward, 0)


def before_kernel(probe_hbm, amp_hbm, amp_out, step_out, probe, amp, ordered, sems):
    amp_copy = pltpu.make_async_copy(amp_hbm, amp, sems.at[0])
    probe_copy = pltpu.make_async_copy(probe_hbm, probe, sems.at[1])
    out_copy = lambda b: pltpu.make_async_copy(ordered.at[b], amp_out.at[b], sems.at[2 + b])
    amp_copy.start()
    probe_copy.start()
    out_at = lax.broadcasted_iota(jnp.int32, (WIN, WIN), 0)
    in_at = lax.broadcasted_iota(jnp.int32, (WIN, WIN), 1)
    wanted = jnp.where(out_at < HALF, 2 * out_at, 2 * (out_at - HALF) + 1)
    pick = jnp.where(in_at == wanted, 1.0, 0.0).astype(jnp.bfloat16)
    amp_copy.wait()
    for b in range(BATCHES):
        rows = jnp.dot(pick, amp[b], preferred_element_type=jnp.float32).astype(jnp.bfloat16)
        ordered[b] = lax.dot_general(rows, pick, (((1,), (1,)), ((), ())), preferred_element_type=jnp.float32)
        out_copy(b).start()
    probe_copy.wait()
    total = jnp.zeros((8, HALF), jnp.float32)
    for m in range(2):
        for k in range(2):
            square = probe[m, k] * probe[m, k]
            square = jnp.sum(square.reshape(WIN // 8, 8, WIN), axis=0)
            total = total + square[:, :HALF] + square[:, HALF:]
    power = jnp.sum(total) / (WIN * WIN)
    step_out[...] = jnp.full((8, HALF), 1.0, jnp.float32) / (power + 1e-06)
    for b in range(BATCHES):
        out_copy(b).wait()


TILE_R = 384
LAST = TILE_R - WIN
WIDE = WIN + HALO
LOW = 192


def cut_window(tiles, tall, win, row, col):
    base, rest = pl.multiple_of(row // 8 * 8, 8), lax.rem(row, 8)
    near = lax.broadcasted_iota(jnp.int32, (TILE_R, HALF), 1) < HALF - col
    upper = lax.broadcasted_iota(jnp.int32, (WIN // 8, 8, WIN), 1) < 8 - rest
    for k in range(2):
        first, second, third = (pltpu.roll(t, HALF - col, 1) for t in tiles(k))
        tall[k, :TILE_R, :HALF] = jnp.where(near, first, second)
        tall[k, :TILE_R, HALF:] = jnp.where(near, second, third)
        x = tall[k, pl.ds(base, WIN + 8), :].reshape(WIN // 8 + 1, 8, WIN)
        x = pltpu.roll(x, lax.rem(8 - rest, 8), 1)
        win[k] = jnp.where(upper, x[:-1], x[1:]).reshape(WIN, WIN)
        tall[k] = jnp.zeros((TILE_R + 8, WIN), jnp.float32)


def placed(grad, scale, tall, row, col, k):
    base, rest = pl.multiple_of(row // 8 * 8, 8), lax.rem(row, 8)
    lower = lax.broadcasted_iota(jnp.int32, (WIN // 8 + 1, 8, WIN), 1) >= rest
    x = pltpu.roll((grad[k] * scale).reshape(WIN // 8, 8, WIN), rest, 1)
    gap = jnp.zeros((1, 8, WIN), jnp.float32)
    x = jnp.where(lower, jnp.concatenate([x, gap], axis=0), jnp.concatenate([gap, x], axis=0))
    tall[k, pl.ds(base, WIN + 8), :] = x.reshape(WIN + 8, WIN)
    inside = lax.broadcasted_iota(jnp.int32, (TILE_R, HALF), 1) >= col
    first = pltpu.roll(tall[k, :TILE_R, :HALF], lax.rem(col, HALF), 1)
    second = pltpu.roll(tall[k, :TILE_R, HALF:], lax.rem(col, HALF), 1)
    return jnp.concatenate(
        [jnp.where(inside, first, 0.0), jnp.where(inside, second, first), jnp.where(inside, 0.0, second)], axis=1)


def first_kernel(pos, obj, halo, probe, amp_hbm, step, high, low, high_t, low_t, rows, cols,
                 new_obj, spill, edge, middle, sum_hbm,
                 far, win, grad, tall, amp, probe_sum, sems):
    row, col = pos[0, 0], pos[0, 1]
    sum_copy = lambda m: pltpu.make_async_copy(probe_sum.at[m], sum_hbm.at[m], sems.at[2 + m])
    amp_copy = pltpu.make_async_copy(amp_hbm.at[0], amp, sems.at[4])
    amp_copy.start()

    cut_window(lambda k: (obj[k, :, :HALO], obj[k, :, HALO:], halo[k]), tall, win, row, col)

    def add_probe(m, real, imag):
        probe_sum[m, 0] = real
        probe_sum[m, 1] = imag
        sum_copy(m).start()

    window_fit(probe, amp, (high, low, high_t, low_t, rows, cols), far, win, grad, add_probe,
               None, amp_copy)
    scale = step[:1, :1]
    for k in range(2):
        g = placed(grad, scale, tall, row, col, k)
        updated = obj[k] + g[:, :WIN]
        new_obj[k] = updated
        edge[k, :HALO] = updated[:HALO, :HALO]
        edge[k, HALO:] = updated[LOW:, :HALO]
        middle[k] = updated[:HALO, HALO:]
        spill[k] = g[:, WIN:]
    for k in range(2):
        sum_copy(k).wait()


def lanes():
    return lax.broadcasted_iota(jnp.int32, (HALO, HALO), 1)


def upward_kernel(above, info, edge, from_left, from_right, spill, upward):
    keep = info[0].astype(jnp.float32)
    for k in range(2):
        own = edge[k, :HALO] + from_left[k, :HALO]
        upward[k] = jnp.where(lanes() >= above[1, 1], own, from_right[k, :HALO] + spill[k, :HALO] * keep)


def merge_kernel(info, obj, from_left, from_right, spill, whole_hbm, source, whole, sems):
    keep = info[0].astype(jnp.float32)
    whole_copy = lambda k: pltpu.make_async_copy(whole.at[k], whole_hbm.at[k], sems.at[k])
    for k in range(2):
        left = obj[k, :, :HALO] + from_left[k]
        whole[k, :, :HALO] = left
        whole[k, :, HALO:] = obj[k, :, HALO:]
        whole_copy(k).start()
        source[k, :, :HALO] = left[LAST:]
        source[k, :, HALO:WIN] = obj[k, LAST:, HALO:]
        source[k, :LOW - LAST, WIN:] = jnp.zeros((LOW - LAST, HALO), jnp.float32)
        source[k, LOW - LAST:, WIN:] = from_right[k, HALO:] + spill[k, LOW:] * keep
    for k in range(2):
        whole_copy(k).wait()


def second_kernel(pos, info, source, below_mid, below_rest, probe_hbm, amp_hbm, step, before_hbm,
                  high, low, high_t, low_t, rows, cols,
                  own_grad, downward, keep_sum, send_sum, far, win, grad, tall, amp, probe, before, sems):
    row, col, core = pos[1, 0] - LAST, pos[1, 1], info[1]
    probe_copy = lambda m: pltpu.make_async_copy(probe_hbm.at[m], probe.at[m], sems.at[m])
    before_copy = lambda m: pltpu.make_async_copy(before_hbm.at[m], before.at[m], sems.at[2 + m])
    amp_copy = pltpu.make_async_copy(amp_hbm.at[1], amp, sems.at[4])
    probe_copy(0).start()
    probe_copy(1).start()
    amp_copy.start()
    before_copy(0).start()
    before_copy(1).start()

    def tiles(k):
        lower = (below_rest[k], below_mid[k], below_rest[k])
        return [jnp.concatenate([source[k, :, HALO * t:HALO * t + HALO], lower[t]], axis=0) for t in range(3)]

    cut_window(tiles, tall, win, row, col)

    def add_probe(m, real, imag):
        before_copy(m).wait()

        @pl.when(m == core)
        def _():
            keep_sum[0] = before[m, 0] + real
            keep_sum[1] = before[m, 1] + imag

        @pl.when(m != core)
        def _():
            send_sum[0] = before[m, 0] + real
            send_sum[1] = before[m, 1] + imag

    window_fit(probe, amp, (high, low, high_t, low_t, rows, cols), far, win, grad, add_probe,
               probe_copy, amp_copy)
    scale = step[:1, :1]
    for k in range(2):
        g = placed(grad, scale, tall, row, col, k)
        own_grad[k] = g[:WIN]
        downward[k, :, :HALO] = g[WIN:, :HALO] + g[WIN:, WIN:]
        downward[k, :, HALO:] = g[WIN:, HALO:WIN]


def spill_kernel(above, own_grad, from_above, new_spill):
    for k in range(2):
        new_spill[k, :HALO] = jnp.where(lanes() < above[1, 1], from_above[k, :, :HALO], 0.0)
        new_spill[k, HALO:] = own_grad[k, :, WIN:]


def object_kernel(above, whole, own_grad, from_above, from_left, out):
    for k in range(2):
        fell = jnp.where(lanes() >= above[1, 1], from_above[k, :, :HALO], 0.0)
        out[k, :LAST, :HALO] = whole[k, :LAST, :HALO] + fell + from_left[k, :LAST]
        out[k, :LAST, HALO:] = whole[k, :LAST, HALO:] + from_above[k, :, HALO:]
        out[k, LAST:, :HALO] = whole[k, LAST:, :HALO] + own_grad[k, :, :HALO] + from_left[k, LAST:]
        out[k, LAST:, HALO:] = whole[k, LAST:, HALO:] + own_grad[k, :, HALO:WIN]


def own_kernel(info, probe_hbm, own, out_hbm, rest, probe, half, sems):
    core = info[1]
    here = pltpu.make_async_copy(probe_hbm.at[core], probe, sems.at[0])
    there = pltpu.make_async_copy(probe_hbm.at[1 - core], rest, sems.at[1])
    done = pltpu.make_async_copy(half, out_hbm.at[core], sems.at[2])
    here.start()
    there.start()
    here.wait()
    half[...] = probe[...] + own[...]
    done.start()
    there.wait()
    done.wait()


def other_kernel(info, partial_hbm, rest, other, out_hbm, half, sems):
    done = pltpu.make_async_copy(half, out_hbm.at[1 - info[1]], sems.at[0])
    half[...] = rest[...] + other[...]
    done.start()
    done.wait()


HBM = object()
AUTO = object()


def call(kernel, outs, scratch, scalars, arrays, copies=0, in_place=None):
    smem = pl.BlockSpec(memory_space=pltpu.SMEM)
    specs = {None: pl.BlockSpec(memory_space=pltpu.VMEM), HBM: pl.BlockSpec(memory_space=pltpu.HBM)}
    specs[AUTO] = specs[None]
    arrays = [x if isinstance(x, tuple) else (x, None) for x in arrays]
    outs = [(o[0], o[1]) if isinstance(o[0], tuple) else (o, None) for o in outs]
    spaces = {None: pltpu.VMEM, HBM: pltpu.HBM, AUTO: pltpu.HBM}
    shapes = [
        jax.ShapeDtypeStruct(shape, jnp.float32) if INTERPRET or where is AUTO else spaces[where](shape, jnp.float32)
        for shape, where in outs
    ]
    operands = [
        x if INTERPRET or where is AUTO else pltpu.with_memory_space_constraint(x, spaces[where]) for x, where in arrays
    ]
    if not INTERPRET:
        scalars = [pltpu.with_memory_space_constraint(x, pltpu.SMEM) for x in scalars]
    return pl.pallas_call(
        kernel,
        out_shape=shapes,
        in_specs=[smem] * len(scalars) + [specs[where] for _, where in arrays],
        out_specs=[specs[where] for _, where in outs],
        scratch_shapes=[pltpu.VMEM(s, jnp.float32) if isinstance(s, tuple) else s for s in scratch]
        + ([pltpu.SemaphoreType.DMA((copies,))] if copies else []),
        compiler_params=pltpu.CompilerParams(vmem_limit_bytes=24 * 1024 * 1024),
        input_output_aliases=in_place or {},
        interpret=INTERPRET,
    )(*scalars, *operands)


def passed_along(block, axis, distance):
    devices = range(lax.axis_size(axis))
    route = [(i - distance, i) for i in devices if i - distance in devices]
    return lax.ppermute(block, axis, route)


def exchanged(parts, axes):
    return lax.all_to_all(parts, axes, 0, 0, tiled=False)


def swapped(block):
    return lax.ppermute(block, CORE, [(0, 1), (1, 0)])


def summed_everywhere(keep, send, divisor):
    plane = lax.axis_size(PLANE)
    mode = keep + swapped(send)
    parts = exchanged(mode.reshape(plane, -1, WIN), PLANE)
    share = jnp.sum(parts, axis=0)
    for axis in ("col_0", "row_1"):
        parts = exchanged(jnp.broadcast_to(share, (lax.axis_size(axis), *share.shape)), axis)
        share = jnp.sum(parts, axis=0)
    share = share / divisor
    mode = exchanged(jnp.broadcast_to(share, (plane, *share.shape)), PLANE).reshape(2, WIN, WIN)
    return mode, swapped(mode)


def step_once(object_field, probe_modes, scan_positions, amplitudes):
    tables = [jnp.asarray(t) for t in dft_constants()]
    positions = scan_positions[0, 0]
    device_count = lax.axis_size(ROW) * lax.axis_size(COL)
    divisor = math.sqrt(device_count * BATCHES)
    has_right = (lax.axis_index(COL) < lax.axis_size(COL) - 1).astype(jnp.int32)
    tile, side, probe_shape = (2, TILE_R, WIN), (2, TILE_R, HALO), (2, 2, WIN, WIN)
    block, window = (2, HALO, HALO), (2, WIN, WIN)
    fit_scratch = [probe_shape, window, window, (2, TILE_R + 8, WIN), (WIN, WIN), probe_shape]

    halo = passed_along(object_field[:, :, :HALO], COL, -1)
    above = passed_along(positions, ROW, 1)
    info = jnp.stack([has_right, lax.axis_index(CORE)])
    amp, step = call(
        before_kernel, [((BATCHES, WIN, WIN), HBM), (8, HALF)],
        [probe_shape, pltpu.VMEM((BATCHES, WIN, WIN), jnp.bfloat16), (BATCHES, WIN, WIN)],
        [], [(probe_modes, HBM), (amplitudes[0, 0], HBM)], copies=4)
    obj, spill, edge, middle, probe_sum = call(
        first_kernel, [tile, side, (2, TILE_R - LOW + HALO, HALO), block, (probe_shape, HBM)], fit_scratch, [positions],
        [object_field, halo, probe_modes, (amp, HBM), step, *tables], copies=5, in_place={1: 0, 2: 1})
    from_right = passed_along(edge, COL, -1)
    from_left = passed_along(spill, COL, 1)
    below_mid = passed_along(middle, ROW, -1)
    (upward,) = call(upward_kernel, [block], [], [above, info], [edge, from_left, from_right, spill])
    below_rest = passed_along(upward, ROW, -1)
    whole, source = call(
        merge_kernel, [(tile, HBM), (2, WIN, WIDE)], [tile], [info], [obj, from_left, from_right, spill], copies=2)
    grad, downward, keep, send = call(
        second_kernel, [(2, WIN, WIDE), (2, HALO, WIN), window, window],
        fit_scratch + [probe_shape], [positions, info],
        [source, below_mid, below_rest, (probe_modes, HBM), (amp, HBM), step, (probe_sum, HBM), *tables], copies=5, in_place={2: 0})
    own, other = summed_everywhere(keep, send, divisor)
    from_above = passed_along(downward, ROW, 1)
    (spill,) = call(spill_kernel, [side], [], [above], [grad, from_above])
    from_left = passed_along(spill, COL, 1)
    (object_out,) = call(
        object_kernel, [(tile, AUTO)], [], [above], [(whole, AUTO), (grad, AUTO), (from_above, AUTO), (from_left, AUTO)])
    partial, rest = call(
        own_kernel, [(probe_shape, HBM), window], [window, window], [info], [(probe_modes, HBM), own], copies=3)
    (probe_out,) = call(
        other_kernel, [(probe_shape, HBM)], [window], [info], [(partial, HBM), rest, other], copies=1, in_place={1: 0})
    return (object_out, probe_out)


def solution(mesh):
    torus = Mesh(mesh.devices.reshape(4, 4, 4, 4, 2), ("row_0", "row_1", "col_0", "col_1", "col_2"))
    in_specs = (P(None, ROW, COL), P(), P(ROW, COL, None, None), P(ROW, COL, None, None, None))
    out_specs = (P(None, ROW, COL), P())
    return jax.shard_map(step_once, mesh=torus, in_specs=in_specs, out_specs=out_specs, check_vma=False)
```

```python
import math

import jax
import jax.numpy as jnp
import numpy as np
from jax import lax
from jax.experimental import pallas as pl
from jax.experimental.pallas import tpu as pltpu
from jax.sharding import Mesh
from jax.sharding import PartitionSpec as P


HALO = 128
BATCHES = 2
WIN = 256
HALF = 128
INTERPRET = False
ROW = ("row_0", "row_1")
COL = ("col_0", "col_1", "col_2")
PLANE = ("row_0", "col_1")
CORE = "col_2"


def halves(x):
    high = x.astype(jnp.bfloat16)
    low = (x - high.astype(np.float64)).astype(jnp.bfloat16)
    return high, low


def dft_constants():
    index = np.arange(HALF)
    angle = 2.0 * np.pi * (np.outer(index, index) % HALF) / HALF
    cosine = np.cos(angle) / 16.0
    sine = -np.sin(angle) / 16.0
    forward = np.block([[cosine, -sine], [sine, cosine]])
    high, low = halves(forward)
    turn = 2.0 * np.pi * index / WIN
    twiddle = np.stack([np.cos(turn), -np.sin(turn)]).astype(np.float32)
    rows = np.ascontiguousarray(np.broadcast_to(twiddle[:, :, None], (2, HALF, HALF)))
    cols = np.ascontiguousarray(np.broadcast_to(twiddle[:, None, :], (2, 8, HALF)))
    return high, low, np.ascontiguousarray(high.T), np.ascontiguousarray(low.T), rows, cols


def split3(x, axis):
    high = x.astype(jnp.bfloat16)
    low = (x - high.astype(jnp.float32)).astype(jnp.bfloat16)
    return jnp.concatenate([high, low, high], axis=axis)


def left_dft(matrix, x):
    return jnp.dot(matrix, split3(x, 0), preferred_element_type=jnp.float32)


def right_dft(x, matrix):
    return jnp.dot(split3(x, 1), matrix, preferred_element_type=jnp.float32)


def forward_dft(real, imag, left, right_t, twr, twc):
    t_r, t_i = twr
    c_r, c_i = twc
    a_r, b_r, a_i, b_i = real[:HALF], real[HALF:], imag[:HALF], imag[HALF:]
    d_r, d_i = a_r - b_r, a_i - b_i
    even = left_dft(left, jnp.concatenate([a_r + b_r, a_i + b_i], axis=0))
    odd = left_dft(left, jnp.concatenate([d_r * t_r - d_i * t_i, d_r * t_i + d_i * t_r], axis=0))
    real = jnp.concatenate([even[:HALF], odd[:HALF]], axis=0)
    imag = jnp.concatenate([even[HALF:], odd[HALF:]], axis=0)
    a_r, b_r, a_i, b_i = real[:, :HALF], real[:, HALF:], imag[:, :HALF], imag[:, HALF:]
    d_r, d_i = a_r - b_r, a_i - b_i
    even = right_dft(jnp.concatenate([a_r + b_r, a_i + b_i], axis=1), right_t)
    odd = right_dft(jnp.concatenate([d_r * c_r - d_i * c_i, d_r * c_i + d_i * c_r], axis=1), right_t)
    real = jnp.concatenate([even[:, :HALF], odd[:, :HALF]], axis=1)
    imag = jnp.concatenate([even[:, HALF:], odd[:, HALF:]], axis=1)
    return real, imag


def inverse_dft(real, imag, left_t, right, twr, twc):
    t_r, t_i = twr
    c_r, c_i = twc
    even = right_dft(jnp.concatenate([real[:, :HALF], imag[:, :HALF]], axis=1), right)
    odd = right_dft(jnp.concatenate([real[:, HALF:], imag[:, HALF:]], axis=1), right)
    o_r, o_i = odd[:, :HALF], odd[:, HALF:]
    o_r, o_i = o_r * c_r + o_i * c_i, o_i * c_r - o_r * c_i
    e_r, e_i = even[:, :HALF], even[:, HALF:]
    real = jnp.concatenate([e_r + o_r, e_r - o_r], axis=1)
    imag = jnp.concatenate([e_i + o_i, e_i - o_i], axis=1)
    even = left_dft(left_t, jnp.concatenate([real[:HALF], imag[:HALF]], axis=0))
    odd = left_dft(left_t, jnp.concatenate([real[HALF:], imag[HALF:]], axis=0))
    o_r, o_i = odd[:HALF], odd[HALF:]
    o_r, o_i = o_r * t_r + o_i * t_i, o_i * t_r - o_r * t_i
    e_r, e_i = even[:HALF], even[HALF:]
    real = jnp.concatenate([e_r + o_r, e_r - o_r], axis=0)
    imag = jnp.concatenate([e_i + o_i, e_i - o_i], axis=0)
    return real, imag


def left_of(high, low):
    return jnp.concatenate([high[...], high[...], low[...]], axis=1)


def right_of(high, low):
    return jnp.concatenate([high[...], high[...], low[...]], axis=0)


def window_fit(probe, amplitude, tables, far, window_ref, gradient, add_probe, probe_copy, amp_copy):
    high, low, high_t, low_t, rows, cols = tables

    def twiddles():
        twr = tuple(jnp.concatenate([rows[k], rows[k]], axis=1) for k in range(2))
        twc = tuple(cols[k][:1] for k in range(2))
        return twr, twc

    def outward(m, carry):
        if probe_copy is not None:
            probe_copy(m).wait()
        twr, twc = twiddles()
        w_r, w_i = window_ref[0], window_ref[1]
        p_r, p_i = probe[m, 0], probe[m, 1]
        f_r, f_i = forward_dft(p_r * w_r - p_i * w_i, p_r * w_i + p_i * w_r,
                               left_of(high, low), right_of(high_t, low_t), twr, twc)
        far[m, 0] = f_r
        far[m, 1] = f_i
        return carry

    lax.fori_loop(0, 2, outward, 0)
    intensity = far[0, 0] * far[0, 0] + far[0, 1] * far[0, 1]
    intensity = intensity + (far[1, 0] * far[1, 0] + far[1, 1] * far[1, 1])
    amp_copy.wait()
    factor = amplitude[...] * lax.rsqrt(jnp.maximum(intensity, 0.1)) - 1.0
    for m in range(2):
        far[m, 0] = far[m, 0] * factor
        far[m, 1] = far[m, 1] * factor
    gradient[...] = jnp.zeros(gradient.shape, jnp.float32)

    def inward(m, carry):
        twr, twc = twiddles()
        x_r, x_i = inverse_dft(far[m, 0], far[m, 1], left_of(high_t, low_t), right_of(high, low), twr, twc)
        w_r, w_i = window_ref[0], window_ref[1]
        p_r, p_i = probe[m, 0], probe[m, 1]
        gradient[0] += p_r * x_r + p_i * x_i
        gradient[1] += p_r * x_i - p_i * x_r
        add_probe(m, w_r * x_r + w_i * x_i, w_r * x_i - w_i * x_r)
        return carry

    lax.fori_loop(0, 2, inward, 0)


def before_kernel(probe_hbm, amp_hbm, amp_out, step_out, probe, amp, ordered, sems):
    amp_copy = pltpu.make_async_copy(amp_hbm, amp, sems.at[0])
    probe_copy = pltpu.make_async_copy(probe_hbm, probe, sems.at[1])
    out_copy = lambda b: pltpu.make_async_copy(ordered.at[b], amp_out.at[b], sems.at[2 + b])
    amp_copy.start()
    probe_copy.start()
    out_at = lax.broadcasted_iota(jnp.int32, (WIN, WIN), 0)
    in_at = lax.broadcasted_iota(jnp.int32, (WIN, WIN), 1)
    wanted = jnp.where(out_at < HALF, 2 * out_at, 2 * (out_at - HALF) + 1)
    pick = jnp.where(in_at == wanted, 1.0, 0.0).astype(jnp.bfloat16)
    amp_copy.wait()
    for b in range(BATCHES):
        rows = jnp.dot(pick, amp[b], preferred_element_type=jnp.float32).astype(jnp.bfloat16)
        ordered[b] = lax.dot_general(rows, pick, (((1,), (1,)), ((), ())), preferred_element_type=jnp.float32)
        out_copy(b).start()
    probe_copy.wait()
    total = jnp.zeros((8, HALF), jnp.float32)
    for m in range(2):
        for k in range(2):
            square = probe[m, k] * probe[m, k]
            square = jnp.sum(square.reshape(WIN // 8, 8, WIN), axis=0)
            total = total + square[:, :HALF] + square[:, HALF:]
    power = jnp.sum(total) / (WIN * WIN)
    step_out[...] = jnp.full((8, HALF), 1.0, jnp.float32) / (power + 1e-06)
    for b in range(BATCHES):
        out_copy(b).wait()


TILE_R = 384
LAST = TILE_R - WIN
WIDE = WIN + HALO
LOW = 192


def cut_window(tiles, tall, win, row, col):
    base, rest = pl.multiple_of(row // 8 * 8, 8), lax.rem(row, 8)
    near = lax.broadcasted_iota(jnp.int32, (TILE_R, HALF), 1) < HALF - col
    upper = lax.broadcasted_iota(jnp.int32, (WIN // 8, 8, WIN), 1) < 8 - rest
    for k in range(2):
        first, second, third = (pltpu.roll(t, HALF - col, 1) for t in tiles(k))
        tall[k, :TILE_R, :HALF] = jnp.where(near, first, second)
        tall[k, :TILE_R, HALF:] = jnp.where(near, second, third)
        x = tall[k, pl.ds(base, WIN + 8), :].reshape(WIN // 8 + 1, 8, WIN)
        x = pltpu.roll(x, lax.rem(8 - rest, 8), 1)
        win[k] = jnp.where(upper, x[:-1], x[1:]).reshape(WIN, WIN)
        tall[k] = jnp.zeros((TILE_R + 8, WIN), jnp.float32)


def placed(grad, scale, tall, row, col, k):
    base, rest = pl.multiple_of(row // 8 * 8, 8), lax.rem(row, 8)
    lower = lax.broadcasted_iota(jnp.int32, (WIN // 8 + 1, 8, WIN), 1) >= rest
    x = pltpu.roll((grad[k] * scale).reshape(WIN // 8, 8, WIN), rest, 1)
    gap = jnp.zeros((1, 8, WIN), jnp.float32)
    x = jnp.where(lower, jnp.concatenate([x, gap], axis=0), jnp.concatenate([gap, x], axis=0))
    tall[k, pl.ds(base, WIN + 8), :] = x.reshape(WIN + 8, WIN)
    inside = lax.broadcasted_iota(jnp.int32, (TILE_R, HALF), 1) >= col
    first = pltpu.roll(tall[k, :TILE_R, :HALF], lax.rem(col, HALF), 1)
    second = pltpu.roll(tall[k, :TILE_R, HALF:], lax.rem(col, HALF), 1)
    return jnp.concatenate(
        [jnp.where(inside, first, 0.0), jnp.where(inside, second, first), jnp.where(inside, 0.0, second)], axis=1)


def first_kernel(pos, obj, halo, probe, amp_hbm, step, high, low, high_t, low_t, rows, cols,
                 new_obj, spill, edge, middle, sum_hbm,
                 far, win, grad, tall, amp, probe_sum, sems):
    row, col = pos[0, 0], pos[0, 1]
    sum_copy = lambda m: pltpu.make_async_copy(probe_sum.at[m], sum_hbm.at[m], sems.at[2 + m])
    amp_copy = pltpu.make_async_copy(amp_hbm.at[0], amp, sems.at[4])
    amp_copy.start()

    cut_window(lambda k: (obj[k, :, :HALO], obj[k, :, HALO:], halo[k]), tall, win, row, col)

    def add_probe(m, real, imag):
        probe_sum[m, 0] = real
        probe_sum[m, 1] = imag
        sum_copy(m).start()

    window_fit(probe, amp, (high, low, high_t, low_t, rows, cols), far, win, grad, add_probe,
               None, amp_copy)
    scale = step[:1, :1]
    for k in range(2):
        g = placed(grad, scale, tall, row, col, k)
        updated = obj[k] + g[:, :WIN]
        new_obj[k] = updated
        edge[k, :HALO] = updated[:HALO, :HALO]
        edge[k, HALO:] = updated[LOW:, :HALO]
        middle[k] = updated[:HALO, HALO:]
        spill[k] = g[:, WIN:]
    for k in range(2):
        sum_copy(k).wait()


def lanes():
    return lax.broadcasted_iota(jnp.int32, (HALO, HALO), 1)


def upward_kernel(above, info, edge, from_left, from_right, spill, upward):
    keep = info[0].astype(jnp.float32)
    for k in range(2):
        own = edge[k, :HALO] + from_left[k, :HALO]
        upward[k] = jnp.where(lanes() >= above[1, 1], own, from_right[k, :HALO] + spill[k, :HALO] * keep)


def merge_kernel(info, obj, from_left, from_right, spill, whole_hbm, source, whole, sems):
    keep = info[0].astype(jnp.float32)
    whole_copy = lambda k: pltpu.make_async_copy(whole.at[k], whole_hbm.at[k], sems.at[k])
    for k in range(2):
        left = obj[k, :, :HALO] + from_left[k]
        whole[k, :, :HALO] = left
        whole[k, :, HALO:] = obj[k, :, HALO:]
        whole_copy(k).start()
        source[k, :, :HALO] = left[LAST:]
        source[k, :, HALO:WIN] = obj[k, LAST:, HALO:]
        source[k, :LOW - LAST, WIN:] = jnp.zeros((LOW - LAST, HALO), jnp.float32)
        source[k, LOW - LAST:, WIN:] = from_right[k, HALO:] + spill[k, LOW:] * keep
    for k in range(2):
        whole_copy(k).wait()


def second_kernel(pos, info, source, below_mid, below_rest, probe_hbm, amp_hbm, before_hbm,
                  high, low, high_t, low_t, rows, cols,
                  grad, keep_sum, send_sum, far, win, tall, amp, probe, before, sems):
    row, col, core = pos[1, 0] - LAST, pos[1, 1], info[1]
    probe_copy = lambda m: pltpu.make_async_copy(probe_hbm.at[m], probe.at[m], sems.at[m])
    before_copy = lambda m: pltpu.make_async_copy(before_hbm.at[m], before.at[m], sems.at[2 + m])
    amp_copy = pltpu.make_async_copy(amp_hbm.at[1], amp, sems.at[4])
    probe_copy(0).start()
    probe_copy(1).start()
    amp_copy.start()
    before_copy(0).start()
    before_copy(1).start()

    def tiles(k):
        lower = (below_rest[k], below_mid[k], below_rest[k])
        return [jnp.concatenate([source[k, :, HALO * t:HALO * t + HALO], lower[t]], axis=0) for t in range(3)]

    cut_window(tiles, tall, win, row, col)

    def add_probe(m, real, imag):
        before_copy(m).wait()

        @pl.when(m == core)
        def _():
            keep_sum[0] = before[m, 0] + real
            keep_sum[1] = before[m, 1] + imag

        @pl.when(m != core)
        def _():
            send_sum[0] = before[m, 0] + real
            send_sum[1] = before[m, 1] + imag

    window_fit(probe, amp, (high, low, high_t, low_t, rows, cols), far, win, grad, add_probe,
               probe_copy, amp_copy)


def place_kernel(pos, grad, step, own_grad, downward, tall):
    row, col = pos[1, 0] - LAST, pos[1, 1]
    scale = step[:1, :1]
    for k in range(2):
        tall[k] = jnp.zeros((TILE_R + 8, WIN), jnp.float32)
        g = placed(grad, scale, tall, row, col, k)
        own_grad[k] = g[:WIN]
        downward[k, :, :HALO] = g[WIN:, :HALO] + g[WIN:, WIN:]
        downward[k, :, HALO:] = g[WIN:, HALO:WIN]


def spill_kernel(above, own_grad, from_above, new_spill):
    for k in range(2):
        new_spill[k, :HALO] = jnp.where(lanes() < above[1, 1], from_above[k, :, :HALO], 0.0)
        new_spill[k, HALO:] = own_grad[k, :, WIN:]


def object_kernel(above, whole, own_grad, from_above, from_left, out):
    for k in range(2):
        fell = jnp.where(lanes() >= above[1, 1], from_above[k, :, :HALO], 0.0)
        out[k, :LAST, :HALO] = whole[k, :LAST, :HALO] + fell + from_left[k, :LAST]
        out[k, :LAST, HALO:] = whole[k, :LAST, HALO:] + from_above[k, :, HALO:]
        out[k, LAST:, :HALO] = whole[k, LAST:, :HALO] + own_grad[k, :, :HALO] + from_left[k, LAST:]
        out[k, LAST:, HALO:] = whole[k, LAST:, HALO:] + own_grad[k, :, HALO:WIN]


def probe_kernel(info, probe, own, other, out):
    core = info[1]
    out[core] = probe[core] + own[...]
    out[1 - core] = probe[1 - core] + other[...]


HBM = object()
AUTO = object()


def call(kernel, outs, scratch, scalars, arrays, copies=0, in_place=None):
    smem = pl.BlockSpec(memory_space=pltpu.SMEM)
    specs = {None: pl.BlockSpec(memory_space=pltpu.VMEM), HBM: pl.BlockSpec(memory_space=pltpu.HBM)}
    specs[AUTO] = specs[None]
    arrays = [x if isinstance(x, tuple) else (x, None) for x in arrays]
    outs = [(o[0], o[1]) if isinstance(o[0], tuple) else (o, None) for o in outs]
    spaces = {None: pltpu.VMEM, HBM: pltpu.HBM, AUTO: pltpu.HBM}
    shapes = [
        jax.ShapeDtypeStruct(shape, jnp.float32) if INTERPRET or where is AUTO else spaces[where](shape, jnp.float32)
        for shape, where in outs
    ]
    operands = [
        x if INTERPRET or where is AUTO else pltpu.with_memory_space_constraint(x, spaces[where]) for x, where in arrays
    ]
    if copies == 5 and not INTERPRET:
        scalars = [pltpu.with_memory_space_constraint(x, pltpu.SMEM) for x in scalars]
    return pl.pallas_call(
        kernel,
        out_shape=shapes,
        in_specs=[smem] * len(scalars) + [specs[where] for _, where in arrays],
        out_specs=[specs[where] for _, where in outs],
        scratch_shapes=[pltpu.VMEM(s, jnp.float32) if isinstance(s, tuple) else s for s in scratch]
        + ([pltpu.SemaphoreType.DMA((copies,))] if copies else []),
        compiler_params=pltpu.CompilerParams(vmem_limit_bytes=24 * 1024 * 1024),
        input_output_aliases=in_place or {},
        interpret=INTERPRET,
    )(*scalars, *operands)


def passed_along(block, axis, distance):
    devices = range(lax.axis_size(axis))
    route = [(i - distance, i) for i in devices if i - distance in devices]
    return lax.ppermute(block, axis, route)


def exchanged(parts, axes):
    return lax.all_to_all(parts, axes, 0, 0, tiled=False)


def swapped(block):
    return lax.ppermute(block, CORE, [(0, 1), (1, 0)])


def summed_everywhere(keep, send, divisor):
    plane = lax.axis_size(PLANE)
    mode = keep + swapped(send)
    parts = exchanged(mode.reshape(plane, -1, WIN), PLANE)
    share = jnp.sum(parts, axis=0)
    for axis in ("col_0", "row_1"):
        parts = exchanged(jnp.broadcast_to(share, (lax.axis_size(axis), *share.shape)), axis)
        share = jnp.sum(parts, axis=0)
    share = share / divisor
    mode = exchanged(jnp.broadcast_to(share, (plane, *share.shape)), PLANE).reshape(2, WIN, WIN)
    return mode, swapped(mode)


def step_once(object_field, probe_modes, scan_positions, amplitudes):
    tables = [jnp.asarray(t) for t in dft_constants()]
    positions = scan_positions[0, 0]
    device_count = lax.axis_size(ROW) * lax.axis_size(COL)
    divisor = math.sqrt(device_count * BATCHES)
    has_right = (lax.axis_index(COL) < lax.axis_size(COL) - 1).astype(jnp.int32)
    tile, side, probe_shape = (2, TILE_R, WIN), (2, TILE_R, HALO), (2, 2, WIN, WIN)
    block, window = (2, HALO, HALO), (2, WIN, WIN)
    fit_scratch = [probe_shape, window, window, (2, TILE_R + 8, WIN), (WIN, WIN), probe_shape]

    halo = passed_along(object_field[:, :, :HALO], COL, -1)
    above = passed_along(positions, ROW, 1)
    info = jnp.stack([has_right, lax.axis_index(CORE)])
    amp, step = call(
        before_kernel, [((BATCHES, WIN, WIN), HBM), (8, HALF)],
        [probe_shape, pltpu.VMEM((BATCHES, WIN, WIN), jnp.bfloat16), (BATCHES, WIN, WIN)],
        [], [(probe_modes, HBM), (amplitudes[0, 0], HBM)], copies=4)
    obj, spill, edge, middle, probe_sum = call(
        first_kernel, [tile, side, (2, TILE_R - LOW + HALO, HALO), block, (probe_shape, HBM)], fit_scratch, [positions],
        [object_field, halo, probe_modes, (amp, HBM), step, *tables], copies=5, in_place={1: 0, 2: 1})
    from_right = passed_along(edge, COL, -1)
    from_left = passed_along(spill, COL, 1)
    below_mid = passed_along(middle, ROW, -1)
    (upward,) = call(upward_kernel, [block], [], [above, info], [edge, from_left, from_right, spill])
    below_rest = passed_along(upward, ROW, -1)
    whole, source = call(
        merge_kernel, [(tile, HBM), (2, WIN, WIDE)], [tile], [info], [obj, from_left, from_right, spill], copies=2)
    grad, keep, send = call(
        second_kernel, [window, window, window],
        [probe_shape, window, (2, TILE_R + 8, WIN), (WIN, WIN), probe_shape, probe_shape], [positions, info],
        [source, below_mid, below_rest, (probe_modes, HBM), (amp, HBM), (probe_sum, HBM), *tables], copies=5)
    grad, downward = call(
        place_kernel, [(2, WIN, WIDE), (2, HALO, WIN)], [(2, TILE_R + 8, WIN)], [positions], [grad, step])
    own, other = summed_everywhere(keep, send, divisor)
    from_above = passed_along(downward, ROW, 1)
    (spill,) = call(spill_kernel, [side], [], [above], [grad, from_above])
    from_left = passed_along(spill, COL, 1)
    (object_out,) = call(
        object_kernel, [(tile, AUTO)], [], [above], [(whole, AUTO), (grad, AUTO), (from_above, AUTO), (from_left, AUTO)])
    (probe_out,) = call(probe_kernel, [(probe_shape, AUTO)], [], [info], [(probe_modes, AUTO), own, other])
    return (object_out, probe_out)


def solution(mesh):
    torus = Mesh(mesh.devices.reshape(4, 4, 4, 4, 2), ("row_0", "row_1", "col_0", "col_1", "col_2"))
    in_specs = (P(None, ROW, COL), P(), P(ROW, COL, None, None), P(ROW, COL, None, None, None))
    out_specs = (P(None, ROW, COL), P())
    return jax.shard_map(step_once, mesh=torus, in_specs=in_specs, out_specs=out_specs, check_vma=False)
```

```python
import math

import jax
import jax.numpy as jnp
import numpy as np
from jax import lax
from jax.experimental import pallas as pl
from jax.experimental.pallas import tpu as pltpu
from jax.sharding import Mesh
from jax.sharding import PartitionSpec as P


HALO = 128
BATCHES = 2
WIN = 256
HALF = 128
INTERPRET = False
ROW = ("row_0", "row_1")
COL = ("col_0", "col_1", "col_2")
PLANE = ("row_0", "col_1")
CORE = "col_2"


def halves(x):
    high = x.astype(jnp.bfloat16)
    low = (x - high.astype(np.float64)).astype(jnp.bfloat16)
    return high, low


def dft_constants():
    index = np.arange(HALF)
    angle = 2.0 * np.pi * (np.outer(index, index) % HALF) / HALF
    cosine = np.cos(angle) / 16.0
    sine = -np.sin(angle) / 16.0
    forward = np.block([[cosine, -sine], [sine, cosine]])
    high, low = halves(forward)
    turn = 2.0 * np.pi * index / WIN
    twiddle = np.stack([np.cos(turn), -np.sin(turn)]).astype(np.float32)
    rows = np.ascontiguousarray(np.broadcast_to(twiddle[:, :, None], (2, HALF, HALF)))
    cols = np.ascontiguousarray(np.broadcast_to(twiddle[:, None, :], (2, 8, HALF)))
    return high, low, np.ascontiguousarray(high.T), np.ascontiguousarray(low.T), rows, cols


def split3(x, axis):
    high = x.astype(jnp.bfloat16)
    low = (x - high.astype(jnp.float32)).astype(jnp.bfloat16)
    return jnp.concatenate([high, low, high], axis=axis)


def left_dft(matrix, x):
    return jnp.dot(matrix, split3(x, 0), preferred_element_type=jnp.float32)


def right_dft(x, matrix):
    return jnp.dot(split3(x, 1), matrix, preferred_element_type=jnp.float32)


def forward_dft(real, imag, left, right_t, twr, twc):
    t_r, t_i = twr
    c_r, c_i = twc
    a_r, b_r, a_i, b_i = real[:HALF], real[HALF:], imag[:HALF], imag[HALF:]
    d_r, d_i = a_r - b_r, a_i - b_i
    even = left_dft(left, jnp.concatenate([a_r + b_r, a_i + b_i], axis=0))
    odd = left_dft(left, jnp.concatenate([d_r * t_r - d_i * t_i, d_r * t_i + d_i * t_r], axis=0))
    real = jnp.concatenate([even[:HALF], odd[:HALF]], axis=0)
    imag = jnp.concatenate([even[HALF:], odd[HALF:]], axis=0)
    a_r, b_r, a_i, b_i = real[:, :HALF], real[:, HALF:], imag[:, :HALF], imag[:, HALF:]
    d_r, d_i = a_r - b_r, a_i - b_i
    even = right_dft(jnp.concatenate([a_r + b_r, a_i + b_i], axis=1), right_t)
    odd = right_dft(jnp.concatenate([d_r * c_r - d_i * c_i, d_r * c_i + d_i * c_r], axis=1), right_t)
    real = jnp.concatenate([even[:, :HALF], odd[:, :HALF]], axis=1)
    imag = jnp.concatenate([even[:, HALF:], odd[:, HALF:]], axis=1)
    return real, imag


def inverse_dft(real, imag, left_t, right, twr, twc):
    t_r, t_i = twr
    c_r, c_i = twc
    even = right_dft(jnp.concatenate([real[:, :HALF], imag[:, :HALF]], axis=1), right)
    odd = right_dft(jnp.concatenate([real[:, HALF:], imag[:, HALF:]], axis=1), right)
    o_r, o_i = odd[:, :HALF], odd[:, HALF:]
    o_r, o_i = o_r * c_r + o_i * c_i, o_i * c_r - o_r * c_i
    e_r, e_i = even[:, :HALF], even[:, HALF:]
    real = jnp.concatenate([e_r + o_r, e_r - o_r], axis=1)
    imag = jnp.concatenate([e_i + o_i, e_i - o_i], axis=1)
    even = left_dft(left_t, jnp.concatenate([real[:HALF], imag[:HALF]], axis=0))
    odd = left_dft(left_t, jnp.concatenate([real[HALF:], imag[HALF:]], axis=0))
    o_r, o_i = odd[:HALF], odd[HALF:]
    o_r, o_i = o_r * t_r + o_i * t_i, o_i * t_r - o_r * t_i
    e_r, e_i = even[:HALF], even[HALF:]
    real = jnp.concatenate([e_r + o_r, e_r - o_r], axis=0)
    imag = jnp.concatenate([e_i + o_i, e_i - o_i], axis=0)
    return real, imag


def left_of(high, low):
    return jnp.concatenate([high[...], high[...], low[...]], axis=1)


def right_of(high, low):
    return jnp.concatenate([high[...], high[...], low[...]], axis=0)


def window_fit(probe, amplitude, tables, far, window_ref, gradient, add_probe, probe_copy, amp_copy):
    high, low, high_t, low_t, rows, cols = tables

    def twiddles():
        twr = tuple(jnp.concatenate([rows[k], rows[k]], axis=1) for k in range(2))
        twc = tuple(cols[k][:1] for k in range(2))
        return twr, twc

    def outward(m, carry):
        if probe_copy is not None:
            probe_copy(m).wait()
        twr, twc = twiddles()
        w_r, w_i = window_ref[0], window_ref[1]
        p_r, p_i = probe[m, 0], probe[m, 1]
        f_r, f_i = forward_dft(p_r * w_r - p_i * w_i, p_r * w_i + p_i * w_r,
                               left_of(high, low), right_of(high_t, low_t), twr, twc)
        far[m, 0] = f_r
        far[m, 1] = f_i
        return carry

    lax.fori_loop(0, 2, outward, 0)
    intensity = far[0, 0] * far[0, 0] + far[0, 1] * far[0, 1]
    intensity = intensity + (far[1, 0] * far[1, 0] + far[1, 1] * far[1, 1])
    amp_copy.wait()
    factor = amplitude[...] * lax.rsqrt(jnp.maximum(intensity, 0.1)) - 1.0
    for m in range(2):
        far[m, 0] = far[m, 0] * factor
        far[m, 1] = far[m, 1] * factor
    gradient[...] = jnp.zeros(gradient.shape, jnp.float32)

    def inward(m, carry):
        twr, twc = twiddles()
        x_r, x_i = inverse_dft(far[m, 0], far[m, 1], left_of(high_t, low_t), right_of(high, low), twr, twc)
        w_r, w_i = window_ref[0], window_ref[1]
        p_r, p_i = probe[m, 0], probe[m, 1]
        gradient[0] += p_r * x_r + p_i * x_i
        gradient[1] += p_r * x_i - p_i * x_r
        add_probe(m, w_r * x_r + w_i * x_i, w_r * x_i - w_i * x_r)
        return carry

    lax.fori_loop(0, 2, inward, 0)


def before_kernel_of(rows_of_share):
    def kernel(*refs):
        before_kernel(rows_of_share, *refs)

    return kernel


def before_kernel(size, info, probe_hbm, amp_hbm, amp_out, step_out, share, probe, amp, ordered, sems):
    amp_copy = pltpu.make_async_copy(amp_hbm, amp, sems.at[0])
    probe_copy = pltpu.make_async_copy(probe_hbm, probe, sems.at[1])
    out_copy = lambda b: pltpu.make_async_copy(ordered.at[b], amp_out.at[b], sems.at[2 + b])
    amp_copy.start()
    probe_copy.start()
    out_at = lax.broadcasted_iota(jnp.int32, (WIN, WIN), 0)
    in_at = lax.broadcasted_iota(jnp.int32, (WIN, WIN), 1)
    wanted = jnp.where(out_at < HALF, 2 * out_at, 2 * (out_at - HALF) + 1)
    pick = jnp.where(in_at == wanted, 1.0, 0.0).astype(jnp.bfloat16)
    amp_copy.wait()
    for b in range(BATCHES):
        rows = jnp.dot(pick, amp[b], preferred_element_type=jnp.float32).astype(jnp.bfloat16)
        ordered[b] = lax.dot_general(rows, pick, (((1,), (1,)), ((), ())), preferred_element_type=jnp.float32)
        out_copy(b).start()
    probe_copy.wait()
    total = jnp.zeros((8, HALF), jnp.float32)
    for m in range(2):
        for k in range(2):
            square = probe[m, k] * probe[m, k]
            square = jnp.sum(square.reshape(WIN // 8, 8, WIN), axis=0)
            total = total + square[:, :HALF] + square[:, HALF:]
    per_part = WIN // size
    start = pl.multiple_of(lax.rem(info[2], per_part) * size, size)
    share[...] = probe[info[1], info[2] // per_part, pl.ds(start, size), :]
    power = jnp.sum(total) / (WIN * WIN)
    step_out[...] = jnp.full((8, HALF), 1.0, jnp.float32) / (power + 1e-06)
    for b in range(BATCHES):
        out_copy(b).wait()


TILE_R = 384
LAST = TILE_R - WIN
WIDE = WIN + HALO
LOW = 192


def cut_window(tiles, tall, win, row, col):
    base, rest = pl.multiple_of(row // 8 * 8, 8), lax.rem(row, 8)
    near = lax.broadcasted_iota(jnp.int32, (TILE_R, HALF), 1) < HALF - col
    upper = lax.broadcasted_iota(jnp.int32, (WIN // 8, 8, WIN), 1) < 8 - rest
    for k in range(2):
        first, second, third = (pltpu.roll(t, HALF - col, 1) for t in tiles(k))
        tall[k, :TILE_R, :HALF] = jnp.where(near, first, second)
        tall[k, :TILE_R, HALF:] = jnp.where(near, second, third)
        x = tall[k, pl.ds(base, WIN + 8), :].reshape(WIN // 8 + 1, 8, WIN)
        x = pltpu.roll(x, lax.rem(8 - rest, 8), 1)
        win[k] = jnp.where(upper, x[:-1], x[1:]).reshape(WIN, WIN)
        tall[k] = jnp.zeros((TILE_R + 8, WIN), jnp.float32)


def placed(grad, scale, tall, row, col, k):
    base, rest = pl.multiple_of(row // 8 * 8, 8), lax.rem(row, 8)
    lower = lax.broadcasted_iota(jnp.int32, (WIN // 8 + 1, 8, WIN), 1) >= rest
    x = pltpu.roll((grad[k] * scale).reshape(WIN // 8, 8, WIN), rest, 1)
    gap = jnp.zeros((1, 8, WIN), jnp.float32)
    x = jnp.where(lower, jnp.concatenate([x, gap], axis=0), jnp.concatenate([gap, x], axis=0))
    tall[k, pl.ds(base, WIN + 8), :] = x.reshape(WIN + 8, WIN)
    inside = lax.broadcasted_iota(jnp.int32, (TILE_R, HALF), 1) >= col
    first = pltpu.roll(tall[k, :TILE_R, :HALF], lax.rem(col, HALF), 1)
    second = pltpu.roll(tall[k, :TILE_R, HALF:], lax.rem(col, HALF), 1)
    return jnp.concatenate(
        [jnp.where(inside, first, 0.0), jnp.where(inside, second, first), jnp.where(inside, 0.0, second)], axis=1)


def first_kernel(pos, obj, halo, probe, amp_hbm, step, high, low, high_t, low_t, rows, cols,
                 new_obj, spill, edge, middle, sum_hbm,
                 far, win, grad, tall, amp, probe_sum, sems):
    row, col = pos[0, 0], pos[0, 1]
    sum_copy = lambda m: pltpu.make_async_copy(probe_sum.at[m], sum_hbm.at[m], sems.at[2 + m])
    amp_copy = pltpu.make_async_copy(amp_hbm.at[0], amp, sems.at[4])
    amp_copy.start()

    cut_window(lambda k: (obj[k, :, :HALO], obj[k, :, HALO:], halo[k]), tall, win, row, col)

    def add_probe(m, real, imag):
        probe_sum[m, 0] = real
        probe_sum[m, 1] = imag
        sum_copy(m).start()

    window_fit(probe, amp, (high, low, high_t, low_t, rows, cols), far, win, grad, add_probe,
               None, amp_copy)
    scale = step[:1, :1]
    for k in range(2):
        g = placed(grad, scale, tall, row, col, k)
        updated = obj[k] + g[:, :WIN]
        new_obj[k] = updated
        edge[k, :HALO] = updated[:HALO, :HALO]
        edge[k, HALO:] = updated[LOW:, :HALO]
        middle[k] = updated[:HALO, HALO:]
        spill[k] = g[:, WIN:]
    for k in range(2):
        sum_copy(k).wait()


def lanes():
    return lax.broadcasted_iota(jnp.int32, (HALO, HALO), 1)


def upward_kernel(above, info, edge, from_left, from_right, spill, upward):
    keep = info[0].astype(jnp.float32)
    for k in range(2):
        own = edge[k, :HALO] + from_left[k, :HALO]
        upward[k] = jnp.where(lanes() >= above[1, 1], own, from_right[k, :HALO] + spill[k, :HALO] * keep)


def merge_kernel(info, obj, from_left, from_right, spill, whole_hbm, source, whole, sems):
    keep = info[0].astype(jnp.float32)
    whole_copy = lambda k: pltpu.make_async_copy(whole.at[k], whole_hbm.at[k], sems.at[k])
    for k in range(2):
        left = obj[k, :, :HALO] + from_left[k]
        whole[k, :, :HALO] = left
        whole[k, :, HALO:] = obj[k, :, HALO:]
        whole_copy(k).start()
        source[k, :, :HALO] = left[LAST:]
        source[k, :, HALO:WIN] = obj[k, LAST:, HALO:]
        source[k, :LOW - LAST, WIN:] = jnp.zeros((LOW - LAST, HALO), jnp.float32)
        source[k, LOW - LAST:, WIN:] = from_right[k, HALO:] + spill[k, LOW:] * keep
    for k in range(2):
        whole_copy(k).wait()


def second_kernel(pos, info, source, below_mid, below_rest, probe_hbm, amp_hbm, before_hbm,
                  high, low, high_t, low_t, rows, cols,
                  grad, keep_sum, send_sum, far, win, tall, amp, probe, before, sems):
    row, col, core = pos[1, 0] - LAST, pos[1, 1], info[1]
    probe_copy = lambda m: pltpu.make_async_copy(probe_hbm.at[m], probe.at[m], sems.at[m])
    before_copy = lambda m: pltpu.make_async_copy(before_hbm.at[m], before.at[m], sems.at[2 + m])
    amp_copy = pltpu.make_async_copy(amp_hbm.at[1], amp, sems.at[4])
    probe_copy(0).start()
    probe_copy(1).start()
    amp_copy.start()
    before_copy(0).start()
    before_copy(1).start()

    def tiles(k):
        lower = (below_rest[k], below_mid[k], below_rest[k])
        return [jnp.concatenate([source[k, :, HALO * t:HALO * t + HALO], lower[t]], axis=0) for t in range(3)]

    cut_window(tiles, tall, win, row, col)

    def add_probe(m, real, imag):
        before_copy(m).wait()

        @pl.when(m == core)
        def _():
            keep_sum[0] = before[m, 0] + real
            keep_sum[1] = before[m, 1] + imag

        @pl.when(m != core)
        def _():
            send_sum[0] = before[m, 0] + real
            send_sum[1] = before[m, 1] + imag

    window_fit(probe, amp, (high, low, high_t, low_t, rows, cols), far, win, grad, add_probe,
               probe_copy, amp_copy)


def place_kernel(pos, grad, step, own_grad, downward, tall):
    row, col = pos[1, 0] - LAST, pos[1, 1]
    scale = step[:1, :1]
    for k in range(2):
        tall[k] = jnp.zeros((TILE_R + 8, WIN), jnp.float32)
        g = placed(grad, scale, tall, row, col, k)
        own_grad[k] = g[:WIN]
        downward[k, :, :HALO] = g[WIN:, :HALO] + g[WIN:, WIN:]
        downward[k, :, HALO:] = g[WIN:, HALO:WIN]


def spill_kernel(above, own_grad, from_above, new_spill):
    for k in range(2):
        new_spill[k, :HALO] = jnp.where(lanes() < above[1, 1], from_above[k, :, :HALO], 0.0)
        new_spill[k, HALO:] = own_grad[k, :, WIN:]


def last_kernel(above, info, whole, own_grad, from_above, from_left, own, other, object_hbm, probe_hbm, out, sems):
    core = info[1]
    own_copy = pltpu.make_async_copy(own, probe_hbm.at[core], sems.at[0])
    other_copy = pltpu.make_async_copy(other, probe_hbm.at[1 - core], sems.at[1])
    object_copy = lambda k: pltpu.make_async_copy(out.at[k], object_hbm.at[k], sems.at[2 + k])
    own_copy.start()
    other_copy.start()
    for k in range(2):
        fell = jnp.where(lanes() >= above[1, 1], from_above[k, :, :HALO], 0.0)
        out[k, :LAST, :HALO] = whole[k, :LAST, :HALO] + fell + from_left[k, :LAST]
        out[k, :LAST, HALO:] = whole[k, :LAST, HALO:] + from_above[k, :, HALO:]
        out[k, LAST:, :HALO] = whole[k, LAST:, :HALO] + own_grad[k, :, :HALO] + from_left[k, LAST:]
        out[k, LAST:, HALO:] = whole[k, LAST:, HALO:] + own_grad[k, :, HALO:WIN]
        object_copy(k).start()
    own_copy.wait()
    other_copy.wait()
    for k in range(2):
        object_copy(k).wait()


HBM = object()
AUTO = object()


def call(kernel, outs, scratch, scalars, arrays, copies=0, in_place=None):
    smem = pl.BlockSpec(memory_space=pltpu.SMEM)
    specs = {None: pl.BlockSpec(memory_space=pltpu.VMEM), HBM: pl.BlockSpec(memory_space=pltpu.HBM)}
    specs[AUTO] = specs[None]
    arrays = [x if isinstance(x, tuple) else (x, None) for x in arrays]
    outs = [(o[0], o[1]) if isinstance(o[0], tuple) else (o, None) for o in outs]
    spaces = {None: pltpu.VMEM, HBM: pltpu.HBM, AUTO: pltpu.HBM}
    shapes = [
        jax.ShapeDtypeStruct(shape, jnp.float32) if INTERPRET or where is AUTO else spaces[where](shape, jnp.float32)
        for shape, where in outs
    ]
    operands = [
        x if INTERPRET or where is AUTO else pltpu.with_memory_space_constraint(x, spaces[where]) for x, where in arrays
    ]
    if copies == 5 and not INTERPRET:
        scalars = [pltpu.with_memory_space_constraint(x, pltpu.SMEM) for x in scalars]
    return pl.pallas_call(
        kernel,
        out_shape=shapes,
        in_specs=[smem] * len(scalars) + [specs[where] for _, where in arrays],
        out_specs=[specs[where] for _, where in outs],
        scratch_shapes=[pltpu.VMEM(s, jnp.float32) if isinstance(s, tuple) else s for s in scratch]
        + ([pltpu.SemaphoreType.DMA((copies,))] if copies else []),
        compiler_params=pltpu.CompilerParams(vmem_limit_bytes=24 * 1024 * 1024),
        input_output_aliases=in_place or {},
        interpret=INTERPRET,
    )(*scalars, *operands)


def passed_along(block, axis, distance):
    devices = range(lax.axis_size(axis))
    route = [(i - distance, i) for i in devices if i - distance in devices]
    return lax.ppermute(block, axis, route)


def exchanged(parts, axes):
    return lax.all_to_all(parts, axes, 0, 0, tiled=False)


def swapped(block):
    return lax.ppermute(block, CORE, [(0, 1), (1, 0)])


def new_modes(keep, send, old_share, divisor):
    plane = lax.axis_size(PLANE)
    mode = keep + swapped(send)
    parts = exchanged(mode.reshape(plane, -1, WIN), PLANE)
    share = jnp.sum(parts, axis=0)
    for axis in ("col_0", "row_1"):
        parts = exchanged(jnp.broadcast_to(share, (lax.axis_size(axis), *share.shape)), axis)
        share = jnp.sum(parts, axis=0)
    share = old_share + share / divisor
    mode = exchanged(jnp.broadcast_to(share, (plane, *share.shape)), PLANE).reshape(2, WIN, WIN)
    return mode, swapped(mode)


def step_once(object_field, probe_modes, scan_positions, amplitudes):
    tables = [jnp.asarray(t) for t in dft_constants()]
    positions = scan_positions[0, 0]
    device_count = lax.axis_size(ROW) * lax.axis_size(COL)
    divisor = math.sqrt(device_count * BATCHES)
    has_right = (lax.axis_index(COL) < lax.axis_size(COL) - 1).astype(jnp.int32)
    tile, side, probe_shape = (2, TILE_R, WIN), (2, TILE_R, HALO), (2, 2, WIN, WIN)
    block, window = (2, HALO, HALO), (2, WIN, WIN)
    fit_scratch = [probe_shape, window, window, (2, TILE_R + 8, WIN), (WIN, WIN), probe_shape]

    halo = passed_along(object_field[:, :, :HALO], COL, -1)
    above = passed_along(positions, ROW, 1)
    info = jnp.stack([has_right, lax.axis_index(CORE), lax.axis_index(PLANE)])
    rows = 2 * WIN // lax.axis_size(PLANE)
    amp, step, old_share = call(
        before_kernel_of(rows), [((BATCHES, WIN, WIN), HBM), (8, HALF), (rows, WIN)],
        [probe_shape, pltpu.VMEM((BATCHES, WIN, WIN), jnp.bfloat16), (BATCHES, WIN, WIN)],
        [info], [(probe_modes, HBM), (amplitudes[0, 0], HBM)], copies=4)
    obj, spill, edge, middle, probe_sum = call(
        first_kernel, [tile, side, (2, TILE_R - LOW + HALO, HALO), block, (probe_shape, HBM)], fit_scratch, [positions],
        [object_field, halo, probe_modes, (amp, HBM), step, *tables], copies=5, in_place={1: 0, 2: 1})
    from_right = passed_along(edge, COL, -1)
    from_left = passed_along(spill, COL, 1)
    below_mid = passed_along(middle, ROW, -1)
    (upward,) = call(upward_kernel, [block], [], [above, info], [edge, from_left, from_right, spill])
    below_rest = passed_along(upward, ROW, -1)
    whole, source = call(
        merge_kernel, [(tile, HBM), (2, WIN, WIDE)], [tile], [info], [obj, from_left, from_right, spill], copies=2)
    grad, keep, send = call(
        second_kernel, [window, window, window],
        [probe_shape, window, (2, TILE_R + 8, WIN), (WIN, WIN), probe_shape, probe_shape], [positions, info],
        [source, below_mid, below_rest, (probe_modes, HBM), (amp, HBM), (probe_sum, HBM), *tables], copies=5)
    grad, downward = call(
        place_kernel, [(2, WIN, WIDE), (2, HALO, WIN)], [(2, TILE_R + 8, WIN)], [positions], [grad, step])
    own, other = new_modes(keep, send, old_share, divisor)
    from_above = passed_along(downward, ROW, 1)
    (spill,) = call(spill_kernel, [side], [], [above], [grad, from_above])
    from_left = passed_along(spill, COL, 1)
    object_out, probe_out = call(
        last_kernel, [(tile, HBM), (probe_shape, HBM)], [tile], [above, info],
        [(whole, AUTO), grad, from_above, from_left, own, other], copies=4)
    return (object_out, probe_out)


def solution(mesh):
    torus = Mesh(mesh.devices.reshape(4, 4, 4, 4, 2), ("row_0", "row_1", "col_0", "col_1", "col_2"))
    in_specs = (P(None, ROW, COL), P(), P(ROW, COL, None, None), P(ROW, COL, None, None, None))
    out_specs = (P(None, ROW, COL), P())
    return jax.shard_map(step_once, mesh=torus, in_specs=in_specs, out_specs=out_specs, check_vma=False)
```

```python
import math

import jax
import jax.numpy as jnp
import numpy as np
from jax import lax
from jax.experimental import pallas as pl
from jax.experimental.pallas import tpu as pltpu
from jax.sharding import Mesh
from jax.sharding import PartitionSpec as P


HALO = 128
BATCHES = 2
WIN = 256
HALF = 128
INTERPRET = False
ROW = ("row_0", "row_1")
COL = ("col_0", "col_1", "col_2")
PLANE = ("row_0", "col_1")
CORE = "col_2"


def halves(x):
    high = x.astype(jnp.bfloat16)
    low = (x - high.astype(np.float64)).astype(jnp.bfloat16)
    return high, low


def dft_constants():
    index = np.arange(HALF)
    angle = 2.0 * np.pi * (np.outer(index, index) % HALF) / HALF
    cosine = np.cos(angle) / 16.0
    sine = -np.sin(angle) / 16.0
    forward = np.block([[cosine, -sine], [sine, cosine]])
    high, low = halves(forward)
    turn = 2.0 * np.pi * index / WIN
    twiddle = np.stack([np.cos(turn), -np.sin(turn)]).astype(np.float32)
    rows = np.ascontiguousarray(np.broadcast_to(twiddle[:, :, None], (2, HALF, HALF)))
    cols = np.ascontiguousarray(np.broadcast_to(twiddle[:, None, :], (2, 8, HALF)))
    return high, low, np.ascontiguousarray(high.T), np.ascontiguousarray(low.T), rows, cols


def split3(x, axis):
    high = x.astype(jnp.bfloat16)
    low = (x - high.astype(jnp.float32)).astype(jnp.bfloat16)
    return jnp.concatenate([high, low, high], axis=axis)


def left_dft(matrix, x):
    return jnp.dot(matrix, split3(x, 0), preferred_element_type=jnp.float32)


def right_dft(x, matrix):
    return jnp.dot(split3(x, 1), matrix, preferred_element_type=jnp.float32)


def forward_dft(real, imag, left, right_t, twr, twc):
    t_r, t_i = twr
    c_r, c_i = twc
    a_r, b_r, a_i, b_i = real[:HALF], real[HALF:], imag[:HALF], imag[HALF:]
    d_r, d_i = a_r - b_r, a_i - b_i
    even = left_dft(left, jnp.concatenate([a_r + b_r, a_i + b_i], axis=0))
    odd = left_dft(left, jnp.concatenate([d_r * t_r - d_i * t_i, d_r * t_i + d_i * t_r], axis=0))
    real = jnp.concatenate([even[:HALF], odd[:HALF]], axis=0)
    imag = jnp.concatenate([even[HALF:], odd[HALF:]], axis=0)
    a_r, b_r, a_i, b_i = real[:, :HALF], real[:, HALF:], imag[:, :HALF], imag[:, HALF:]
    d_r, d_i = a_r - b_r, a_i - b_i
    even = right_dft(jnp.concatenate([a_r + b_r, a_i + b_i], axis=1), right_t)
    odd = right_dft(jnp.concatenate([d_r * c_r - d_i * c_i, d_r * c_i + d_i * c_r], axis=1), right_t)
    real = jnp.concatenate([even[:, :HALF], odd[:, :HALF]], axis=1)
    imag = jnp.concatenate([even[:, HALF:], odd[:, HALF:]], axis=1)
    return real, imag


def inverse_dft(real, imag, left_t, right, twr, twc):
    t_r, t_i = twr
    c_r, c_i = twc
    even = right_dft(jnp.concatenate([real[:, :HALF], imag[:, :HALF]], axis=1), right)
    odd = right_dft(jnp.concatenate([real[:, HALF:], imag[:, HALF:]], axis=1), right)
    o_r, o_i = odd[:, :HALF], odd[:, HALF:]
    o_r, o_i = o_r * c_r + o_i * c_i, o_i * c_r - o_r * c_i
    e_r, e_i = even[:, :HALF], even[:, HALF:]
    real = jnp.concatenate([e_r + o_r, e_r - o_r], axis=1)
    imag = jnp.concatenate([e_i + o_i, e_i - o_i], axis=1)
    even = left_dft(left_t, jnp.concatenate([real[:HALF], imag[:HALF]], axis=0))
    odd = left_dft(left_t, jnp.concatenate([real[HALF:], imag[HALF:]], axis=0))
    o_r, o_i = odd[:HALF], odd[HALF:]
    o_r, o_i = o_r * t_r + o_i * t_i, o_i * t_r - o_r * t_i
    e_r, e_i = even[:HALF], even[HALF:]
    real = jnp.concatenate([e_r + o_r, e_r - o_r], axis=0)
    imag = jnp.concatenate([e_i + o_i, e_i - o_i], axis=0)
    return real, imag


def left_of(high, low):
    return jnp.concatenate([high[...], high[...], low[...]], axis=1)


def right_of(high, low):
    return jnp.concatenate([high[...], high[...], low[...]], axis=0)


def window_fit(probe, amplitude, tables, far, window_ref, gradient, add_probe, probe_copy, amp_copy):
    high, low, high_t, low_t, rows, cols = tables

    def twiddles():
        twr = tuple(jnp.concatenate([rows[k], rows[k]], axis=1) for k in range(2))
        twc = tuple(cols[k][:1] for k in range(2))
        return twr, twc

    def outward(m, carry):
        if probe_copy is not None:
            probe_copy(m).wait()
        twr, twc = twiddles()
        w_r, w_i = window_ref[0], window_ref[1]
        p_r, p_i = probe[m, 0], probe[m, 1]
        f_r, f_i = forward_dft(p_r * w_r - p_i * w_i, p_r * w_i + p_i * w_r,
                               left_of(high, low), right_of(high_t, low_t), twr, twc)
        far[m, 0] = f_r
        far[m, 1] = f_i
        return carry

    lax.fori_loop(0, 2, outward, 0)
    intensity = far[0, 0] * far[0, 0] + far[0, 1] * far[0, 1]
    intensity = intensity + (far[1, 0] * far[1, 0] + far[1, 1] * far[1, 1])
    amp_copy.wait()
    factor = amplitude[...] * lax.rsqrt(jnp.maximum(intensity, 0.1)) - 1.0
    for m in range(2):
        far[m, 0] = far[m, 0] * factor
        far[m, 1] = far[m, 1] * factor
    gradient[...] = jnp.zeros(gradient.shape, jnp.float32)

    def inward(m, carry):
        twr, twc = twiddles()
        x_r, x_i = inverse_dft(far[m, 0], far[m, 1], left_of(high_t, low_t), right_of(high, low), twr, twc)
        w_r, w_i = window_ref[0], window_ref[1]
        p_r, p_i = probe[m, 0], probe[m, 1]
        gradient[0] += p_r * x_r + p_i * x_i
        gradient[1] += p_r * x_i - p_i * x_r
        add_probe(m, w_r * x_r + w_i * x_i, w_r * x_i - w_i * x_r)
        return carry

    lax.fori_loop(0, 2, inward, 0)


def before_kernel_of(rows_of_share):
    def kernel(*refs):
        before_kernel(rows_of_share, *refs)

    return kernel


def before_kernel(size, info, probe_hbm, amp_hbm, amp_out, step_out, share, probe, amp, ordered, sems):
    amp_copy = pltpu.make_async_copy(amp_hbm, amp, sems.at[0])
    probe_copy = pltpu.make_async_copy(probe_hbm, probe, sems.at[1])
    out_copy = lambda b: pltpu.make_async_copy(ordered.at[b], amp_out.at[b], sems.at[2 + b])
    amp_copy.start()
    probe_copy.start()
    out_at = lax.broadcasted_iota(jnp.int32, (WIN, WIN), 0)
    in_at = lax.broadcasted_iota(jnp.int32, (WIN, WIN), 1)
    wanted = jnp.where(out_at < HALF, 2 * out_at, 2 * (out_at - HALF) + 1)
    pick = jnp.where(in_at == wanted, 1.0, 0.0).astype(jnp.bfloat16)
    amp_copy.wait()
    for b in range(BATCHES):
        rows = jnp.dot(pick, amp[b], preferred_element_type=jnp.float32).astype(jnp.bfloat16)
        ordered[b] = lax.dot_general(rows, pick, (((1,), (1,)), ((), ())), preferred_element_type=jnp.float32)
        out_copy(b).start()
    probe_copy.wait()
    total = jnp.zeros((8, HALF), jnp.float32)
    for m in range(2):
        for k in range(2):
            square = probe[m, k] * probe[m, k]
            square = jnp.sum(square.reshape(WIN // 8, 8, WIN), axis=0)
            total = total + square[:, :HALF] + square[:, HALF:]
    per_part = WIN // size
    start = pl.multiple_of(lax.rem(info[2], per_part) * size, size)
    share[...] = probe[info[1], info[2] // per_part, pl.ds(start, size), :]
    power = jnp.sum(total) / (WIN * WIN)
    step_out[...] = jnp.full((8, HALF), 1.0, jnp.float32) / (power + 1e-06)
    for b in range(BATCHES):
        out_copy(b).wait()


TILE_R = 384
LAST = TILE_R - WIN
WIDE = WIN + HALO
LOW = 192


def cut_window(tiles, tall, win, row, col):
    base, rest = pl.multiple_of(row // 8 * 8, 8), lax.rem(row, 8)
    near = lax.broadcasted_iota(jnp.int32, (TILE_R, HALF), 1) < HALF - col
    upper = lax.broadcasted_iota(jnp.int32, (WIN // 8, 8, WIN), 1) < 8 - rest
    for k in range(2):
        first, second, third = (pltpu.roll(t, HALF - col, 1) for t in tiles(k))
        tall[k, :TILE_R, :HALF] = jnp.where(near, first, second)
        tall[k, :TILE_R, HALF:] = jnp.where(near, second, third)
        x = tall[k, pl.ds(base, WIN + 8), :].reshape(WIN // 8 + 1, 8, WIN)
        x = pltpu.roll(x, lax.rem(8 - rest, 8), 1)
        win[k] = jnp.where(upper, x[:-1], x[1:]).reshape(WIN, WIN)
        tall[k] = jnp.zeros((TILE_R + 8, WIN), jnp.float32)


def placed(grad, scale, tall, row, col, k):
    base, rest = pl.multiple_of(row // 8 * 8, 8), lax.rem(row, 8)
    lower = lax.broadcasted_iota(jnp.int32, (WIN // 8 + 1, 8, WIN), 1) >= rest
    x = pltpu.roll((grad[k] * scale).reshape(WIN // 8, 8, WIN), rest, 1)
    gap = jnp.zeros((1, 8, WIN), jnp.float32)
    x = jnp.where(lower, jnp.concatenate([x, gap], axis=0), jnp.concatenate([gap, x], axis=0))
    tall[k, pl.ds(base, WIN + 8), :] = x.reshape(WIN + 8, WIN)
    inside = lax.broadcasted_iota(jnp.int32, (TILE_R, HALF), 1) >= col
    first = pltpu.roll(tall[k, :TILE_R, :HALF], lax.rem(col, HALF), 1)
    second = pltpu.roll(tall[k, :TILE_R, HALF:], lax.rem(col, HALF), 1)
    return jnp.concatenate(
        [jnp.where(inside, first, 0.0), jnp.where(inside, second, first), jnp.where(inside, 0.0, second)], axis=1)


def first_kernel(pos, obj, halo, probe, amp_hbm, step, high, low, high_t, low_t, rows, cols,
                 new_obj, spill, edge, middle, sum_hbm,
                 far, win, grad, tall, amp, probe_sum, sems):
    row, col = pos[0, 0], pos[0, 1]
    sum_copy = lambda m: pltpu.make_async_copy(probe_sum.at[m], sum_hbm.at[m], sems.at[2 + m])
    amp_copy = pltpu.make_async_copy(amp_hbm.at[0], amp, sems.at[4])
    amp_copy.start()

    cut_window(lambda k: (obj[k, :, :HALO], obj[k, :, HALO:], halo[k]), tall, win, row, col)

    def add_probe(m, real, imag):
        probe_sum[m, 0] = real
        probe_sum[m, 1] = imag
        sum_copy(m).start()

    window_fit(probe, amp, (high, low, high_t, low_t, rows, cols), far, win, grad, add_probe,
               None, amp_copy)
    scale = step[:1, :1]
    for k in range(2):
        g = placed(grad, scale, tall, row, col, k)
        updated = obj[k] + g[:, :WIN]
        new_obj[k] = updated
        edge[k, :HALO] = updated[:HALO, :HALO]
        edge[k, HALO:] = updated[LOW:, :HALO]
        middle[k] = updated[:HALO, HALO:]
        spill[k] = g[:, WIN:]
    for k in range(2):
        sum_copy(k).wait()


def lanes():
    return lax.broadcasted_iota(jnp.int32, (HALO, HALO), 1)


def upward_kernel(above, info, edge, from_left, from_right, spill, upward):
    keep = info[0].astype(jnp.float32)
    for k in range(2):
        own = edge[k, :HALO] + from_left[k, :HALO]
        upward[k] = jnp.where(lanes() >= above[1, 1], own, from_right[k, :HALO] + spill[k, :HALO] * keep)


def merge_kernel(info, obj, from_left, from_right, spill, whole_hbm, source, whole, sems):
    keep = info[0].astype(jnp.float32)
    whole_copy = lambda k: pltpu.make_async_copy(whole.at[k], whole_hbm.at[k], sems.at[k])
    for k in range(2):
        left = obj[k, :, :HALO] + from_left[k]
        whole[k, :, :HALO] = left
        whole[k, :, HALO:] = obj[k, :, HALO:]
        whole_copy(k).start()
        source[k, :, :HALO] = left[LAST:]
        source[k, :, HALO:WIN] = obj[k, LAST:, HALO:]
        source[k, :LOW - LAST, WIN:] = jnp.zeros((LOW - LAST, HALO), jnp.float32)
        source[k, LOW - LAST:, WIN:] = from_right[k, HALO:] + spill[k, LOW:] * keep
    for k in range(2):
        whole_copy(k).wait()


def second_kernel(pos, info, source, below_mid, below_rest, probe_hbm, amp_hbm, before_hbm,
                  high, low, high_t, low_t, rows, cols,
                  grad, keep_sum, send_sum, far, win, tall, amp, probe, before, sems):
    row, col, core = pos[1, 0] - LAST, pos[1, 1], info[1]
    probe_copy = lambda m: pltpu.make_async_copy(probe_hbm.at[m], probe.at[m], sems.at[m])
    before_copy = lambda m: pltpu.make_async_copy(before_hbm.at[m], before.at[m], sems.at[2 + m])
    amp_copy = pltpu.make_async_copy(amp_hbm.at[1], amp, sems.at[4])
    probe_copy(0).start()
    probe_copy(1).start()
    amp_copy.start()
    before_copy(0).start()
    before_copy(1).start()

    def tiles(k):
        lower = (below_rest[k], below_mid[k], below_rest[k])
        return [jnp.concatenate([source[k, :, HALO * t:HALO * t + HALO], lower[t]], axis=0) for t in range(3)]

    cut_window(tiles, tall, win, row, col)

    def add_probe(m, real, imag):
        before_copy(m).wait()

        @pl.when(m == core)
        def _():
            keep_sum[0] = before[m, 0] + real
            keep_sum[1] = before[m, 1] + imag

        @pl.when(m != core)
        def _():
            send_sum[0] = before[m, 0] + real
            send_sum[1] = before[m, 1] + imag

    window_fit(probe, amp, (high, low, high_t, low_t, rows, cols), far, win, grad, add_probe,
               probe_copy, amp_copy)


def place_kernel(pos, grad, step, own_grad, downward, tall):
    row, col = pos[1, 0] - LAST, pos[1, 1]
    scale = step[:1, :1]
    for k in range(2):
        tall[k] = jnp.zeros((TILE_R + 8, WIN), jnp.float32)
        g = placed(grad, scale, tall, row, col, k)
        own_grad[k] = g[:WIN]
        downward[k, :, :HALO] = g[WIN:, :HALO] + g[WIN:, WIN:]
        downward[k, :, HALO:] = g[WIN:, HALO:WIN]


def spill_kernel(above, own_grad, from_above, new_spill):
    for k in range(2):
        new_spill[k, :HALO] = jnp.where(lanes() < above[1, 1], from_above[k, :, :HALO], 0.0)
        new_spill[k, HALO:] = own_grad[k, :, WIN:]


def object_kernel(above, whole, own_grad, from_above, from_left, out):
    for k in range(2):
        fell = jnp.where(lanes() >= above[1, 1], from_above[k, :, :HALO], 0.0)
        out[k, :LAST, :HALO] = whole[k, :LAST, :HALO] + fell + from_left[k, :LAST]
        out[k, :LAST, HALO:] = whole[k, :LAST, HALO:] + from_above[k, :, HALO:]
        out[k, LAST:, :HALO] = whole[k, LAST:, :HALO] + own_grad[k, :, :HALO] + from_left[k, LAST:]
        out[k, LAST:, HALO:] = whole[k, LAST:, HALO:] + own_grad[k, :, HALO:WIN]


def last_kernel(info, own, other, probe_hbm, sems):
    core = info[1]
    own_copy = pltpu.make_async_copy(own, probe_hbm.at[core], sems.at[0])
    other_copy = pltpu.make_async_copy(other, probe_hbm.at[1 - core], sems.at[1])
    own_copy.start()
    other_copy.start()
    own_copy.wait()
    other_copy.wait()


HBM = object()
AUTO = object()


def call(kernel, outs, scratch, scalars, arrays, copies=0, in_place=None):
    smem = pl.BlockSpec(memory_space=pltpu.SMEM)
    specs = {None: pl.BlockSpec(memory_space=pltpu.VMEM), HBM: pl.BlockSpec(memory_space=pltpu.HBM)}
    specs[AUTO] = specs[None]
    arrays = [x if isinstance(x, tuple) else (x, None) for x in arrays]
    outs = [(o[0], o[1]) if isinstance(o[0], tuple) else (o, None) for o in outs]
    spaces = {None: pltpu.VMEM, HBM: pltpu.HBM, AUTO: pltpu.HBM}
    shapes = [
        jax.ShapeDtypeStruct(shape, jnp.float32) if INTERPRET or where is AUTO else spaces[where](shape, jnp.float32)
        for shape, where in outs
    ]
    operands = [
        x if INTERPRET or where is AUTO else pltpu.with_memory_space_constraint(x, spaces[where]) for x, where in arrays
    ]
    if copies == 5 and not INTERPRET:
        scalars = [pltpu.with_memory_space_constraint(x, pltpu.SMEM) for x in scalars]
    return pl.pallas_call(
        kernel,
        out_shape=shapes,
        in_specs=[smem] * len(scalars) + [specs[where] for _, where in arrays],
        out_specs=[specs[where] for _, where in outs],
        scratch_shapes=[pltpu.VMEM(s, jnp.float32) if isinstance(s, tuple) else s for s in scratch]
        + ([pltpu.SemaphoreType.DMA((copies,))] if copies else []),
        compiler_params=pltpu.CompilerParams(vmem_limit_bytes=24 * 1024 * 1024),
        input_output_aliases=in_place or {},
        interpret=INTERPRET,
    )(*scalars, *operands)


def passed_along(block, axis, distance):
    devices = range(lax.axis_size(axis))
    route = [(i - distance, i) for i in devices if i - distance in devices]
    return lax.ppermute(block, axis, route)


def exchanged(parts, axes):
    return lax.all_to_all(parts, axes, 0, 0, tiled=False)


def swapped(block):
    return lax.ppermute(block, CORE, [(0, 1), (1, 0)])


def new_modes(keep, send, old_share, divisor):
    plane = lax.axis_size(PLANE)
    mode = keep + swapped(send)
    parts = exchanged(mode.reshape(plane, -1, WIN), PLANE)
    share = jnp.sum(parts, axis=0)
    for axis in ("col_0", "row_1"):
        parts = exchanged(jnp.broadcast_to(share, (lax.axis_size(axis), *share.shape)), axis)
        share = jnp.sum(parts, axis=0)
    share = old_share + share / divisor
    mode = exchanged(jnp.broadcast_to(share, (plane, *share.shape)), PLANE).reshape(2, WIN, WIN)
    return mode, swapped(mode)


def step_once(object_field, probe_modes, scan_positions, amplitudes):
    tables = [jnp.asarray(t) for t in dft_constants()]
    positions = scan_positions[0, 0]
    device_count = lax.axis_size(ROW) * lax.axis_size(COL)
    divisor = math.sqrt(device_count * BATCHES)
    has_right = (lax.axis_index(COL) < lax.axis_size(COL) - 1).astype(jnp.int32)
    tile, side, probe_shape = (2, TILE_R, WIN), (2, TILE_R, HALO), (2, 2, WIN, WIN)
    block, window = (2, HALO, HALO), (2, WIN, WIN)
    fit_scratch = [probe_shape, window, window, (2, TILE_R + 8, WIN), (WIN, WIN), probe_shape]

    halo = passed_along(object_field[:, :, :HALO], COL, -1)
    above = passed_along(positions, ROW, 1)
    info = jnp.stack([has_right, lax.axis_index(CORE), lax.axis_index(PLANE)])
    rows = 2 * WIN // lax.axis_size(PLANE)
    amp, step, old_share = call(
        before_kernel_of(rows), [((BATCHES, WIN, WIN), HBM), (8, HALF), (rows, WIN)],
        [probe_shape, pltpu.VMEM((BATCHES, WIN, WIN), jnp.bfloat16), (BATCHES, WIN, WIN)],
        [info], [(probe_modes, HBM), (amplitudes[0, 0], HBM)], copies=4)
    obj, spill, edge, middle, probe_sum = call(
        first_kernel, [tile, side, (2, TILE_R - LOW + HALO, HALO), block, (probe_shape, HBM)], fit_scratch, [positions],
        [object_field, halo, probe_modes, (amp, HBM), step, *tables], copies=5, in_place={1: 0, 2: 1})
    from_right = passed_along(edge, COL, -1)
    from_left = passed_along(spill, COL, 1)
    below_mid = passed_along(middle, ROW, -1)
    (upward,) = call(upward_kernel, [block], [], [above, info], [edge, from_left, from_right, spill])
    below_rest = passed_along(upward, ROW, -1)
    whole, source = call(
        merge_kernel, [(tile, HBM), (2, WIN, WIDE)], [tile], [info], [obj, from_left, from_right, spill], copies=2)
    grad, keep, send = call(
        second_kernel, [window, window, window],
        [probe_shape, window, (2, TILE_R + 8, WIN), (WIN, WIN), probe_shape, probe_shape], [positions, info],
        [source, below_mid, below_rest, (probe_modes, HBM), (amp, HBM), (probe_sum, HBM), *tables], copies=5)
    grad, downward = call(
        place_kernel, [(2, WIN, WIDE), (2, HALO, WIN)], [(2, TILE_R + 8, WIN)], [positions], [grad, step])
    own, other = new_modes(keep, send, old_share, divisor)
    from_above = passed_along(downward, ROW, 1)
    (spill,) = call(spill_kernel, [side], [], [above], [grad, from_above])
    from_left = passed_along(spill, COL, 1)
    (object_out,) = call(
        object_kernel, [(tile, AUTO)], [], [above], [(whole, AUTO), (grad, AUTO), (from_above, AUTO), (from_left, AUTO)])
    (probe_out,) = call(last_kernel, [(probe_shape, HBM)], [], [info], [own, other], copies=2)
    return (object_out, probe_out)


def solution(mesh):
    torus = Mesh(mesh.devices.reshape(4, 4, 4, 4, 2), ("row_0", "row_1", "col_0", "col_1", "col_2"))
    in_specs = (P(None, ROW, COL), P(), P(ROW, COL, None, None), P(ROW, COL, None, None, None))
    out_specs = (P(None, ROW, COL), P())
    return jax.shard_map(step_once, mesh=torus, in_specs=in_specs, out_specs=out_specs, check_vma=False)
```
